256 devices in a mesh: seq: 64 (over x, z, core), head: 4 (over y).
Axes of the slice: x: 4, y: 4, z: 8, core: 2. Of those that a mesh axis runs over, the one named last changes fastest.
Arguments:
- query_rows: bfloat16 [8192, 2048], P(('seq', 'head')), may hold values from -160 to 160
- key_rows: bfloat16 [8192, 2048], P(('seq', 'head')), may hold values from -6 to 6
- value_rows: bfloat16 [8192, 2048], P(('seq', 'head')), may hold values from -6 to 6
- out_grad: bfloat16 [8192, 2048], P('seq', 'head'), may hold values from -48 to 48
- random_blocks: int32 [16, 64, 3], P('head'), may hold values from 0 to 63, as said below
Outputs:
- attended: bfloat16 [8192, 2048], P('seq', 'head')
- query_grad: bfloat16 [8192, 2048], P('seq', 'head')
- key_grad: bfloat16 [8192, 2048], P('seq', 'head')
- value_grad: bfloat16 [8192, 2048], P('seq', 'head')
The draws below stay inside these ranges and needn't reach their ends.
Inputs may be any that keep to these rules, and one draw needn't show every extreme that they name: `random_blocks`: take the 4 heads of one index of head and the 1 query block of one index of seq: among their 12 entries, at most 2 equal k for any k (so at most 2 are held by any one index of seq), and for every such group of entries some k occurs exactly twice.
All inputs are finite; a program needn't handle non-finite values.
Results may differ from the reference program's by a relative error of at most 0.029.
Values may be sent and summed in bfloat16 or wider, within the bound.
A program may use at most 128 MiB of HBM per device.

```python
import math
import jax
import jax.numpy as jnp
from jax import lax

HD = 128
HEADS = 16
BLK = 128
BLK_DEV = 1
HEADS_DEV = 4
NB = 64
TOKENS = 8192
CAP = 2
N_SEQ = 64


def paired_fields(key):
    folded = jax.random.fold_in(key, 7)
    pieces = jax.random.split(folded, 2)
    extent = (TOKENS, HEADS * HD)
    queries = jnp.clip(jax.random.normal(pieces[0], extent, jnp.float32), -5.0, 5.0)
    key_part = jnp.clip(jax.random.normal(pieces[1], extent, jnp.float32), -5.0, 5.0)
    return (queries, key_part)


def draw_query_rows(key, part):
    return paired_fields(key)[0].astype(jnp.bfloat16)


def draw_key_rows(key, part):
    return paired_fields(key)[1].astype(jnp.bfloat16)


def draw_random_blocks(key, part):
    group_total = HEADS // HEADS_DEV
    item_count = HEADS_DEV * BLK_DEV * 3
    slot_count = N_SEQ * CAP
    folded = jax.random.fold_in(key, 11)
    owner_of_slot = jnp.arange(slot_count) // CAP

    def one_group(group_seed):
        seeds = jax.random.split(group_seed, 3)
        raw_score = jax.random.randint(seeds[0], (slot_count,), 0, 1 << 20)
        scores = raw_score * slot_count + jnp.arange(slot_count)
        leader = owner_of_slot[jax.lax.top_k(scores, 1)[1][0]]
        boosted = scores + (owner_of_slot == leader).astype(jnp.int32) * (1 << 30)
        ranking = jnp.argsort(-boosted, stable=True)
        chosen = owner_of_slot[ranking[:item_count]]
        shuffle = jax.random.permutation(seeds[1], item_count)
        owners = chosen[shuffle]
        offsets = jax.random.randint(seeds[2], (item_count,), 0, BLK_DEV)
        return owners * BLK_DEV + offsets
    group_seeds = jax.random.split(folded, group_total * N_SEQ)
    blocks = jax.vmap(one_group)(group_seeds)
    blocks = blocks.reshape(group_total, N_SEQ, HEADS_DEV, BLK_DEV, 3)
    blocks = blocks.transpose(0, 2, 1, 3, 4).reshape(HEADS, N_SEQ * BLK_DEV, 3)
    return blocks.astype(jnp.int32)


def level_of(stream_key, shape, shards, smallest, top_value):
    def one(axis_at, blocks):
        steps = jax.random.uniform(jax.random.fold_in(jax.random.fold_in(stream_key, 6), axis_at), (blocks,), jnp.float32, smallest / len(shards), top_value / len(shards))
        return jnp.repeat(jnp.exp(steps), shape[axis_at] // blocks).reshape((-1,) + (1,) * (len(shape) - axis_at - 1))

    loudness = one(*shards[0])
    for cut in shards[1:]:
        loudness = loudness * one(*cut)
    return loudness


def scatter_about(key, shape, width, most, cuts=(), held_as=jnp.bfloat16):
    result = width * jax.random.normal(key, shape, jnp.float32)
    if cuts:
        result = result * level_of(key, shape, cuts, -0.22, 0.18)
    return jnp.clip(result, -most, most).astype(held_as)


def setup_inputs(seed: int = 0) -> dict:
    splits = jax.random.split(jax.random.key(seed), 6)
    return {
        "query_rows": draw_query_rows(jax.random.fold_in(splits[5], 71), 0),
        "key_rows": draw_key_rows(jax.random.fold_in(splits[5], 71), 0),
        "value_rows": scatter_about(splits[2], (TOKENS, HEADS * HD), 1.0, 6.0, ((0, 256),)),
        "out_grad": scatter_about(splits[3], (TOKENS, HEADS * HD), 8.0, 48.0, ((0, 64), (1, 4))),
        "random_blocks": draw_random_blocks(jax.random.fold_in(splits[5], 71), 0),
    }


ROUNDED_SLOTS = (False, False, True, False, True, True, True, True)

def key_lists(random_head):
    blocks = jnp.arange(NB, dtype=jnp.int32)
    columns = [jnp.zeros((NB,), jnp.int32), jnp.full((NB,), NB - 1, jnp.int32), (blocks + NB - 1) % NB, blocks, (blocks + 1) % NB]
    return jnp.concatenate([jnp.stack(columns, axis=1), random_head.astype(jnp.int32)], axis=1)

def one_head(inputs):
    queries, keyset, valueset, gradient, random_head = inputs
    score_scale = 1.0 / math.sqrt(HD)
    listing = key_lists(random_head)
    keys_all = keyset[listing].reshape(NB, 8 * BLK, HD).astype(jnp.float32)
    values_all = valueset[listing].reshape(NB, 8 * BLK, HD).astype(jnp.float32)
    queries_wide = queries.astype(jnp.float32)
    gradient_wide = gradient.astype(jnp.float32)
    scores = jnp.einsum('nqd,nkd->nqk', queries_wide, keys_all) * score_scale
    peaks = lax.optimization_barrier(jnp.max(scores, axis=-1, keepdims=True))
    exponent = jnp.exp(scores - peaks)
    weights = exponent / lax.optimization_barrier(jnp.sum(exponent, axis=-1, keepdims=True))
    rounded = weights.astype(jnp.bfloat16).astype(jnp.float32)
    attended = jnp.einsum('nqk,nkd->nqd', rounded, values_all).astype(jnp.bfloat16)
    row_delta = lax.optimization_barrier(jnp.sum(gradient_wide * attended.astype(jnp.float32), axis=-1))
    value_terms = jnp.einsum('nqk,nqd->nkd', rounded, gradient_wide)
    prob_grad = jnp.einsum('nqd,nkd->nqk', gradient_wide, values_all)
    score_grad = (weights * (prob_grad - row_delta[..., None])).astype(jnp.bfloat16).astype(jnp.float32)
    query_grad = (jnp.einsum('nqk,nkd->nqd', score_grad, keys_all) * score_scale).astype(jnp.bfloat16)
    key_terms = jnp.einsum('nqk,nqd->nkd', score_grad, queries_wide) * score_scale
    terms = jnp.stack([key_terms.reshape(NB, 8, BLK, HD), value_terms.reshape(NB, 8, BLK, HD)], axis=2)
    narrowed = lax.optimization_barrier(terms.astype(jnp.bfloat16)).astype(jnp.float32)
    slot_mask = jnp.array(ROUNDED_SLOTS)[None, :, None, None, None]
    mixed = jnp.where(slot_mask, narrowed, terms)
    summed = jax.ops.segment_sum(mixed.reshape(NB * 8, 2, BLK, HD), listing.reshape(-1), num_segments=NB)
    summed = summed.astype(jnp.bfloat16)
    return (attended, query_grad, summed[:, 0], summed[:, 1])

def reference(query_rows, key_rows, value_rows, out_grad, random_blocks):

    def per_head(matrix):
        return matrix.reshape(NB, BLK, HEADS, HD).transpose(2, 0, 1, 3)

    def per_token(tensor):
        return tensor.transpose(1, 2, 0, 3).reshape(TOKENS, HEADS * HD)
    attended, query_grad, key_grad, value_grad = lax.map(one_head, (per_head(query_rows), per_head(key_rows), per_head(value_rows), per_head(out_grad), random_blocks))
    return (per_token(attended), per_token(query_grad), per_token(key_grad), per_token(value_grad))
```

```python
import math

import jax
import jax.numpy as jnp
from jax import lax
from jax.experimental import pallas as pl
from jax.experimental.pallas import tpu as pltpu
from jax.sharding import PartitionSpec as P

HD = 128
BLK = 128
NX = 4
NZ = 8
NY = 4
PAIR = 2 * HD
COL = 2 * NZ
ROW = 2 * NX
SCALE = 1.0 / math.sqrt(HD)
NEG = -1e30
MESH = pl.DeviceIdType.MESH
NT = (((1,), (1,)), ((), ()))
NN = (((1,), (0,)), ((), ()))
TN = (((0,), (0,)), ((), ()))


def dot(a, b, dims):
    return lax.dot_general(a, b, dims, preferred_element_type=jnp.float32)


def position():
    s = lax.axis_index("seq")
    y = lax.axis_index("head")
    x = s // (2 * NZ)
    z = (s // 2) % NZ
    c = s % 2
    return x, z, c, y


def place_of(x, z, c):
    return (x * NZ + z) * 2 + c


def remote(src, dst, send_sem, recv_sem, dev):
    return pltpu.make_async_remote_copy(
        src_ref=src, dst_ref=dst, send_sem=send_sem, recv_sem=recv_sem,
        device_id=dev, device_id_type=MESH,
    )


def meet(devs):
    barrier = pltpu.get_barrier_semaphore()
    for dev in devs:
        pl.semaphore_signal(barrier, inc=1, device_id=dev, device_id_type=MESH)
    pl.semaphore_wait(barrier, len(devs))


def unit_slots(xr, cb, x, z, c, h, rb_ref):
    xq = (x + xr) % NX
    block = COL * xq + 2 * z + cb
    base = ((2 * c + h) * (NX * COL) + block) * 3
    slots = []
    for r in range(3):
        j = rb_ref[base + r] - COL * x
        here = (j >= 0) & (j < COL)
        slots.append((jnp.clip(j, 0, COL - 1), jnp.where(here, 0.0, NEG)))
    edge = (x == 0) | (x == NX - 1)
    slots.append((jnp.where(x == NX - 1, COL - 1, 0), jnp.where(edge, 0.0, NEG)))
    if xr == 0:
        slots.append((2 * z, None))
        slots.append((2 * z + 1, None))
    if cb == 0 and xr in (0, 1):
        ok = (z != 0) if xr == 0 else (z == 0)
        slots.append(((2 * z + COL - 1) % COL, jnp.where(ok, 0.0, NEG)))
    if cb == 1 and xr in (0, NX - 1):
        ok = (z != NZ - 1) if xr == 0 else (z == NZ - 1)
        slots.append(((2 * z + 2) % COL, jnp.where(ok, 0.0, NEG)))
    return xq, slots


def gather_kernel(rb_ref, q_ref, k_ref, v_ref, g_ref, kall, vall, qrow, grow, stats,
                  a_send, a_recv, a_own, g_send, g_recv, z_send, z_recv, x_send, x_recv, s_send, s_recv):
    x, z, c, y = position()
    me = y * 2 + c

    def member(d):
        other = (me + d) % (2 * NY)
        return other % 2, other // 2

    def at(xx, zz):
        return (place_of(xx, zz, c), y)

    group = []
    for d in range(1, 2 * NY):
        cc, yy = member(d)
        group.append((place_of(x, z, cc), yy))
    zdev = (at(x, (z + 1) % NZ), at(x, (z + NZ - 1) % NZ))
    xdev = [at((x + d) % NX, z) for d in range(1, NX)]
    partner = (place_of(x, z, 1 - c), y)
    meet(group + list(zdev) + xdev)

    def cols(cc, yy):
        return pl.ds(pl.multiple_of((yy * 2 + cc) * PAIR, PAIR), PAIR)

    rows = pl.ds(pl.multiple_of(y * 32, 32), 32)
    ins = (k_ref, v_ref, q_ref)
    bufs = (kall, vall, qrow)
    slot = (2 * z, 2 * z, 2 * x)
    sends = []
    own = []
    for t in range(3):
        dst = bufs[t].at[slot[t] + c, rows, :]
        for d in range(1, 2 * NY):
            cc, yy = member(d)
            cp = remote(ins[t].at[:, cols(cc, yy)], dst, a_send.at[t, d], a_recv.at[t, d], group[d - 1])
            cp.start()
            sends.append(cp)
        cp = pltpu.make_async_copy(ins[t].at[:, cols(c, y)], dst, a_own.at[t])
        cp.start()
        own.append(cp)
        if t == 1:
            gs = remote(g_ref.at[:, pl.ds(pl.multiple_of((1 - c) * PAIR, PAIR), PAIR)], grow.at[2 * x + c],
                        g_send, g_recv, partner)
            gs.start()
            sends.append(gs)
            go = pltpu.make_async_copy(g_ref.at[:, pl.ds(pl.multiple_of(c * PAIR, PAIR), PAIR)],
                                       grow.at[2 * x + c], a_own.at[3])
            go.start()

    def arrived(t):
        own[t].wait()
        for d in range(1, 2 * NY):
            other = (me + 2 * NY - d) % (2 * NY)
            cs, ys = other % 2, other // 2
            dst = bufs[t].at[slot[t] + cs, pl.ds(pl.multiple_of(ys * 32, 32), 32), :]
            remote(dst, dst, a_send.at[t, d], a_recv.at[t, d], partner).wait_recv()

    def zpiece(t, owner):
        return (kall, vall)[t].at[pl.ds(2 * owner, 2)]

    def zcopy(direction, step, t):
        owner = (z - step + NZ) % NZ if direction == 0 else (z + step) % NZ
        ref = zpiece(t, owner)
        return remote(ref, ref, z_send.at[direction, step, t], z_recv.at[direction, step, t], zdev[direction])

    def zwait(direction, step, t):
        owner = (z - 1 - step + NZ) % NZ if direction == 0 else (z + 1 + step) % NZ
        ref = zpiece(t, owner)
        remote(ref, ref, z_send.at[direction, step, t], z_recv.at[direction, step, t], zdev[direction]).wait_recv()

    def xpiece(t, owner):
        return (qrow, grow)[t].at[pl.ds(2 * owner, 2)]

    def xcopy(direction, step, t):
        owner = (x - step + NX) % NX if direction == 0 else (x + step) % NX
        ref = xpiece(t, owner)
        return remote(ref, ref, x_send.at[direction, step, t], x_recv.at[direction, step, t],
                      xdev[0] if direction == 0 else xdev[NX - 2])

    def xwait(direction, step, t):
        owner = (x - 1 - step + NX) % NX if direction == 0 else (x + 1 + step) % NX
        ref = xpiece(t, owner)
        remote(ref, ref, x_send.at[direction, step, t], x_recv.at[direction, step, t], xdev[0]).wait_recv()

    def go_on(cp):
        cp.start()
        sends.append(cp)

    for t in range(2):
        arrived(t)
        for direction in range(2):
            go_on(zcopy(direction, 0, t))
    go.wait()
    remote(grow.at[2 * x + 1 - c], grow.at[2 * x + 1 - c], g_send, g_recv, partner).wait_recv()
    for direction in range(2):
        go_on(xcopy(direction, 0, 1))
    arrived(2)
    for direction in range(2):
        go_on(xcopy(direction, 0, 0))
    last = NZ // 2 - 1
    for step in range(last):
        for t in range(2):
            for direction in range(2):
                zwait(direction, step, t)
                if step + 1 < last or direction == t:
                    go_on(zcopy(direction, step + 1, t))
        if step == 0:
            for t in (1, 0):
                for direction in range(2):
                    xwait(direction, 0, t)
                    if direction == t:
                        go_on(xcopy(direction, 1, t))
    for t in range(2):
        xwait(t, 1, t)
    for t in range(2):
        zwait(t, last, t)

    def one_head(h, carry):
        lanes = pl.ds(pl.multiple_of(h * HD, HD), HD)
        for xr in range(NX):
            for cb in range(2):
                xq, slots = unit_slots(xr, cb, x, z, c, h, rb_ref)
                q = qrow[2 * xq + cb, :, lanes]
                g = grow[2 * xq + cb, :, lanes]
                scores = []
                for j, bias in slots:
                    sc = dot(kall[j, :, lanes], q, NT) * SCALE
                    scores.append(sc if bias is None else sc + bias)
                peak = scores[0]
                for sc in scores[1:]:
                    peak = jnp.maximum(peak, sc)
                peak = jnp.max(peak, axis=0, keepdims=True)
                total = None
                weighted = None
                for (j, _), sc in zip(slots, scores):
                    e = jnp.exp(sc - peak)
                    w = e * dot(vall[j, :, lanes], g, NT)
                    total = e if total is None else total + e
                    weighted = w if weighted is None else weighted + w
                u = h * ROW + 2 * xq + cb
                stats[x, 0, pl.ds(u, 1), :] = peak
                stats[x, 1, pl.ds(u, 1), :] = jnp.sum(total, axis=0, keepdims=True)
                stats[x, 2, pl.ds(u, 1), :] = jnp.sum(weighted, axis=0, keepdims=True)
        return carry

    lax.fori_loop(0, 2, one_head, 0)
    for d in range(1, NX):
        go_on(remote(stats.at[x], stats.at[x], s_send.at[d], s_recv.at[d], xdev[d - 1]))
    for d in range(1, NX):
        src = (x + NX - d) % NX
        remote(stats.at[src], stats.at[src], s_send.at[d], s_recv.at[d], xdev[d - 1]).wait_recv()
    for cp in sends:
        cp.wait_send()


def grad_kernel(rb_ref, kall, vall, qrow, grow, stats, dk_ref, dv_ref, o_ref, dq_ref, dk_acc, dv_acc):
    x, z, c, y = position()
    dk_acc[...] = jnp.zeros_like(dk_acc)
    dv_acc[...] = jnp.zeros_like(dv_acc)

    def one_head(h, carry):
        lanes = pl.ds(pl.multiple_of(h * HD, HD), HD)
        for xr in range(NX):
            for cb in range(2):
                xq, slots = unit_slots(xr, cb, x, z, c, h, rb_ref)
                u = h * ROW + 2 * xq + cb
                peaks = [stats[i, 0, pl.ds(u, 1), :] for i in range(NX)]
                peak = jnp.maximum(jnp.maximum(peaks[0], peaks[1]), jnp.maximum(peaks[2], peaks[3]))
                shift = [jnp.exp(p - peak) for p in peaks]
                total = sum(stats[i, 1, pl.ds(u, 1), :] * shift[i] for i in range(NX))
                delta = sum(stats[i, 2, pl.ds(u, 1), :] * shift[i] for i in range(NX))
                inverse = 1.0 / total
                delta = delta * inverse
                q = qrow[2 * xq + cb, :, lanes]
                g = grow[2 * xq + cb, :, lanes]
                out = None
                dq = None
                for j, bias in slots:
                    k = kall[j, :, lanes]
                    v = vall[j, :, lanes]
                    sc = dot(k, q, NT) * SCALE
                    if bias is not None:
                        sc = sc + bias
                    w = jnp.exp(sc - peak) * inverse
                    wb = w.astype(jnp.bfloat16)
                    ds = (w * (dot(v, g, NT) - delta)).astype(jnp.bfloat16)
                    dv_acc[j, :, lanes] += dot(wb, g, NN)
                    dk_acc[j, :, lanes] += dot(ds, q, NN)
                    o1 = dot(wb, v, TN)
                    q1 = dot(ds, k, TN)
                    out = o1 if out is None else out + o1
                    dq = q1 if dq is None else dq + q1
                o_ref[2 * xq + cb, :, lanes] = out.astype(jnp.bfloat16)
                dq_ref[2 * xq + cb, :, lanes] = (dq * SCALE).astype(jnp.bfloat16)
        return carry

    lax.fori_loop(0, 2, one_head, 0)
    dk_ref[...] = (dk_acc[...] * SCALE).astype(jnp.bfloat16)
    dv_ref[...] = dv_acc[...].astype(jnp.bfloat16)


def reduce_kernel(dk, dv, o, dq, o_out, dq_out, dk_out, dv_out,
                  zin, zsum, xin, xsum, final, z_send, z_recv, x_send, x_recv, f_send, f_recv):
    x, z, c, y = position()

    def at(xx, zz):
        return (place_of(xx, zz, c), y)

    zdev = (at(x, (z + 1) % NZ), at(x, (z + NZ - 1) % NZ))
    xdev = (at((x + 1) % NX, z), at((x + NX - 1) % NX, z))
    partner = (place_of(x, z, 1 - c), y)
    meet(list(zdev) + list(xdev) + [partner])
    sends = []
    f32 = jnp.float32

    def go_on(cp):
        cp.start()
        sends.append(cp)

    def chain(parts, arrive, summed, ssem, rsem, devs, pos, count, half):
        steps = count // 2

        def target(direction, step):
            away = steps - step
            return (pos + away) % count if direction == 0 else (pos + count - away) % count

        def first(direction, t):
            return 0 if t == half[direction] else 1

        def send(direction, step, t):
            mine = parts[t].at[pl.ds(2 * target(direction, step), 2)]
            if step == first(direction, t):
                src = mine
            else:
                src = summed.at[direction, step, t]
                got = wait(direction, step - 1, t)
                src[...] = (got[...].astype(f32) + mine[...].astype(f32)).astype(jnp.bfloat16)
            go_on(remote(src, arrive.at[direction, step, t], ssem.at[direction, step, t],
                         rsem.at[direction, step, t], devs[direction]))

        def wait(direction, step, t):
            ref = arrive.at[direction, step, t]
            remote(ref, ref, ssem.at[direction, step, t], rsem.at[direction, step, t], devs[direction]).wait_recv()
            return ref

        return steps, first, send, wait

    zsteps, zfirst, zgo, zwait = chain((dk, dv), zin, zsum, z_send, z_recv, zdev, z, NZ, (0, 1))
    xsteps, xfirst, xgo, xwait = chain((o, dq), xin, xsum, x_send, x_recv, xdev, x, NX, (0, 1))

    def both(go, first, step):
        for late in (True, False):
            for direction in range(2):
                for t in range(2):
                    if step >= first(direction, t) and (first(direction, t) == 1) == late:
                        go(direction, step, t)

    both(zgo, zfirst, 0)
    both(xgo, xfirst, 0)
    for step in range(1, zsteps):
        both(zgo, zfirst, step)
        if step < xsteps:
            both(xgo, xfirst, step)

    outs = (o_out, dq_out, dk_out, dv_out)
    here = pl.ds(pl.multiple_of(c * PAIR, PAIR), PAIR)

    def finish(n, parts, t, pos, wait, steps):
        a = wait(0, steps - 1, t)
        b = wait(1, steps - 1, t)
        mine = parts[t].at[pl.ds(2 * pos, 2)]
        final[n] = (mine[1 - c].astype(f32) + a[1 - c].astype(f32) + b[1 - c].astype(f32)).astype(jnp.bfloat16)
        go_on(remote(final.at[n], outs[n].at[:, here], f_send.at[n], f_recv.at[n], partner))
        outs[n][:, here] = (mine[c].astype(f32) + a[c].astype(f32) + b[c].astype(f32)).astype(jnp.bfloat16)

    for t in range(2):
        finish(t, (o, dq), t, x, xwait, xsteps)
    for t in (1, 0):
        finish(2 + t, (dk, dv), t, z, zwait, zsteps)
    there = pl.ds(pl.multiple_of((1 - c) * PAIR, PAIR), PAIR)
    for n in (0, 1, 3, 2):
        remote(final.at[n], outs[n].at[:, there], f_send.at[n], f_recv.at[n], partner).wait_recv()
    for cp in sends:
        cp.wait_send()


def vmem():
    return pl.BlockSpec(memory_space=pltpu.VMEM)


def smem():
    return pl.BlockSpec(memory_space=pltpu.SMEM)


def on_device(query_rows, key_rows, value_rows, out_grad, random_blocks):
    bf16, f32 = jnp.bfloat16, jnp.float32
    dma = pltpu.SemaphoreType.DMA
    lists = random_blocks.reshape(-1)
    column = jax.ShapeDtypeStruct((COL, BLK, PAIR), bf16)
    row = jax.ShapeDtypeStruct((ROW, BLK, PAIR), bf16)
    gathered = pl.pallas_call(
        gather_kernel,
        out_shape=(column, column, row, row, jax.ShapeDtypeStruct((NX, 3, 2 * ROW, HD), f32)),
        in_specs=[smem()] + [vmem()] * 4,
        out_specs=[vmem()] * 5,
        scratch_shapes=[
            dma((3, 2 * NY)), dma((3, 2 * NY)), dma((4,)), dma, dma,
            dma((2, NZ // 2, 2)), dma((2, NZ // 2, 2)),
            dma((2, NX // 2, 2)), dma((2, NX // 2, 2)),
            dma((NX,)), dma((NX,)),
        ],
        compiler_params=pltpu.CompilerParams(collective_id=0, has_side_effects=True),
        name="gather",
    )(lists, query_rows, key_rows, value_rows, out_grad)
    parts = pl.pallas_call(
        grad_kernel,
        out_shape=(column, column, row, row),
        in_specs=[smem()] + [vmem()] * 5,
        out_specs=[vmem()] * 4,
        scratch_shapes=[pltpu.VMEM((COL, BLK, PAIR), f32)] * 2,
        name="grads",
    )(lists, *gathered)
    full = jax.ShapeDtypeStruct((BLK, 2 * PAIR), bf16)
    return pl.pallas_call(
        reduce_kernel,
        out_shape=(full,) * 4,
        in_specs=[vmem()] * 4,
        out_specs=[vmem()] * 4,
        scratch_shapes=[
            pltpu.VMEM((2, NZ // 2, 2, 2, BLK, PAIR), bf16), pltpu.VMEM((2, NZ // 2, 2, 2, BLK, PAIR), bf16),
            pltpu.VMEM((2, NX // 2, 2, 2, BLK, PAIR), bf16), pltpu.VMEM((2, NX // 2, 2, 2, BLK, PAIR), bf16),
            pltpu.VMEM((4, BLK, PAIR), bf16),
            dma((2, NZ // 2, 2)), dma((2, NZ // 2, 2)),
            dma((2, NX // 2, 2)), dma((2, NX // 2, 2)),
            dma((4,)), dma((4,)),
        ],
        compiler_params=pltpu.CompilerParams(collective_id=1, has_side_effects=True),
        name="reduce",
    )(*parts)


def solution(mesh):
    in_specs = (
        P(("seq", "head"), None),
        P(("seq", "head"), None),
        P(("seq", "head"), None),
        P("seq", "head"),
        P("head", None, None),
    )
    out_specs = (P("seq", "head"),) * 4
    return jax.shard_map(
        on_device, mesh=mesh, in_specs=in_specs, out_specs=out_specs, check_vma=False
    )
```

```python
import math

import jax
import jax.numpy as jnp
from jax import lax
from jax.experimental import pallas as pl
from jax.experimental.pallas import tpu as pltpu
from jax.sharding import PartitionSpec as P

HD = 128
BLK = 128
NX = 4
NZ = 8
NY = 4
PAIR = 2 * HD
COL = 2 * NZ
ROW = 2 * NX
SCALE = 1.0 / math.sqrt(HD)
NEG = -1e30
GROUP = 4
MESH = pl.DeviceIdType.MESH
NT = (((1,), (1,)), ((), ()))
NN = (((1,), (0,)), ((), ()))
TN = (((0,), (0,)), ((), ()))


def dot(a, b, dims):
    return lax.dot_general(a, b, dims, preferred_element_type=jnp.float32)


def position():
    s = lax.axis_index("seq")
    y = lax.axis_index("head")
    x = s // (2 * NZ)
    z = (s // 2) % NZ
    c = s % 2
    return x, z, c, y


def place_of(x, z, c):
    return (x * NZ + z) * 2 + c


def remote(src, dst, send_sem, recv_sem, dev):
    return pltpu.make_async_remote_copy(
        src_ref=src, dst_ref=dst, send_sem=send_sem, recv_sem=recv_sem,
        device_id=dev, device_id_type=MESH,
    )


def meet(devs):
    barrier = pltpu.get_barrier_semaphore()
    for dev in devs:
        pl.semaphore_signal(barrier, inc=1, device_id=dev, device_id_type=MESH)
    pl.semaphore_wait(barrier, len(devs))


def unit_slots(xr, cb, x, z, c, h, rb_ref):
    xq = (x + xr) % NX
    block = COL * xq + 2 * z + cb
    slots = []
    for r in range(3):
        j = rb_ref[r, 2 * c + h, block] - COL * x
        here = (j >= 0) & (j < COL)
        slots.append((jnp.clip(j, 0, COL - 1), jnp.where(here, 0.0, NEG)))
    edge = (x == 0) | (x == NX - 1)
    slots.append((jnp.where(x == NX - 1, COL - 1, 0), jnp.where(edge, 0.0, NEG)))
    if xr == 0:
        slots.append((2 * z, None))
        slots.append((2 * z + 1, None))
    if cb == 0 and xr in (0, 1):
        ok = (z != 0) if xr == 0 else (z == 0)
        slots.append(((2 * z + COL - 1) % COL, jnp.where(ok, 0.0, NEG)))
    if cb == 1 and xr in (0, NX - 1):
        ok = (z != NZ - 1) if xr == 0 else (z == NZ - 1)
        slots.append(((2 * z + 2) % COL, jnp.where(ok, 0.0, NEG)))
    return xq, slots


def gather_kernel(rb_ref, q_ref, k_ref, v_ref, g_ref, kall, vall, qrow, grow, stats,
                  a_send, a_recv, a_own, g_send, g_recv, z_send, z_recv, x_send, x_recv, s_send, s_recv):
    x, z, c, y = position()
    me = y * 2 + c

    def member(d):
        other = (me + d) % (2 * NY)
        return other % 2, other // 2

    def at(xx, zz):
        return (place_of(xx, zz, c), y)

    group = []
    for d in range(1, 2 * NY):
        cc, yy = member(d)
        group.append((place_of(x, z, cc), yy))
    zdev = (at(x, (z + 1) % NZ), at(x, (z + NZ - 1) % NZ))
    xdev = [at((x + d) % NX, z) for d in range(1, NX)]
    partner = (place_of(x, z, 1 - c), y)
    meet(group + list(zdev) + xdev)

    def cols(cc, yy):
        return pl.ds(pl.multiple_of((yy * 2 + cc) * PAIR, PAIR), PAIR)

    rows = pl.ds(pl.multiple_of(y * 32, 32), 32)
    ins = (k_ref, v_ref, q_ref)
    bufs = (kall, vall, qrow)
    slot = (2 * z, 2 * z, 2 * x)
    sends = []
    own = []
    for t in range(3):
        dst = bufs[t].at[slot[t] + c, rows, :]
        for d in range(1, 2 * NY):
            cc, yy = member(d)
            cp = remote(ins[t].at[:, cols(cc, yy)], dst, a_send.at[t, d], a_recv.at[t, d], group[d - 1])
            cp.start()
            sends.append(cp)
        cp = pltpu.make_async_copy(ins[t].at[:, cols(c, y)], dst, a_own.at[t])
        cp.start()
        own.append(cp)
        if t == 1:
            gs = remote(g_ref.at[:, pl.ds(pl.multiple_of((1 - c) * PAIR, PAIR), PAIR)], grow.at[2 * x + c],
                        g_send, g_recv, partner)
            gs.start()
            sends.append(gs)
            go = pltpu.make_async_copy(g_ref.at[:, pl.ds(pl.multiple_of(c * PAIR, PAIR), PAIR)],
                                       grow.at[2 * x + c], a_own.at[3])
            go.start()

    def arrived(t):
        own[t].wait()
        for d in range(1, 2 * NY):
            other = (me + 2 * NY - d) % (2 * NY)
            cs, ys = other % 2, other // 2
            dst = bufs[t].at[slot[t] + cs, pl.ds(pl.multiple_of(ys * 32, 32), 32), :]
            remote(dst, dst, a_send.at[t, d], a_recv.at[t, d], partner).wait_recv()

    def zpiece(t, owner):
        return (kall, vall)[t].at[pl.ds(2 * owner, 2)]

    def zcopy(direction, step, t):
        owner = (z - step + NZ) % NZ if direction == 0 else (z + step) % NZ
        ref = zpiece(t, owner)
        return remote(ref, ref, z_send.at[direction, step, t], z_recv.at[direction, step, t], zdev[direction])

    def zwait(direction, step, t):
        owner = (z - 1 - step + NZ) % NZ if direction == 0 else (z + 1 + step) % NZ
        ref = zpiece(t, owner)
        remote(ref, ref, z_send.at[direction, step, t], z_recv.at[direction, step, t], zdev[direction]).wait_recv()

    def xpiece(t, owner):
        return (qrow, grow)[t].at[pl.ds(2 * owner, 2)]

    def xcopy(direction, step, t):
        owner = (x - step + NX) % NX if direction == 0 else (x + step) % NX
        ref = xpiece(t, owner)
        return remote(ref, ref, x_send.at[direction, step, t], x_recv.at[direction, step, t],
                      xdev[0] if direction == 0 else xdev[NX - 2])

    def xwait(direction, step, t):
        owner = (x - 1 - step + NX) % NX if direction == 0 else (x + 1 + step) % NX
        ref = xpiece(t, owner)
        remote(ref, ref, x_send.at[direction, step, t], x_recv.at[direction, step, t], xdev[0]).wait_recv()

    def go_on(cp):
        cp.start()
        sends.append(cp)

    for t in range(2):
        arrived(t)
        for direction in range(2):
            go_on(zcopy(direction, 0, t))
    go.wait()
    remote(grow.at[2 * x + 1 - c], grow.at[2 * x + 1 - c], g_send, g_recv, partner).wait_recv()
    for direction in range(2):
        go_on(xcopy(direction, 0, 1))
    arrived(2)
    for direction in range(2):
        go_on(xcopy(direction, 0, 0))
    last = NZ // 2 - 1
    for step in range(last):
        for t in range(2):
            for direction in range(2):
                zwait(direction, step, t)
                if step + 1 < last or direction == t:
                    go_on(zcopy(direction, step + 1, t))
        if step == 0:
            for t in (1, 0):
                for direction in range(2):
                    xwait(direction, 0, t)
                    if direction == t:
                        go_on(xcopy(direction, 1, t))
    for t in range(2):
        xwait(t, 1, t)
    for t in range(2):
        zwait(t, last, t)

    def one_head(h, carry):
        lanes = pl.ds(pl.multiple_of(h * HD, HD), HD)
        for xr in range(NX):
            for cb in range(2):
                xq, slots = unit_slots(xr, cb, x, z, c, h, rb_ref)
                q = qrow[2 * xq + cb, :, lanes]
                g = grow[2 * xq + cb, :, lanes]
                scores = []
                for j, bias in slots:
                    sc = dot(kall[j, :, lanes], q, NT) * SCALE
                    scores.append(sc if bias is None else sc + bias)
                peak = scores[0]
                for sc in scores[1:]:
                    peak = jnp.maximum(peak, sc)
                peak = jnp.max(peak, axis=0, keepdims=True)
                total = None
                weighted = None
                for (j, _), sc in zip(slots, scores):
                    e = jnp.exp(sc - peak)
                    w = e * dot(vall[j, :, lanes], g, NT)
                    total = e if total is None else total + e
                    weighted = w if weighted is None else weighted + w
                u = h * ROW + 2 * xq + cb
                stats[x, 0, pl.ds(u, 1), :] = peak
                stats[x, 1, pl.ds(u, 1), :] = jnp.sum(total, axis=0, keepdims=True)
                stats[x, 2, pl.ds(u, 1), :] = jnp.sum(weighted, axis=0, keepdims=True)
        return carry

    lax.fori_loop(0, 2, one_head, 0)
    for d in range(1, NX):
        go_on(remote(stats.at[x], stats.at[x], s_send.at[d], s_recv.at[d], xdev[d - 1]))
    for d in range(1, NX):
        src = (x + NX - d) % NX
        remote(stats.at[src], stats.at[src], s_send.at[d], s_recv.at[d], xdev[d - 1]).wait_recv()
    for cp in sends:
        cp.wait_send()


def grad_kernel(rb_ref, kall, vall, qrow, grow, stats, dk_ref, dv_ref, o_ref, dq_ref,
                dk_acc, dv_acc, o_acc, dq_acc, peak_ref, inv_ref, delta_ref, todo):
    x, z, c, _ = position()
    bf16 = jnp.bfloat16

    peaks = [stats[i, 0] for i in range(NX)]
    peak = jnp.maximum(jnp.maximum(peaks[0], peaks[1]), jnp.maximum(peaks[2], peaks[3]))
    shift = [jnp.exp(p - peak) for p in peaks]
    inverse = 1.0 / sum(stats[i, 1] * shift[i] for i in range(NX))
    peak_ref[...] = peak
    inv_ref[...] = inverse
    delta_ref[...] = sum(stats[i, 2] * shift[i] for i in range(NX)) * inverse

    for acc in (dk_acc, dv_acc, o_acc, dq_acc):
        acc[...] = jnp.zeros_like(acc)

    count = jnp.int32(0)
    for h in range(2):
        ql = 2 * ((x + jnp.where(z == 0, 1, 0)) % NX)
        qr = 2 * ((x + jnp.where(z == NZ - 1, NX - 1, 0)) % NX) + 1
        todo[count] = ((h * ROW + ql) * COL) + (2 * z + COL - 1) % COL
        todo[count + 1] = ((h * ROW + qr) * COL) + (2 * z + 2) % COL
        count = count + 2
    for h in range(2):
        for i in range(ROW):
            for r in range(3):
                j = rb_ref[r, 2 * c + h, COL * (i // 2) + 2 * z + i % 2] - COL * x
                here = (j >= 0) & (j < COL)
                todo[count] = (h * ROW + i) * COL + j
                count = count + here.astype(jnp.int32)

    def pair_grads(k, v, q, g, peak, inverse, delta, bias):
        sc = dot(k, q, NT) * SCALE
        w = jnp.exp(sc - peak) * inverse
        if bias is not None:
            w = w * bias
        ds = (w * (dot(v, g, NT) - delta)).astype(bf16)
        return w.astype(bf16), ds

    @pl.when((x == 0) | (x == NX - 1))
    def _():
        j = jnp.where(x == 0, 0, COL - 1)
        for h in range(2):
            lanes = slice(h * HD, (h + 1) * HD)
            k, v = kall[j, :, lanes], vall[j, :, lanes]
            dk = dv = None
            for i in range(0, ROW, 2):
                u = h * ROW + i
                rows = [jnp.concatenate([ref[u:u + 1, :], ref[u + 1:u + 2, :]], axis=1)
                        for ref in (peak_ref, inv_ref, delta_ref)]
                q = qrow[i:i + 2, :, lanes].reshape(2 * BLK, HD)
                g = grow[i:i + 2, :, lanes].reshape(2 * BLK, HD)
                wb, ds = pair_grads(k, v, q, g, *rows, None)
                dv1, dk1 = dot(wb, g, NN), dot(ds, q, NN)
                dv = dv1 if dv is None else dv + dv1
                dk = dk1 if dk is None else dk + dk1
                o_acc[i:i + 2, :, lanes] = dot(wb, v, TN).reshape(2, BLK, HD)
                dq_acc[i:i + 2, :, lanes] = dot(ds, k, TN).reshape(2, BLK, HD)
            dk_acc[j, :, lanes] = dk
            dv_acc[j, :, lanes] = dv

    for h in range(2):
        lanes = slice(h * HD, (h + 1) * HD)
        mine = pl.ds(2 * z, 2)
        own = pl.ds(2 * x, 2)
        k = kall[mine, :, lanes].reshape(2 * BLK, HD)
        v = vall[mine, :, lanes].reshape(2 * BLK, HD)
        q = qrow[own, :, lanes].reshape(2 * BLK, HD)
        g = grow[own, :, lanes].reshape(2 * BLK, HD)
        u = h * ROW + 2 * x
        rows = [jnp.concatenate([ref[pl.ds(u, 1), :], ref[pl.ds(u + 1, 1), :]], axis=1)
                for ref in (peak_ref, inv_ref, delta_ref)]
        wb, ds = pair_grads(k, v, q, g, *rows, None)
        dv_acc[mine, :, lanes] += dot(wb, g, NN).reshape(2, BLK, HD)
        dk_acc[mine, :, lanes] += dot(ds, q, NN).reshape(2, BLK, HD)
        o_acc[own, :, lanes] += dot(wb, v, TN).reshape(2, BLK, HD)
        dq_acc[own, :, lanes] += dot(ds, k, TN).reshape(2, BLK, HD)

    def group(n, carry):
        done = []
        for t in range(GROUP):
            at = n * GROUP + t
            good = at < count
            code = jnp.where(good, todo[at], todo[0])
            u, j = code // COL, code % COL
            h, i = u // ROW, u % ROW
            lanes = pl.ds(pl.multiple_of(h * HD, HD), HD)
            k, v = kall[j, :, lanes], vall[j, :, lanes]
            q, g = qrow[i, :, lanes], grow[i, :, lanes]
            wb, ds = pair_grads(k, v, q, g, peak_ref[pl.ds(u, 1), :], inv_ref[pl.ds(u, 1), :],
                                delta_ref[pl.ds(u, 1), :], jnp.where(good, 1.0, 0.0))
            done.append((i, j, lanes, dot(wb, g, NN), dot(ds, q, NN), dot(wb, v, TN), dot(ds, k, TN)))
        for i, j, lanes, dv, dk, o, dq in done:
            dv_acc[j, :, lanes] += dv
            dk_acc[j, :, lanes] += dk
            o_acc[i, :, lanes] += o
            dq_acc[i, :, lanes] += dq
        return carry

    lax.fori_loop(0, (count + GROUP - 1) // GROUP, group, 0)
    dk_ref[...] = (dk_acc[...] * SCALE).astype(bf16)
    dv_ref[...] = dv_acc[...].astype(bf16)
    o_ref[...] = o_acc[...].astype(bf16)
    dq_ref[...] = (dq_acc[...] * SCALE).astype(bf16)


def place_kernel(*refs):
    for n in range(4):
        refs[4 + n][...] = refs[n][...]


def reduce_kernel(dk, dv, o, dq, o_out, dq_out, dk_out, dv_out,
                  zin, zsum, xin, xsum, final, z_send, z_recv, x_send, x_recv, f_send, f_recv):
    x, z, c, y = position()

    def at(xx, zz):
        return (place_of(xx, zz, c), y)

    zdev = (at(x, (z + 1) % NZ), at(x, (z + NZ - 1) % NZ))
    xdev = (at((x + 1) % NX, z), at((x + NX - 1) % NX, z))
    partner = (place_of(x, z, 1 - c), y)
    meet(list(zdev) + list(xdev) + [partner])
    sends = []
    f32 = jnp.float32

    def go_on(cp):
        cp.start()
        sends.append(cp)

    def chain(parts, arrive, summed, ssem, rsem, devs, pos, count, half):
        steps = count // 2

        def target(direction, step):
            away = steps - step
            return (pos + away) % count if direction == 0 else (pos + count - away) % count

        def first(direction, t):
            return 0 if t == half[direction] else 1

        def send(direction, step, t):
            mine = parts[t].at[pl.ds(2 * target(direction, step), 2)]
            if step == first(direction, t):
                src = mine
            else:
                src = summed.at[direction, step, t]
                got = wait(direction, step - 1, t)
                src[...] = (got[...].astype(f32) + mine[...].astype(f32)).astype(jnp.bfloat16)
            go_on(remote(src, arrive.at[direction, step, t], ssem.at[direction, step, t],
                         rsem.at[direction, step, t], devs[direction]))

        def wait(direction, step, t):
            ref = arrive.at[direction, step, t]
            remote(ref, ref, ssem.at[direction, step, t], rsem.at[direction, step, t], devs[direction]).wait_recv()
            return ref

        return steps, first, send, wait

    zsteps, zfirst, zgo, zwait = chain((dk, dv), zin, zsum, z_send, z_recv, zdev, z, NZ, (0, 1))
    xsteps, xfirst, xgo, xwait = chain((o, dq), xin, xsum, x_send, x_recv, xdev, x, NX, (0, 1))

    def both(go, first, step):
        for late in (True, False):
            for direction in range(2):
                for t in range(2):
                    if step >= first(direction, t) and (first(direction, t) == 1) == late:
                        go(direction, step, t)

    both(zgo, zfirst, 0)
    both(xgo, xfirst, 0)
    for step in range(1, zsteps):
        both(zgo, zfirst, step)
        if step < xsteps:
            both(xgo, xfirst, step)

    outs = (o_out, dq_out, dk_out, dv_out)
    here = pl.ds(pl.multiple_of(c * PAIR, PAIR), PAIR)

    def finish(n, parts, t, pos, wait, steps):
        a = wait(0, steps - 1, t)
        b = wait(1, steps - 1, t)
        mine = parts[t].at[pl.ds(2 * pos, 2)]
        final[n] = (mine[1 - c].astype(f32) + a[1 - c].astype(f32) + b[1 - c].astype(f32)).astype(jnp.bfloat16)
        go_on(remote(final.at[n], outs[n].at[:, here], f_send.at[n], f_recv.at[n], partner))
        outs[n][:, here] = (mine[c].astype(f32) + a[c].astype(f32) + b[c].astype(f32)).astype(jnp.bfloat16)

    for t in range(2):
        finish(t, (o, dq), t, x, xwait, xsteps)
    for t in (1, 0):
        finish(2 + t, (dk, dv), t, z, zwait, zsteps)
    there = pl.ds(pl.multiple_of((1 - c) * PAIR, PAIR), PAIR)
    for n in (0, 1, 3, 2):
        remote(final.at[n], outs[n].at[:, there], f_send.at[n], f_recv.at[n], partner).wait_recv()
    for cp in sends:
        cp.wait_send()


def vmem():
    return pl.BlockSpec(memory_space=pltpu.VMEM)


def smem():
    return pl.BlockSpec(memory_space=pltpu.SMEM)


def on_device(query_rows, key_rows, value_rows, out_grad, random_blocks):
    bf16, f32 = jnp.bfloat16, jnp.float32
    dma = pltpu.SemaphoreType.DMA
    lists = random_blocks.transpose(2, 0, 1)
    column = jax.ShapeDtypeStruct((COL, BLK, PAIR), bf16)
    row = jax.ShapeDtypeStruct((ROW, BLK, PAIR), bf16)
    gathered = pl.pallas_call(
        gather_kernel,
        out_shape=(column, column, row, row, jax.ShapeDtypeStruct((NX, 3, 2 * ROW, HD), f32)),
        in_specs=[smem()] + [vmem()] * 4,
        out_specs=[vmem()] * 5,
        scratch_shapes=[
            dma((3, 2 * NY)), dma((3, 2 * NY)), dma((4,)), dma, dma,
            dma((2, NZ // 2, 2)), dma((2, NZ // 2, 2)),
            dma((2, NX // 2, 2)), dma((2, NX // 2, 2)),
            dma((NX,)), dma((NX,)),
        ],
        compiler_params=pltpu.CompilerParams(collective_id=0, has_side_effects=True),
        name="gather",
    )(lists, query_rows, key_rows, value_rows, out_grad)
    parts = pl.pallas_call(
        grad_kernel,
        out_shape=(column, column, row, row),
        in_specs=[smem()] + [vmem()] * 5,
        out_specs=[vmem()] * 4,
        scratch_shapes=[pltpu.VMEM((COL, BLK, PAIR), f32)] * 2 + [pltpu.VMEM((ROW, BLK, PAIR), f32)] * 2
        + [pltpu.VMEM((2 * ROW, HD), f32)] * 3 + [pltpu.SMEM((6 * ROW + 16,), jnp.int32)],
        name="grads",
    )(lists, *gathered)
    full = jax.ShapeDtypeStruct((BLK, 2 * PAIR), bf16)
    outs = pl.pallas_call(
        reduce_kernel,
        out_shape=(full,) * 4,
        in_specs=[vmem()] * 4,
        out_specs=[vmem()] * 4,
        scratch_shapes=[
            pltpu.VMEM((2, NZ // 2, 2, 2, BLK, PAIR), bf16), pltpu.VMEM((2, NZ // 2, 2, 2, BLK, PAIR), bf16),
            pltpu.VMEM((2, NX // 2, 2, 2, BLK, PAIR), bf16), pltpu.VMEM((2, NX // 2, 2, 2, BLK, PAIR), bf16),
            pltpu.VMEM((4, BLK, PAIR), bf16),
            dma((2, NZ // 2, 2)), dma((2, NZ // 2, 2)),
            dma((2, NX // 2, 2)), dma((2, NX // 2, 2)),
            dma((4,)), dma((4,)),
        ],
        compiler_params=pltpu.CompilerParams(collective_id=1, has_side_effects=True),
        name="reduce",
    )(*parts)
    return pl.pallas_call(
        place_kernel,
        out_shape=(full,) * 4,
        in_specs=[vmem()] * 4,
        out_specs=[vmem()] * 4,
        name="place",
    )(*outs)


def solution(mesh):
    in_specs = (
        P(("seq", "head"), None),
        P(("seq", "head"), None),
        P(("seq", "head"), None),
        P("seq", "head"),
        P("head", None, None),
    )
    out_specs = (P("seq", "head"),) * 4
    return jax.shard_map(
        on_device, mesh=mesh, in_specs=in_specs, out_specs=out_specs, check_vma=False
    )
```

```python
import math

import jax
import jax.numpy as jnp
from jax import lax
from jax.experimental import pallas as pl
from jax.experimental.pallas import tpu as pltpu
from jax.sharding import PartitionSpec as P

HD = 128
BLK = 128
NX = 4
NZ = 8
NY = 4
COL = 2 * NZ
ROW = 2 * NX
RAND = 3
LEFT = RAND * ROW
RIGHT = LEFT + 1
WIDE = LEFT + 2
ENTRIES = LEFT + 3
SCALE = 1.0 / math.sqrt(HD)
NEG = -1e30
MESH = pl.DeviceIdType.MESH
NT = (((1,), (1,)), ((), ()))
NN = (((1,), (0,)), ((), ()))
TN = (((0,), (0,)), ((), ()))
F32 = jnp.float32
BF16 = jnp.bfloat16


def dot(a, b, dims):
    return lax.dot_general(a, b, dims, preferred_element_type=F32)


def place_of(x, z, c):
    return (x * NZ + z) * 2 + c


def remote(src, dst, send_sem, recv_sem, dev):
    return pltpu.make_async_remote_copy(
        src_ref=src, dst_ref=dst, send_sem=send_sem, recv_sem=recv_sem,
        device_id=dev, device_id_type=MESH,
    )


def meet(devs):
    barrier = pltpu.get_barrier_semaphore()
    for dev in devs:
        pl.semaphore_signal(barrier, inc=1, device_id=dev, device_id_type=MESH)
    pl.semaphore_wait(barrier, len(devs))


def attention_kernel(rb_ref, q_ref, k_ref, v_ref, g_ref, o_out, dq_out, dk_out, dv_out,
                     kall0, kall1, vall0, vall1, qrow0, qrow1, grow0, grow1, sets, stats, rows, acc, wide_acc, own_acc, o_acc, dq_acc,
                     zin, zsum, xin, xsum, final, owner_s, prev_s, last_s,
                     a_send, a_recv, a_own, g_send, g_recv, g_own, z_send, z_recv, x_send, x_recv, s_send, s_recv,
                     rz_send, rz_recv, rx_send, rx_recv, f_send, f_recv):
    s = lax.axis_index("seq")
    y = lax.axis_index("head")
    x = s // (2 * NZ)
    z = (s // 2) % NZ
    c = s % 2
    me = y * 2 + c
    kall, vall, qrow, grow = (kall0, kall1), (vall0, vall1), (qrow0, qrow1), (grow0, grow1)

    def member(d):
        other = (me + d) % (2 * NY)
        return other % 2, other // 2

    def at(xx, zz):
        return (place_of(xx, zz, c), y)

    group = []
    for d in range(1, 2 * NY):
        cc, yy = member(d)
        group.append((place_of(x, z, cc), yy))
    zdev = (at(x, (z + 1) % NZ), at(x, (z + NZ - 1) % NZ))
    xall = [at((x + d) % NX, z) for d in range(1, NX)]
    xdev = (xall[0], xall[NX - 2])
    partner = (place_of(x, z, 1 - c), y)
    meet(group + list(zdev) + xall)

    sends = []

    def go_on(cp):
        cp.start()
        sends.append(cp)

    def lanes_of(n):
        return pl.ds(pl.multiple_of(n * HD, HD), HD)

    ins = (k_ref, v_ref, q_ref)
    bufs = (kall, vall, qrow)
    slot = (2 * z, 2 * z, 2 * x)
    own = {}

    def exchange(h, t):
        dst = bufs[t][h].at[slot[t] + c, pl.ds(pl.multiple_of(y * 32, 32), 32), :]
        for d in range(1, 2 * NY):
            cc, yy = member(d)
            go_on(remote(ins[t].at[:, lanes_of(yy * 4 + cc * 2 + h)], dst, a_send.at[h, t, d], a_recv.at[h, t, d],
                         group[d - 1]))
        own[h, t] = pltpu.make_async_copy(ins[t].at[:, lanes_of(me * 2 + h)], dst, a_own.at[h, t])
        own[h, t].start()

    def exchange_grad(h):
        go_on(remote(g_ref.at[:, lanes_of(2 * (1 - c) + h)], grow[h].at[2 * x + c], g_send.at[h], g_recv.at[h], partner))
        own[h, 3] = pltpu.make_async_copy(g_ref.at[:, lanes_of(2 * c + h)], grow[h].at[2 * x + c], g_own.at[h])
        own[h, 3].start()

    def arrived(h, t):
        own[h, t].wait()
        for d in range(1, 2 * NY):
            other = (me + 2 * NY - d) % (2 * NY)
            cs, ys = other % 2, other // 2
            dst = bufs[t][h].at[slot[t] + cs, pl.ds(pl.multiple_of(ys * 32, 32), 32), :]
            remote(dst, dst, a_send.at[h, t, d], a_recv.at[h, t, d], partner).wait_recv()

    def arrived_grad(h):
        own[h, 3].wait()
        dst = grow[h].at[2 * x + 1 - c]
        remote(dst, dst, g_send.at[h], g_recv.at[h], partner).wait_recv()

    def ring(bufs2, send, recv, devs, pos, count):
        def piece(h, t, owner):
            return bufs2[t][h].at[pl.ds(2 * owner, 2)]

        def copy(h, direction, step, t):
            owner = (pos + count - step) % count if direction == 0 else (pos + step) % count
            ref = piece(h, t, owner)
            go_on(remote(ref, ref, send.at[h, direction, step, t], recv.at[h, direction, step, t], devs[direction]))

        def wait(h, direction, step, t):
            owner = (pos + count - 1 - step) % count if direction == 0 else (pos + 1 + step) % count
            ref = piece(h, t, owner)
            remote(ref, ref, send.at[h, direction, step, t], recv.at[h, direction, step, t],
                   devs[direction]).wait_recv()

        return copy, wait

    zcopy, zwait = ring((kall, vall), z_send, z_recv, zdev, z, NZ)
    xcopy, xwait = ring((qrow, grow), x_send, x_recv, xdev, x, NX)
    zlast = NZ // 2 - 1

    def zstart(h):
        for t in range(2):
            arrived(h, t)
            for direction in range(2):
                zcopy(h, direction, 0, t)

    def xstart(h):
        arrived_grad(h)
        for direction in range(2):
            xcopy(h, direction, 0, 1)
        arrived(h, 2)
        for direction in range(2):
            xcopy(h, direction, 0, 0)

    def zstep(h, step):
        for t in range(2):
            for direction in range(2):
                zwait(h, direction, step, t)
                if step + 1 < zlast or direction == t:
                    zcopy(h, direction, step + 1, t)

    def xstep(h):
        for t in (1, 0):
            for direction in range(2):
                xwait(h, direction, 0, t)
                if direction == t:
                    xcopy(h, direction, 1, t)

    def zend(h):
        for t in range(2):
            zwait(h, t, zlast, t)

    def xend(h):
        for t in range(2):
            xwait(h, t, 1, t)

    edge = (x == 0) | (x == NX - 1)
    wide_at = jnp.where(x == 0, 0, COL - 1)
    left_q = 2 * ((x + jnp.where(z == 0, 1, 0)) % NX)
    right_q = 2 * ((x + jnp.where(z == NZ - 1, NX - 1, 0)) % NX) + 1
    left_k = (2 * z + COL - 1) % COL
    right_k = (2 * z + 2) % COL

    def plan(h):
        owners = []
        for i in range(ROW):
            for r in range(RAND):
                j = rb_ref[r, 2 * c + h, COL * (i // 2) + 2 * z + i % 2] - COL * x
                owners.append(jnp.where((j >= 0) & (j < COL), j, -1))
        owners += [left_k, right_k, jnp.where(edge, wide_at, -1)]
        for e in range(ENTRIES):
            prev = jnp.int32(-1)
            for f in range(e):
                prev = jnp.where(owners[f] == owners[e], f, prev)
            owner_s[h * ENTRIES + e] = owners[e]
            prev_s[h * ENTRIES + e] = prev
        for j in range(COL):
            last = jnp.int32(-1)
            for e in range(ENTRIES):
                last = jnp.where(owners[e] == j, e, last)
            last_s[h * COL + j] = last

    def listed(h, e):
        j = owner_s[h * ENTRIES + e]
        return jnp.maximum(j, 0), jnp.where(j < 0, NEG, 0.0)

    wide_bias = jnp.where(edge, 0.0, NEG)

    def measure(ks, vs, q, g):
        scores = []
        for k, bias in ks:
            sc = dot(k, q, NT) * SCALE
            scores.append(sc if bias is None else sc + bias)
        peak = scores[0]
        for sc in scores[1:]:
            peak = jnp.maximum(peak, sc)
        peak = jnp.max(peak, axis=0, keepdims=True)
        total = weighted = None
        for v, sc in zip(vs, scores):
            e = jnp.exp(sc - peak)
            w = e * dot(v, g, NT)
            total = e if total is None else total + e
            weighted = w if weighted is None else weighted + w
        return peak, jnp.sum(total, axis=0, keepdims=True), jnp.sum(weighted, axis=0, keepdims=True)

    def window(h):
        mine = pl.ds(2 * z, 2)
        here = pl.ds(2 * x, 2)
        return tuple(ref[h][at_, :, :].reshape(2 * BLK, HD)
                     for ref, at_ in ((kall, mine), (vall, mine), (qrow, here), (grow, here)))

    def count_units(h, units):
        for i in units:
            ks, vs = [], []
            for r in range(RAND):
                j, bias = listed(h, RAND * i + r)
                ks.append((kall[h][j], bias))
                vs.append(vall[h][j])
            ks.append((kall[h][wide_at], wide_bias))
            vs.append(vall[h][wide_at])
            for n, row in enumerate(measure(ks, vs, qrow[h][i], grow[h][i])):
                sets[h, 0, n, i:i + 1, :] = row

    def count_rest(h):
        for part in range(1, 4):
            sets[h, part, 0] = jnp.full((ROW, HD), NEG, F32)
            sets[h, part, 1] = jnp.zeros((ROW, HD), F32)
            sets[h, part, 2] = jnp.zeros((ROW, HD), F32)
        k, v, q, g = window(h)
        for n, row in enumerate(measure([(k, None)], [v], q, g)):
            sets[h, 1, n, pl.ds(2 * x, 1), :] = row[:, :HD]
            sets[h, 1, n, pl.ds(2 * x + 1, 1), :] = row[:, HD:]
        for part, qi, kj in ((2, left_q, left_k), (3, right_q, right_k)):
            for n, row in enumerate(measure([(kall[h][kj], None)], [vall[h][kj]], qrow[h][qi], grow[h][qi])):
                sets[h, part, n, pl.ds(qi, 1), :] = row

    def merge(parts):
        peak = jnp.maximum(jnp.maximum(parts[0][0], parts[1][0]), jnp.maximum(parts[2][0], parts[3][0]))
        shift = [jnp.exp(p[0] - peak) for p in parts]
        total = sum(p[1] * f for p, f in zip(parts, shift))
        return peak, total, sum(p[2] * f for p, f in zip(parts, shift))

    def send_stats(h):
        for n, value in enumerate(merge([[sets[h, part, n] for n in range(3)] for part in range(4)])):
            stats[h, x, n] = value
        for d in range(1, NX):
            go_on(remote(stats.at[h, x], stats.at[h, x], s_send.at[h, d], s_recv.at[h, d], xall[d - 1]))

    def take_stats(h):
        for d in range(1, NX):
            src = (x + NX - d) % NX
            remote(stats.at[h, src], stats.at[h, src], s_send.at[h, d], s_recv.at[h, d], xall[d - 1]).wait_recv()
        peak, total, weighted = merge([[stats[h, i, n] for n in range(3)] for i in range(NX)])
        inverse = 1.0 / total
        rows[h, 0] = peak
        rows[h, 1] = inverse
        rows[h, 2] = weighted * inverse

    def weigh(k, v, q, g, row, bias):
        peak, inverse, delta = row
        sc = dot(k, q, NT) * SCALE
        if bias is not None:
            sc = sc + bias
        w = jnp.exp(sc - peak) * inverse
        return w.astype(BF16), (w * (dot(v, g, NT) - delta)).astype(BF16)

    def row_of(h, i):
        return [rows[h, n, pl.ds(i, 1), :] for n in range(3)]

    def store_entry(h, e, dk, dv):
        prev = prev_s[h * ENTRIES + e]
        back = jnp.maximum(prev, 0)
        acc[h, 0, e] = dk + jnp.where(prev < 0, 0.0, acc[h, 0, back])
        acc[h, 1, e] = dv + jnp.where(prev < 0, 0.0, acc[h, 1, back])

    def grad_units(h, units):
        for i in units:
            row = row_of(h, i)
            q, g = qrow[h][i], grow[h][i]
            o = dq = None
            for r in range(RAND + 1):
                if r < RAND:
                    j, bias = listed(h, RAND * i + r)
                else:
                    j, bias = wide_at, wide_bias
                k, v = kall[h][j], vall[h][j]
                wb, ds = weigh(k, v, q, g, row, bias)
                dk, dv = dot(ds, q, NN), dot(wb, g, NN)
                if r < RAND:
                    store_entry(h, RAND * i + r, dk, dv)
                elif i == 0:
                    wide_acc[h, 0] = dk
                    wide_acc[h, 1] = dv
                else:
                    wide_acc[h, 0] += dk
                    wide_acc[h, 1] += dv
                o1, q1 = dot(wb, v, TN), dot(ds, k, TN)
                o = o1 if o is None else o + o1
                dq = q1 if dq is None else dq + q1
            o_acc[h, i] = o
            dq_acc[h, i] = dq

    def grad_rim(h):
        for e, qi, kj in ((LEFT, left_q, left_k), (RIGHT, right_q, right_k)):
            k, v, q, g = kall[h][kj], vall[h][kj], qrow[h][qi], grow[h][qi]
            wb, ds = weigh(k, v, q, g, row_of(h, qi), None)
            store_entry(h, e, dot(ds, q, NN), dot(wb, g, NN))
            o_acc[h, qi] += dot(wb, v, TN)
            dq_acc[h, qi] += dot(ds, k, TN)
        store_entry(h, WIDE, wide_acc[h, 0], wide_acc[h, 1])

    def grad_own(h):
        k, v, q, g = window(h)
        row = [jnp.concatenate([a, b], axis=1) for a, b in zip(row_of(h, 2 * x), row_of(h, 2 * x + 1))]
        wb, ds = weigh(k, v, q, g, row, None)
        own_acc[h, 0] = dot(ds, q, NN).reshape(2, BLK, HD)
        own_acc[h, 1] = dot(wb, g, NN).reshape(2, BLK, HD)
        here = pl.ds(2 * x, 2)
        o_acc[h, here] += dot(wb, v, TN).reshape(2, BLK, HD)
        dq_acc[h, here] += dot(ds, k, TN).reshape(2, BLK, HD)

    def key_part(h, t, target):
        def one(b):
            last = last_s[h * COL + 2 * target + b]
            value = acc[h, t, jnp.maximum(last, 0)]
            value = jnp.where(last < 0, 0.0, value)
            return value * SCALE if t == 0 else value
        return one

    def query_part(h, t, target):
        def one(b):
            value = (o_acc, dq_acc)[t][h, 2 * target + b]
            return value * SCALE if t == 1 else value
        return one

    def summing(part, arrive, summed, send, recv, devs, pos, count):
        steps = count // 2

        def wait(h, direction, step, t):
            ref = arrive.at[h, direction, step, t]
            remote(ref, ref, send.at[h, direction, step, t], recv.at[h, direction, step, t],
                   devs[direction]).wait_recv()
            return ref

        def go(h, direction, step, t):
            away = steps - step
            target = (pos + away) % count if direction == 0 else (pos + count - away) % count
            mine = part(h, t, target)
            src = summed.at[h, direction, step, t]
            got = None if step == (0 if t == direction else 1) else wait(h, direction, step - 1, t)
            for b in range(2):
                value = mine(b)
                if got is not None:
                    value = value + got[b].astype(F32)
                src[b] = value.astype(BF16)
            go_on(remote(src, arrive.at[h, direction, step, t], send.at[h, direction, step, t],
                         recv.at[h, direction, step, t], devs[direction]))

        def begin(h):
            for direction in range(2):
                go(h, direction, 0, direction)
            for direction in range(2):
                go(h, direction, 1, 1 - direction)

        def step_on(h, step):
            for t in (1, 0):
                for direction in range(2):
                    if not (step == 1 and t != direction):
                        go(h, direction, step, t)

        return begin, step_on, lambda h, t: (wait(h, 0, steps - 1, t), wait(h, 1, steps - 1, t))

    zbegin, zsum_on, zfinal = summing(key_part, zin, zsum, rz_send, rz_recv, zdev, z, NZ)
    xbegin, xsum_on, xfinal = summing(query_part, xin, xsum, rx_send, rx_recv, xdev, x, NX)
    outs = (o_out, dq_out, dk_out, dv_out)

    def finish(h, n, got, mine, extra):
        def value(b):
            v = mine(b) + got[0][b].astype(F32) + got[1][b].astype(F32)
            return (v if extra is None else v + extra(b)).astype(BF16)
        lanes = lanes_of(2 * c + h)
        final[h, n] = value(1 - c)
        go_on(remote(final.at[h, n], outs[n].at[:, lanes], f_send.at[h, n], f_recv.at[h, n], partner))
        outs[n][:, lanes] = value(c)

    def finish_queries(h):
        for t in range(2):
            finish(h, t, xfinal(h, t), query_part(h, t, x), None)

    def finish_keys(h):
        for t in range(2):
            finish(h, 2 + t, zfinal(h, t), key_part(h, t, z),
                   lambda b, t=t: own_acc[h, t, b] * SCALE if t == 0 else own_acc[h, t, b])

    for h in range(2):
        exchange(h, 0)
        exchange(h, 1)
        exchange_grad(h)
        exchange(h, 2)
    plan(0)
    zstart(0)
    xstart(0)
    plan(1)
    zstep(0, 0)
    xstep(0)
    zstep(0, 1)
    zstep(0, 2)
    zstart(1)
    xstart(1)
    xend(0)
    zend(0)
    pairs = [(i, i + 1) for i in range(0, ROW, 2)]
    for units in pairs:
        count_units(0, units)
    count_rest(0)
    send_stats(0)
    zstep(1, 0)
    xstep(1)
    take_stats(0)
    grad_units(0, pairs[0])
    zstep(1, 1)
    grad_units(0, pairs[1])
    xend(1)
    grad_units(0, pairs[2])
    zstep(1, 2)
    grad_units(0, pairs[3])
    grad_rim(0)
    zbegin(0)
    xbegin(0)
    zend(1)
    for units in pairs:
        count_units(1, units)
    count_rest(1)
    send_stats(1)
    zsum_on(0, 1)
    xsum_on(0, 1)
    grad_own(0)
    zsum_on(0, 2)
    take_stats(1)
    grad_units(1, pairs[0])
    finish_queries(0)
    grad_units(1, pairs[1])
    zsum_on(0, 3)
    grad_units(1, pairs[2])
    grad_units(1, pairs[3])
    grad_rim(1)
    zbegin(1)
    xbegin(1)
    grad_own(1)
    finish_keys(0)
    zsum_on(1, 1)
    xsum_on(1, 1)
    zsum_on(1, 2)
    finish_queries(1)
    zsum_on(1, 3)
    finish_keys(1)
    for h in range(2):
        for n in range(4):
            dst = outs[n].at[:, lanes_of(2 * (1 - c) + h)]
            remote(final.at[h, n], dst, f_send.at[h, n], f_recv.at[h, n], partner).wait_recv()
    for cp in sends:
        cp.wait_send()


def place_kernel(*refs):
    for n in range(4):
        refs[4 + n][...] = refs[n][...]


def vmem():
    return pl.BlockSpec(memory_space=pltpu.VMEM)


def smem():
    return pl.BlockSpec(memory_space=pltpu.SMEM)


def on_device(query_rows, key_rows, value_rows, out_grad, random_blocks):
    dma = pltpu.SemaphoreType.DMA
    mem = pltpu.VMEM
    tile = (BLK, HD)
    full = jax.ShapeDtypeStruct((BLK, 4 * HD), BF16)
    zs, xs = NZ // 2, NX // 2
    outs = pl.pallas_call(
        attention_kernel,
        out_shape=(full,) * 4,
        in_specs=[smem()] + [vmem()] * 4,
        out_specs=[vmem()] * 4,
        scratch_shapes=[
            *[mem((COL,) + tile, BF16)] * 4, *[mem((ROW,) + tile, BF16)] * 4,
            mem((2, 4, 3, ROW, HD), F32), mem((2, NX, 3, ROW, HD), F32), mem((2, 3, ROW, HD), F32),
            mem((2, 2, ENTRIES) + tile, F32), mem((2, 2) + tile, F32), mem((2, 2, 2) + tile, F32),
            mem((2, ROW) + tile, F32), mem((2, ROW) + tile, F32),
            mem((2, 2, zs, 2, 2) + tile, BF16), mem((2, 2, zs, 2, 2) + tile, BF16),
            mem((2, 2, xs, 2, 2) + tile, BF16), mem((2, 2, xs, 2, 2) + tile, BF16),
            mem((2, 4) + tile, BF16),
            pltpu.SMEM((2 * ENTRIES,), jnp.int32), pltpu.SMEM((2 * ENTRIES,), jnp.int32), pltpu.SMEM((2 * COL,), jnp.int32),
            dma((2, 3, 2 * NY)), dma((2, 3, 2 * NY)), dma((2, 3)), dma((2,)), dma((2,)), dma((2,)),
            dma((2, 2, zs, 2)), dma((2, 2, zs, 2)), dma((2, 2, xs, 2)), dma((2, 2, xs, 2)),
            dma((2, NX)), dma((2, NX)),
            dma((2, 2, zs, 2)), dma((2, 2, zs, 2)), dma((2, 2, xs, 2)), dma((2, 2, xs, 2)),
            dma((2, 4)), dma((2, 4)),
        ],
        compiler_params=pltpu.CompilerParams(collective_id=0, has_side_effects=True),
        name="attention",
    )(random_blocks.transpose(2, 0, 1), query_rows, key_rows, value_rows, out_grad)
    return pl.pallas_call(
        place_kernel,
        out_shape=(full,) * 4,
        in_specs=[vmem()] * 4,
        out_specs=[vmem()] * 4,
        name="place",
    )(*outs)


def solution(mesh):
    in_specs = (
        P(("seq", "head"), None),
        P(("seq", "head"), None),
        P(("seq", "head"), None),
        P("seq", "head"),
        P("head", None, None),
    )
    out_specs = (P("seq", "head"),) * 4
    return jax.shard_map(
        on_device, mesh=mesh, in_specs=in_specs, out_specs=out_specs, check_vma=False
    )
```

```python
import math

import jax
import jax.numpy as jnp
from jax import lax
from jax.experimental import pallas as pl
from jax.experimental.pallas import tpu as pltpu
from jax.sharding import PartitionSpec as P

HD = 128
BLK = 128
NX = 4
NZ = 8
NY = 4
COL = 2 * NZ
ROW = 2 * NX
RAND = 3
LEFT = RAND * ROW
RIGHT = LEFT + 1
WIDE = LEFT + 2
ENTRIES = LEFT + 3
SCALE = 1.0 / math.sqrt(HD)
NEG = -1e30
MESH = pl.DeviceIdType.MESH
NT = (((1,), (1,)), ((), ()))
NN = (((1,), (0,)), ((), ()))
TN = (((0,), (0,)), ((), ()))
F32 = jnp.float32
BF16 = jnp.bfloat16


def dot(a, b, dims):
    return lax.dot_general(a, b, dims, preferred_element_type=F32)


def place_of(x, z, c):
    return (x * NZ + z) * 2 + c


def remote(src, dst, send_sem, recv_sem, dev):
    return pltpu.make_async_remote_copy(
        src_ref=src, dst_ref=dst, send_sem=send_sem, recv_sem=recv_sem,
        device_id=dev, device_id_type=MESH,
    )


def meet(devs):
    barrier = pltpu.get_barrier_semaphore()
    for dev in devs:
        pl.semaphore_signal(barrier, inc=1, device_id=dev, device_id_type=MESH)
    pl.semaphore_wait(barrier, len(devs))


def attention_kernel(rb_ref, q_ref, k_ref, v_ref, g_ref, o_out, dq_out, dk_out, dv_out,
                     kall0, kall1, vall0, vall1, qrow0, qrow1, grow0, grow1, sets, stats, rows, acc, wide_acc, own_acc, o_acc, dq_acc,
                     zin, zsum, xin, xsum, final, owner_s, prev_s, last_s,
                     a_send, a_recv, a_own, g_send, g_recv, g_own, z_send, z_recv, x_send, x_recv, s_send, s_recv,
                     rz_send, rz_recv, rx_send, rx_recv, f_send, f_recv):
    s = lax.axis_index("seq")
    y = lax.axis_index("head")
    x = s // (2 * NZ)
    z = (s // 2) % NZ
    c = s % 2
    me = y * 2 + c
    kall, vall, qrow, grow = (kall0, kall1), (vall0, vall1), (qrow0, qrow1), (grow0, grow1)

    def member(d):
        other = (me + d) % (2 * NY)
        return other % 2, other // 2

    def at(xx, zz):
        return (place_of(xx, zz, c), y)

    group = []
    for d in range(1, 2 * NY):
        cc, yy = member(d)
        group.append((place_of(x, z, cc), yy))
    zdev = (at(x, (z + 1) % NZ), at(x, (z + NZ - 1) % NZ))
    xall = [at((x + d) % NX, z) for d in range(1, NX)]
    xdev = (xall[0], xall[NX - 2])
    partner = (place_of(x, z, 1 - c), y)
    meet(group + list(zdev) + xall)

    sends = []

    def go_on(cp):
        cp.start()
        sends.append(cp)

    def lanes_of(n):
        return pl.ds(pl.multiple_of(n * HD, HD), HD)

    ins = (k_ref, v_ref, q_ref)
    bufs = (kall, vall, qrow)
    slot = (2 * z, 2 * z, 2 * x)
    own = {}

    def exchange(h, t):
        dst = bufs[t][h].at[slot[t] + c, pl.ds(pl.multiple_of(y * 32, 32), 32), :]
        for d in range(1, 2 * NY):
            cc, yy = member(d)
            go_on(remote(ins[t].at[:, lanes_of(yy * 4 + cc * 2 + h)], dst, a_send.at[h, t, d], a_recv.at[h, t, d],
                         group[d - 1]))
        own[h, t] = pltpu.make_async_copy(ins[t].at[:, lanes_of(me * 2 + h)], dst, a_own.at[h, t])
        own[h, t].start()

    def exchange_grad(h):
        go_on(remote(g_ref.at[:, lanes_of(2 * (1 - c) + h)], grow[h].at[2 * x + c], g_send.at[h], g_recv.at[h], partner))
        own[h, 3] = pltpu.make_async_copy(g_ref.at[:, lanes_of(2 * c + h)], grow[h].at[2 * x + c], g_own.at[h])
        own[h, 3].start()

    def arrived(h, t):
        own[h, t].wait()
        for d in range(1, 2 * NY):
            other = (me + 2 * NY - d) % (2 * NY)
            cs, ys = other % 2, other // 2
            dst = bufs[t][h].at[slot[t] + cs, pl.ds(pl.multiple_of(ys * 32, 32), 32), :]
            remote(dst, dst, a_send.at[h, t, d], a_recv.at[h, t, d], partner).wait_recv()

    def arrived_grad(h):
        own[h, 3].wait()
        dst = grow[h].at[2 * x + 1 - c]
        remote(dst, dst, g_send.at[h], g_recv.at[h], partner).wait_recv()

    def ring(bufs2, send, recv, devs, pos, count):
        def piece(h, t, owner):
            return bufs2[t][h].at[pl.ds(2 * owner, 2)]

        def copy(h, direction, step, t):
            owner = (pos + count - step) % count if direction == 0 else (pos + step) % count
            ref = piece(h, t, owner)
            go_on(remote(ref, ref, send.at[h, direction, step, t], recv.at[h, direction, step, t], devs[direction]))

        def wait(h, direction, step, t):
            owner = (pos + count - 1 - step) % count if direction == 0 else (pos + 1 + step) % count
            ref = piece(h, t, owner)
            remote(ref, ref, send.at[h, direction, step, t], recv.at[h, direction, step, t],
                   devs[direction]).wait_recv()

        return copy, wait

    zcopy, zwait = ring((kall, vall), z_send, z_recv, zdev, z, NZ)
    xcopy, xwait = ring((qrow, grow), x_send, x_recv, xdev, x, NX)
    zlast = NZ // 2 - 1

    def zstart(h, t):
        arrived(h, t)
        for direction in range(2):
            zcopy(h, direction, 0, t)

    def xstart(h):
        arrived_grad(h)
        for direction in range(2):
            xcopy(h, direction, 0, 1)
        arrived(h, 2)
        for direction in range(2):
            xcopy(h, direction, 0, 0)

    def zstep(h, step, tensors=(0, 1)):
        for t in tensors:
            for direction in range(2):
                zwait(h, direction, step, t)
                if step + 1 < zlast or direction == t:
                    zcopy(h, direction, step + 1, t)

    def xstep(h):
        for t in (1, 0):
            for direction in range(2):
                xwait(h, direction, 0, t)
                if direction == t:
                    xcopy(h, direction, 1, t)

    def zend(h):
        for t in range(2):
            zwait(h, t, zlast, t)

    def xend(h):
        for t in range(2):
            xwait(h, t, 1, t)

    edge = (x == 0) | (x == NX - 1)
    wide_at = jnp.where(x == 0, 0, COL - 1)
    left_q = 2 * ((x + jnp.where(z == 0, 1, 0)) % NX)
    right_q = 2 * ((x + jnp.where(z == NZ - 1, NX - 1, 0)) % NX) + 1
    left_k = (2 * z + COL - 1) % COL
    right_k = (2 * z + 2) % COL

    def plan(h):
        owners = []
        for i in range(ROW):
            for r in range(RAND):
                j = rb_ref[r, 2 * c + h, COL * (i // 2) + 2 * z + i % 2] - COL * x
                owners.append(jnp.where((j >= 0) & (j < COL), j, -1))
        owners += [left_k, right_k, jnp.where(edge, wide_at, -1)]
        for e in range(ENTRIES):
            prev = jnp.int32(-1)
            for f in range(e):
                prev = jnp.where(owners[f] == owners[e], f, prev)
            owner_s[h * ENTRIES + e] = owners[e]
            prev_s[h * ENTRIES + e] = prev
        for j in range(COL):
            last = jnp.int32(-1)
            for e in range(ENTRIES):
                last = jnp.where(owners[e] == j, e, last)
            last_s[h * COL + j] = last

    def listed(h, e):
        j = owner_s[h * ENTRIES + e]
        return jnp.maximum(j, 0), jnp.where(j < 0, NEG, 0.0)

    wide_bias = jnp.where(edge, 0.0, NEG)

    def stack(tiles):
        return tiles[0] if len(tiles) == 1 else jnp.concatenate(tiles, axis=0)

    def pieces(value, count):
        size = value.shape[0] // count
        return [value[n * size:(n + 1) * size] for n in range(count)]

    def score(ks, q):
        scores = pieces(dot(stack([k for k, _ in ks]), q, NT), len(ks))
        return [sc * SCALE if bias is None else sc * SCALE + bias for sc, (_, bias) in zip(scores, ks)]

    def measure(ks, vs, q, g):
        scores = score(ks, q)
        peak = scores[0]
        for sc in scores[1:]:
            peak = jnp.maximum(peak, sc)
        peak = jnp.max(peak, axis=0, keepdims=True)
        total = weighted = None
        for sc, dp in zip(scores, pieces(dot(stack(vs), g, NT), len(vs))):
            e = jnp.exp(sc - peak)
            w = e * dp
            total = e if total is None else total + e
            weighted = w if weighted is None else weighted + w
        return peak, jnp.sum(total, axis=0, keepdims=True), jnp.sum(weighted, axis=0, keepdims=True)

    def window(h):
        mine = pl.ds(2 * z, 2)
        here = pl.ds(2 * x, 2)
        return tuple(ref[h][at_, :, :].reshape(2 * BLK, HD)
                     for ref, at_ in ((kall, mine), (vall, mine), (qrow, here), (grow, here)))

    def tiles_of(h, i):
        ks, vs = [], []
        for r in range(RAND):
            j, bias = listed(h, RAND * i + r)
            ks.append((kall[h][j], bias))
            vs.append(vall[h][j])
        ks.append((kall[h][wide_at], wide_bias))
        vs.append(vall[h][wide_at])
        return ks, vs

    def count_units(h, units):
        for i in units:
            ks, vs = tiles_of(h, i)
            for n, row in enumerate(measure(ks, vs, qrow[h][i], grow[h][i])):
                sets[h, 0, n, i:i + 1, :] = row

    def count_rest(h):
        for part in range(1, 4):
            sets[h, part, 0] = jnp.full((ROW, HD), NEG, F32)
            sets[h, part, 1] = jnp.zeros((ROW, HD), F32)
            sets[h, part, 2] = jnp.zeros((ROW, HD), F32)
        k, v, q, g = window(h)
        for n, row in enumerate(measure([(k, None)], [v], q, g)):
            sets[h, 1, n, pl.ds(2 * x, 1), :] = row[:, :HD]
            sets[h, 1, n, pl.ds(2 * x + 1, 1), :] = row[:, HD:]
        for part, qi, kj in ((2, left_q, left_k), (3, right_q, right_k)):
            for n, row in enumerate(measure([(kall[h][kj], None)], [vall[h][kj]], qrow[h][qi], grow[h][qi])):
                sets[h, part, n, pl.ds(qi, 1), :] = row

    def merge(parts):
        peak = jnp.maximum(jnp.maximum(parts[0][0], parts[1][0]), jnp.maximum(parts[2][0], parts[3][0]))
        shift = [jnp.exp(p[0] - peak) for p in parts]
        total = sum(p[1] * f for p, f in zip(parts, shift))
        return peak, total, sum(p[2] * f for p, f in zip(parts, shift))

    def send_stats(h):
        for n, value in enumerate(merge([[sets[h, part, n] for n in range(3)] for part in range(4)])):
            stats[h, x, n] = value
        for d in range(1, NX):
            go_on(remote(stats.at[h, x], stats.at[h, x], s_send.at[h, d], s_recv.at[h, d], xall[d - 1]))

    def take_stats(h):
        for d in range(1, NX):
            src = (x + NX - d) % NX
            remote(stats.at[h, src], stats.at[h, src], s_send.at[h, d], s_recv.at[h, d], xall[d - 1]).wait_recv()
        peak, total, weighted = merge([[stats[h, i, n] for n in range(3)] for i in range(NX)])
        inverse = 1.0 / total
        rows[h, 0] = peak
        rows[h, 1] = inverse
        rows[h, 2] = weighted * inverse

    def weigh(ks, vs, q, g, row):
        peak, inverse, delta = row
        wb, ds = [], []
        for sc, dp in zip(score(ks, q), pieces(dot(stack(vs), g, NT), len(vs))):
            w = jnp.exp(sc - peak) * inverse
            wb.append(w.astype(BF16))
            ds.append((w * (dp - delta)).astype(BF16))
        wb, ds = stack(wb), stack(ds)
        k, v = stack([k for k, _ in ks]), stack(vs)
        return dot(ds, q, NN), dot(wb, g, NN), dot(wb, v, TN), dot(ds, k, TN)

    def row_of(h, i):
        return [rows[h, n, pl.ds(i, 1), :] for n in range(3)]

    def store_entry(h, e, dk, dv):
        prev = prev_s[h * ENTRIES + e]
        back = jnp.maximum(prev, 0)
        acc[h, 0, e] = dk + jnp.where(prev < 0, 0.0, acc[h, 0, back])
        acc[h, 1, e] = dv + jnp.where(prev < 0, 0.0, acc[h, 1, back])

    def grad_units(h, units):
        for i in units:
            ks, vs = tiles_of(h, i)
            dks, dvs, o, dq = weigh(ks, vs, qrow[h][i], grow[h][i], row_of(h, i))
            for r, (dk, dv) in enumerate(zip(pieces(dks, len(ks)), pieces(dvs, len(vs)))):
                if r < RAND:
                    store_entry(h, RAND * i + r, dk, dv)
                elif i == 0:
                    wide_acc[h, 0] = dk
                    wide_acc[h, 1] = dv
                else:
                    wide_acc[h, 0] += dk
                    wide_acc[h, 1] += dv
            o_acc[h, i] = o
            dq_acc[h, i] = dq

    def grad_rim(h):
        for e, qi, kj in ((LEFT, left_q, left_k), (RIGHT, right_q, right_k)):
            dk, dv, o, dq = weigh([(kall[h][kj], None)], [vall[h][kj]], qrow[h][qi], grow[h][qi], row_of(h, qi))
            store_entry(h, e, dk, dv)
            o_acc[h, qi] += o
            dq_acc[h, qi] += dq
        store_entry(h, WIDE, wide_acc[h, 0], wide_acc[h, 1])

    def grad_own(h):
        k, v, q, g = window(h)
        row = [jnp.concatenate([a, b], axis=1) for a, b in zip(row_of(h, 2 * x), row_of(h, 2 * x + 1))]
        dk, dv, o, dq = weigh([(k, None)], [v], q, g, row)
        own_acc[h, 0] = dk.reshape(2, BLK, HD)
        own_acc[h, 1] = dv.reshape(2, BLK, HD)
        here = pl.ds(2 * x, 2)
        o_acc[h, here] += o.reshape(2, BLK, HD)
        dq_acc[h, here] += dq.reshape(2, BLK, HD)

    def key_part(h, t, target):
        def one(b):
            last = last_s[h * COL + 2 * target + b]
            value = acc[h, t, jnp.maximum(last, 0)]
            value = jnp.where(last < 0, 0.0, value)
            return value * SCALE if t == 0 else value
        return one

    def query_part(h, t, target):
        def one(b):
            value = (o_acc, dq_acc)[t][h, 2 * target + b]
            return value * SCALE if t == 1 else value
        return one

    def summing(part, arrive, summed, send, recv, devs, pos, count):
        steps = count // 2

        def wait(h, direction, step, t):
            ref = arrive.at[h, direction, step, t]
            remote(ref, ref, send.at[h, direction, step, t], recv.at[h, direction, step, t],
                   devs[direction]).wait_recv()
            return ref

        def go(h, direction, step, t):
            away = steps - step
            target = (pos + away) % count if direction == 0 else (pos + count - away) % count
            mine = part(h, t, target)
            src = summed.at[h, direction, step, t]
            got = None if step == (0 if t == direction else 1) else wait(h, direction, step - 1, t)
            for b in range(2):
                value = mine(b)
                if got is not None:
                    value = value + got[b].astype(F32)
                src[b] = value.astype(BF16)
            go_on(remote(src, arrive.at[h, direction, step, t], send.at[h, direction, step, t],
                         recv.at[h, direction, step, t], devs[direction]))

        def begin(h):
            for direction in range(2):
                go(h, direction, 0, direction)
            for direction in range(2):
                go(h, direction, 1, 1 - direction)

        def step_on(h, step):
            for t in (1, 0):
                for direction in range(2):
                    if not (step == 1 and t != direction):
                        go(h, direction, step, t)

        return begin, step_on, lambda h, t: (wait(h, 0, steps - 1, t), wait(h, 1, steps - 1, t))

    zbegin, zsum_on, zfinal = summing(key_part, zin, zsum, rz_send, rz_recv, zdev, z, NZ)
    xbegin, xsum_on, xfinal = summing(query_part, xin, xsum, rx_send, rx_recv, xdev, x, NX)
    outs = (o_out, dq_out, dk_out, dv_out)

    def finish(h, n, got, mine, extra):
        def value(b):
            v = mine(b) + got[0][b].astype(F32) + got[1][b].astype(F32)
            return (v if extra is None else v + extra(b)).astype(BF16)
        lanes = lanes_of(2 * c + h)
        final[h, n] = value(1 - c)
        go_on(remote(final.at[h, n], outs[n].at[:, lanes], f_send.at[h, n], f_recv.at[h, n], partner))
        outs[n][:, lanes] = value(c)

    def finish_queries(h):
        for t in range(2):
            finish(h, t, xfinal(h, t), query_part(h, t, x), None)

    def finish_keys(h):
        for t in range(2):
            finish(h, 2 + t, zfinal(h, t), key_part(h, t, z),
                   lambda b, t=t: own_acc[h, t, b] * SCALE if t == 0 else own_acc[h, t, b])

    exchange(0, 0)
    exchange(0, 1)
    exchange(1, 0)
    exchange(1, 1)
    for h in range(2):
        exchange_grad(h)
        exchange(h, 2)
    zstart(0, 0)
    zstart(0, 1)
    zstart(1, 0)
    zstep(0, 0)
    zstart(1, 1)
    xstart(0)
    plan(0)
    zstep(0, 1)
    zstep(1, 0, (0,))
    xstart(1)
    xstep(0)
    zstep(0, 2)
    zstep(1, 0, (1,))
    plan(1)
    xend(0)
    zend(0)
    pairs = [(i, i + 1) for i in range(0, ROW, 2)]
    count_units(0, pairs[0])
    count_units(0, pairs[1])
    zstep(1, 1)
    count_units(0, pairs[2])
    count_units(0, pairs[3])
    count_rest(0)
    send_stats(0)
    xstep(1)
    zstep(1, 2)
    take_stats(0)
    grad_units(0, pairs[0])
    grad_units(0, pairs[1])
    xend(1)
    grad_units(0, pairs[2])
    grad_units(0, pairs[3])
    grad_rim(0)
    zbegin(0)
    xbegin(0)
    zend(1)
    for units in pairs:
        count_units(1, units)
    count_rest(1)
    send_stats(1)
    zsum_on(0, 1)
    xsum_on(0, 1)
    grad_own(0)
    zsum_on(0, 2)
    take_stats(1)
    grad_units(1, pairs[0])
    finish_queries(0)
    grad_units(1, pairs[1])
    zsum_on(0, 3)
    grad_units(1, pairs[2])
    grad_units(1, pairs[3])
    grad_rim(1)
    zbegin(1)
    xbegin(1)
    grad_own(1)
    finish_keys(0)
    zsum_on(1, 1)
    xsum_on(1, 1)
    zsum_on(1, 2)
    finish_queries(1)
    zsum_on(1, 3)
    finish_keys(1)
    for h in range(2):
        for n in range(4):
            dst = outs[n].at[:, lanes_of(2 * (1 - c) + h)]
            remote(final.at[h, n], dst, f_send.at[h, n], f_recv.at[h, n], partner).wait_recv()
    for cp in sends:
        cp.wait_send()


def place_kernel(*refs):
    for n in range(4):
        refs[4 + n][...] = refs[n][...]


def vmem():
    return pl.BlockSpec(memory_space=pltpu.VMEM)


def smem():
    return pl.BlockSpec(memory_space=pltpu.SMEM)


def on_device(query_rows, key_rows, value_rows, out_grad, random_blocks):
    dma = pltpu.SemaphoreType.DMA
    mem = pltpu.VMEM
    tile = (BLK, HD)
    full = jax.ShapeDtypeStruct((BLK, 4 * HD), BF16)
    zs, xs = NZ // 2, NX // 2
    outs = pl.pallas_call(
        attention_kernel,
        out_shape=(full,) * 4,
        in_specs=[smem()] + [vmem()] * 4,
        out_specs=[vmem()] * 4,
        scratch_shapes=[
            *[mem((COL,) + tile, BF16)] * 4, *[mem((ROW,) + tile, BF16)] * 4,
            mem((2, 4, 3, ROW, HD), F32), mem((2, NX, 3, ROW, HD), F32), mem((2, 3, ROW, HD), F32),
            mem((2, 2, ENTRIES) + tile, F32), mem((2, 2) + tile, F32), mem((2, 2, 2) + tile, F32),
            mem((2, ROW) + tile, F32), mem((2, ROW) + tile, F32),
            mem((2, 2, zs, 2, 2) + tile, BF16), mem((2, 2, zs, 2, 2) + tile, BF16),
            mem((2, 2, xs, 2, 2) + tile, BF16), mem((2, 2, xs, 2, 2) + tile, BF16),
            mem((2, 4) + tile, BF16),
            pltpu.SMEM((2 * ENTRIES,), jnp.int32), pltpu.SMEM((2 * ENTRIES,), jnp.int32), pltpu.SMEM((2 * COL,), jnp.int32),
            dma((2, 3, 2 * NY)), dma((2, 3, 2 * NY)), dma((2, 3)), dma((2,)), dma((2,)), dma((2,)),
            dma((2, 2, zs, 2)), dma((2, 2, zs, 2)), dma((2, 2, xs, 2)), dma((2, 2, xs, 2)),
            dma((2, NX)), dma((2, NX)),
            dma((2, 2, zs, 2)), dma((2, 2, zs, 2)), dma((2, 2, xs, 2)), dma((2, 2, xs, 2)),
            dma((2, 4)), dma((2, 4)),
        ],
        compiler_params=pltpu.CompilerParams(collective_id=0, has_side_effects=True),
        name="attention",
    )(random_blocks.transpose(2, 0, 1), query_rows, key_rows, value_rows, out_grad)
    return pl.pallas_call(
        place_kernel,
        out_shape=(full,) * 4,
        in_specs=[vmem()] * 4,
        out_specs=[vmem()] * 4,
        name="place",
    )(*outs)


def solution(mesh):
    in_specs = (
        P(("seq", "head"), None),
        P(("seq", "head"), None),
        P(("seq", "head"), None),
        P("seq", "head"),
        P("head", None, None),
    )
    out_specs = (P("seq", "head"),) * 4
    return jax.shard_map(
        on_device, mesh=mesh, in_specs=in_specs, out_specs=out_specs, check_vma=False
    )
```

```python
import math

import jax
import jax.numpy as jnp
from jax import lax
from jax.experimental import pallas as pl
from jax.experimental.pallas import tpu as pltpu
from jax.sharding import PartitionSpec as P

HD = 128
BLK = 128
NX = 4
NZ = 8
NY = 4
COL = 2 * NZ
ROW = 2 * NX
RAND = 3
LEFT = RAND * ROW
RIGHT = LEFT + 1
WIDE = LEFT + 2
ENTRIES = LEFT + 3
SCALE = 1.0 / math.sqrt(HD)
NEG = -1e30
MESH = pl.DeviceIdType.MESH
NT = (((1,), (1,)), ((), ()))
NN = (((1,), (0,)), ((), ()))
TN = (((0,), (0,)), ((), ()))
F32 = jnp.float32
BF16 = jnp.bfloat16


def dot(a, b, dims):
    return lax.dot_general(a, b, dims, preferred_element_type=F32)


def place_of(x, z, c):
    return (x * NZ + z) * 2 + c


def remote(src, dst, send_sem, recv_sem, dev):
    return pltpu.make_async_remote_copy(
        src_ref=src, dst_ref=dst, send_sem=send_sem, recv_sem=recv_sem,
        device_id=dev, device_id_type=MESH,
    )


def meet(devs):
    barrier = pltpu.get_barrier_semaphore()
    for dev in devs:
        pl.semaphore_signal(barrier, inc=1, device_id=dev, device_id_type=MESH)
    pl.semaphore_wait(barrier, len(devs))


def attention_kernel(rb_ref, q_ref, k_ref, v_ref, g_ref, o_out, dq_out, dk_out, dv_out,
                     kall0, kall1, vall0, vall1, qrow0, qrow1, grow0, grow1, sets, stats, rows, acc, wide_acc, own_acc, o_acc, dq_acc,
                     zin, zsum, xin, xsum, zfin, xfin, final, gift, owner_s, prev_s, last_s,
                     a_send, a_recv, a_own, g_send, g_recv, g_own, z_send, z_recv, x_send, x_recv, s_send, s_recv,
                     rz_send, rz_recv, rx_send, rx_recv, lz_send, lz_recv, lx_send, lx_recv, f_send, f_recv):
    s = lax.axis_index("seq")
    y = lax.axis_index("head")
    x = s // (2 * NZ)
    z = (s // 2) % NZ
    c = s % 2
    me = y * 2 + c
    kall, vall, qrow, grow = (kall0, kall1), (vall0, vall1), (qrow0, qrow1), (grow0, grow1)

    def member(d):
        other = (me + d) % (2 * NY)
        return other % 2, other // 2

    def at(xx, zz):
        return (place_of(xx, zz, c), y)

    group = []
    for d in range(1, 2 * NY):
        cc, yy = member(d)
        group.append((place_of(x, z, cc), yy))
    zdev = (at(x, (z + 1) % NZ), at(x, (z + NZ - 1) % NZ))
    xall = [at((x + d) % NX, z) for d in range(1, NX)]
    xdev = (xall[0], xall[NX - 2])
    partner = (place_of(x, z, 1 - c), y)

    def either(xx, zz):
        return [(place_of(xx, zz, b), y) for b in range(2)]

    def across(xx, zz):
        return (place_of(xx, zz, 1 - c), y)

    zcores = (either(x, (z + 1) % NZ), either(x, (z + NZ - 1) % NZ))
    xcores = (either((x + 1) % NX, z), either((x + NX - 1) % NX, z))
    meet(group + list(zdev) + xall + [across(x, (z + 1) % NZ), across(x, (z + NZ - 1) % NZ),
                                      across((x + 1) % NX, z), across((x + NX - 1) % NX, z)])

    sends = []

    def go_on(cp):
        cp.start()
        sends.append(cp)

    def lanes_of(n):
        return pl.ds(pl.multiple_of(n * HD, HD), HD)

    ins = (k_ref, v_ref, q_ref)
    bufs = (kall, vall, qrow)
    slot = (2 * z, 2 * z, 2 * x)
    own = {}

    def exchange(h, t):
        dst = bufs[t][h].at[slot[t] + c, pl.ds(pl.multiple_of(y * 32, 32), 32), :]
        for d in range(1, 2 * NY):
            cc, yy = member(d)
            go_on(remote(ins[t].at[:, lanes_of(yy * 4 + cc * 2 + h)], dst, a_send.at[h, t, d], a_recv.at[h, t, d],
                         group[d - 1]))
        own[h, t] = pltpu.make_async_copy(ins[t].at[:, lanes_of(me * 2 + h)], dst, a_own.at[h, t])
        own[h, t].start()

    def exchange_grad(h):
        go_on(remote(g_ref.at[:, lanes_of(2 * (1 - c) + h)], grow[h].at[2 * x + c], g_send.at[h], g_recv.at[h], partner))
        own[h, 3] = pltpu.make_async_copy(g_ref.at[:, lanes_of(2 * c + h)], grow[h].at[2 * x + c], g_own.at[h])
        own[h, 3].start()

    def arrived(h, t):
        own[h, t].wait()
        for d in range(1, 2 * NY):
            other = (me + 2 * NY - d) % (2 * NY)
            cs, ys = other % 2, other // 2
            dst = bufs[t][h].at[slot[t] + cs, pl.ds(pl.multiple_of(ys * 32, 32), 32), :]
            remote(dst, dst, a_send.at[h, t, d], a_recv.at[h, t, d], partner).wait_recv()

    def arrived_grad(h):
        own[h, 3].wait()
        dst = grow[h].at[2 * x + 1 - c]
        remote(dst, dst, g_send.at[h], g_recv.at[h], partner).wait_recv()

    def ring(bufs2, send, recv, devs, pos, count):
        def piece(h, t, owner):
            return bufs2[t][h].at[pl.ds(2 * owner, 2)]

        def copy(h, direction, step, t):
            owner = (pos + count - step) % count if direction == 0 else (pos + step) % count
            ref = piece(h, t, owner)
            go_on(remote(ref, ref, send.at[h, direction, step, t], recv.at[h, direction, step, t], devs[direction]))

        def wait(h, direction, step, t):
            owner = (pos + count - 1 - step) % count if direction == 0 else (pos + 1 + step) % count
            ref = piece(h, t, owner)
            remote(ref, ref, send.at[h, direction, step, t], recv.at[h, direction, step, t],
                   devs[direction]).wait_recv()

        return copy, wait

    zcopy, zwait = ring((kall, vall), z_send, z_recv, zdev, z, NZ)
    xcopy, xwait = ring((qrow, grow), x_send, x_recv, xdev, x, NX)
    zlast = NZ // 2 - 1

    def zstart(h, t):
        arrived(h, t)
        for direction in range(2):
            zcopy(h, direction, 0, t)

    def xstart(h):
        arrived_grad(h)
        for direction in range(2):
            xcopy(h, direction, 0, 1)
        arrived(h, 2)
        for direction in range(2):
            xcopy(h, direction, 0, 0)

    def zstep(h, step, tensors=(0, 1)):
        for t in tensors:
            for direction in range(2):
                zwait(h, direction, step, t)
                if step + 1 < zlast or direction == t:
                    zcopy(h, direction, step + 1, t)

    def xstep(h):
        for t in (1, 0):
            for direction in range(2):
                xwait(h, direction, 0, t)
                if direction == t:
                    xcopy(h, direction, 1, t)

    def zend(h):
        for t in range(2):
            zwait(h, t, zlast, t)

    def xend(h):
        for t in range(2):
            xwait(h, t, 1, t)

    edge = (x == 0) | (x == NX - 1)
    wide_at = jnp.where(x == 0, 0, COL - 1)
    left_q = 2 * ((x + jnp.where(z == 0, 1, 0)) % NX)
    right_q = 2 * ((x + jnp.where(z == NZ - 1, NX - 1, 0)) % NX) + 1
    left_k = (2 * z + COL - 1) % COL
    right_k = (2 * z + 2) % COL

    def plan(h):
        owners = []
        for i in range(ROW):
            for r in range(RAND):
                j = rb_ref[r, 2 * c + h, COL * (i // 2) + 2 * z + i % 2] - COL * x
                owners.append(jnp.where((j >= 0) & (j < COL), j, -1))
        owners += [left_k, right_k, jnp.where(edge, wide_at, -1)]
        for e in range(ENTRIES):
            prev = jnp.int32(-1)
            for f in range(e):
                prev = jnp.where(owners[f] == owners[e], f, prev)
            owner_s[h * ENTRIES + e] = owners[e]
            prev_s[h * ENTRIES + e] = prev
        for j in range(COL):
            last = jnp.int32(-1)
            for e in range(ENTRIES):
                last = jnp.where(owners[e] == j, e, last)
            last_s[h * COL + j] = last

    def listed(h, e):
        j = owner_s[h * ENTRIES + e]
        return jnp.maximum(j, 0), jnp.where(j < 0, NEG, 0.0)

    wide_bias = jnp.where(edge, 0.0, NEG)

    def stack(tiles):
        return tiles[0] if len(tiles) == 1 else jnp.concatenate(tiles, axis=0)

    def pieces(value, count):
        size = value.shape[0] // count
        return [value[n * size:(n + 1) * size] for n in range(count)]

    def score(ks, q):
        scores = pieces(dot(stack([k for k, _ in ks]), q, NT), len(ks))
        return [sc * SCALE if bias is None else sc * SCALE + bias for sc, (_, bias) in zip(scores, ks)]

    def measure(ks, vs, q, g):
        scores = score(ks, q)
        peak = scores[0]
        for sc in scores[1:]:
            peak = jnp.maximum(peak, sc)
        peak = jnp.max(peak, axis=0, keepdims=True)
        total = weighted = None
        for sc, dp in zip(scores, pieces(dot(stack(vs), g, NT), len(vs))):
            e = jnp.exp(sc - peak)
            w = e * dp
            total = e if total is None else total + e
            weighted = w if weighted is None else weighted + w
        return peak, jnp.sum(total, axis=0, keepdims=True), jnp.sum(weighted, axis=0, keepdims=True)

    def window(h):
        mine = pl.ds(2 * z, 2)
        here = pl.ds(2 * x, 2)
        return tuple(ref[h][at_, :, :].reshape(2 * BLK, HD)
                     for ref, at_ in ((kall, mine), (vall, mine), (qrow, here), (grow, here)))

    def tiles_of(h, i):
        ks, vs = [], []
        for r in range(RAND):
            j, bias = listed(h, RAND * i + r)
            ks.append((kall[h][j], bias))
            vs.append(vall[h][j])
        ks.append((kall[h][wide_at], wide_bias))
        vs.append(vall[h][wide_at])
        return ks, vs

    def count_units(h, units):
        for i in units:
            ks, vs = tiles_of(h, i)
            for n, row in enumerate(measure(ks, vs, qrow[h][i], grow[h][i])):
                sets[h, 0, n, i:i + 1, :] = row

    def count_rest(h):
        for part in range(1, 4):
            sets[h, part, 0] = jnp.full((ROW, HD), NEG, F32)
            sets[h, part, 1] = jnp.zeros((ROW, HD), F32)
            sets[h, part, 2] = jnp.zeros((ROW, HD), F32)
        k, v, q, g = window(h)
        for n, row in enumerate(measure([(k, None)], [v], q, g)):
            sets[h, 1, n, pl.ds(2 * x, 1), :] = row[:, :HD]
            sets[h, 1, n, pl.ds(2 * x + 1, 1), :] = row[:, HD:]
        for part, qi, kj in ((2, left_q, left_k), (3, right_q, right_k)):
            for n, row in enumerate(measure([(kall[h][kj], None)], [vall[h][kj]], qrow[h][qi], grow[h][qi])):
                sets[h, part, n, pl.ds(qi, 1), :] = row

    def merge(parts):
        peak = jnp.maximum(jnp.maximum(parts[0][0], parts[1][0]), jnp.maximum(parts[2][0], parts[3][0]))
        shift = [jnp.exp(p[0] - peak) for p in parts]
        total = sum(p[1] * f for p, f in zip(parts, shift))
        return peak, total, sum(p[2] * f for p, f in zip(parts, shift))

    def send_stats(h):
        for n, value in enumerate(merge([[sets[h, part, n] for n in range(3)] for part in range(4)])):
            stats[h, x, n] = value
        for d in range(1, NX):
            go_on(remote(stats.at[h, x], stats.at[h, x], s_send.at[h, d], s_recv.at[h, d], xall[d - 1]))

    def take_stats(h):
        for d in range(1, NX):
            src = (x + NX - d) % NX
            remote(stats.at[h, src], stats.at[h, src], s_send.at[h, d], s_recv.at[h, d], xall[d - 1]).wait_recv()
        peak, total, weighted = merge([[stats[h, i, n] for n in range(3)] for i in range(NX)])
        inverse = 1.0 / total
        rows[h, 0] = peak
        rows[h, 1] = inverse
        rows[h, 2] = weighted * inverse

    def weigh(ks, vs, q, g, row):
        peak, inverse, delta = row
        wb, ds = [], []
        for sc, dp in zip(score(ks, q), pieces(dot(stack(vs), g, NT), len(vs))):
            w = jnp.exp(sc - peak) * inverse
            wb.append(w.astype(BF16))
            ds.append((w * (dp - delta)).astype(BF16))
        wb, ds = stack(wb), stack(ds)
        k, v = stack([k for k, _ in ks]), stack(vs)
        return dot(ds, q, NN), dot(wb, g, NN), dot(wb, v, TN), dot(ds, k, TN)

    def row_of(h, i):
        return [rows[h, n, pl.ds(i, 1), :] for n in range(3)]

    def store_entry(h, e, dk, dv):
        prev = prev_s[h * ENTRIES + e]
        back = jnp.maximum(prev, 0)
        acc[h, 0, e] = dk + jnp.where(prev < 0, 0.0, acc[h, 0, back])
        acc[h, 1, e] = dv + jnp.where(prev < 0, 0.0, acc[h, 1, back])

    def grad_units(h, units):
        for i in units:
            ks, vs = tiles_of(h, i)
            dks, dvs, o, dq = weigh(ks, vs, qrow[h][i], grow[h][i], row_of(h, i))
            for r, (dk, dv) in enumerate(zip(pieces(dks, len(ks)), pieces(dvs, len(vs)))):
                if r < RAND:
                    store_entry(h, RAND * i + r, dk, dv)
                elif i == 0:
                    wide_acc[h, 0] = dk
                    wide_acc[h, 1] = dv
                else:
                    wide_acc[h, 0] += dk
                    wide_acc[h, 1] += dv
            o_acc[h, i] = o
            dq_acc[h, i] = dq

    def grad_rim(h):
        for e, qi, kj in ((LEFT, left_q, left_k), (RIGHT, right_q, right_k)):
            dk, dv, o, dq = weigh([(kall[h][kj], None)], [vall[h][kj]], qrow[h][qi], grow[h][qi], row_of(h, qi))
            store_entry(h, e, dk, dv)
            o_acc[h, qi] += o
            dq_acc[h, qi] += dq
        store_entry(h, WIDE, wide_acc[h, 0], wide_acc[h, 1])

    def grad_own(h):
        k, v, q, g = window(h)
        row = [jnp.concatenate([a, b], axis=1) for a, b in zip(row_of(h, 2 * x), row_of(h, 2 * x + 1))]
        dk, dv, o, dq = weigh([(k, None)], [v], q, g, row)
        own_acc[h, 0] = dk.reshape(2, BLK, HD)
        own_acc[h, 1] = dv.reshape(2, BLK, HD)
        here = pl.ds(2 * x, 2)
        o_acc[h, here] += o.reshape(2, BLK, HD)
        dq_acc[h, here] += dq.reshape(2, BLK, HD)

    def key_part(h, t, target):
        def one(b):
            last = last_s[h * COL + 2 * target + b]
            value = acc[h, t, jnp.maximum(last, 0)]
            value = jnp.where(last < 0, 0.0, value)
            return value * SCALE if t == 0 else value
        return one

    def query_part(h, t, target):
        def one(b):
            value = (o_acc, dq_acc)[t][h, 2 * target + b]
            return value * SCALE if t == 1 else value
        return one

    def summing(part, arrive, summed, send, recv, devs, last, last_send, last_recv, cores, pos, count):
        steps = count // 2

        def wait(h, direction, step, t, b):
            ref = arrive.at[h, direction, step, t, b]
            remote(ref, ref, send.at[h, direction, step, t, b], recv.at[h, direction, step, t, b],
                   devs[direction]).wait_recv()
            return ref

        def go(h, direction, step, t):
            away = steps - step
            target = (pos + away) % count if direction == 0 else (pos + count - away) % count
            mine = part(h, t, target)
            for b in range(2):
                value = mine(b)
                if step != (0 if t == direction else 1):
                    value = value + wait(h, direction, step - 1, t, b)[...].astype(F32)
                src = summed.at[h, direction, step, t, b]
                src[...] = value.astype(BF16)
                if step == steps - 1:
                    go_on(remote(src, last.at[h, t, c, direction], last_send.at[h, direction, t, b],
                                 last_recv.at[h, direction, t, c], cores[direction][b]))
                else:
                    go_on(remote(src, arrive.at[h, direction, step, t, b], send.at[h, direction, step, t, b],
                                 recv.at[h, direction, step, t, b], devs[direction]))

        def begin(h):
            for direction in range(2):
                go(h, direction, 0, direction)
            for direction in range(2):
                go(h, direction, 1, 1 - direction)

        def step_on(h, step):
            for t in (1, 0):
                for direction in range(2):
                    if not (step == 1 and t != direction):
                        go(h, direction, step, t)

        def ended(h, t, core):
            total = None
            for direction in range(2):
                ref = last.at[h, t, core, direction]
                remote(ref, ref, last_send.at[h, direction, t, 0], last_recv.at[h, direction, t, core],
                       partner).wait_recv()
                total = ref[...].astype(F32) if total is None else total + ref[...].astype(F32)
            return total

        return begin, step_on, ended

    zbegin, zsum_on, zended = summing(key_part, zin, zsum, rz_send, rz_recv, zdev, zfin, lz_send, lz_recv, zcores, z, NZ)
    xbegin, xsum_on, xended = summing(query_part, xin, xsum, rx_send, rx_recv, xdev, xfin, lx_send, lx_recv, xcores, x, NX)
    outs = (o_out, dq_out, dk_out, dv_out)

    def own_part(h, n, b):
        if n < 2:
            return query_part(h, n, x)(b)
        value = own_acc[h, n - 2, b]
        return key_part(h, n - 2, z)(b) + (value * SCALE if n == 2 else value)

    def give(h, ns):
        for n in ns:
            final[h, n] = own_part(h, n, 1 - c).astype(BF16)
            go_on(remote(final.at[h, n], gift.at[h, n], f_send.at[h, n], f_recv.at[h, n], partner))

    def finish(h, ns):
        for n in ns:
            ended = xended if n < 2 else zended
            mine = own_part(h, n, c) + ended(h, n % 2, c)
            outs[n][:, lanes_of(2 * c + h)] = mine.astype(BF16)
            remote(gift.at[h, n], gift.at[h, n], f_send.at[h, n], f_recv.at[h, n], partner).wait_recv()
            theirs = gift[h, n].astype(F32) + ended(h, n % 2, 1 - c)
            outs[n][:, lanes_of(2 * (1 - c) + h)] = theirs.astype(BF16)

    exchange(0, 0)
    exchange(0, 1)
    exchange(1, 0)
    zstart(0, 0)
    exchange(1, 1)
    zstart(0, 1)
    exchange_grad(0)
    exchange(0, 2)
    zstart(1, 0)
    exchange_grad(1)
    exchange(1, 2)
    zstep(0, 0)
    zstart(1, 1)
    xstart(0)
    plan(0)
    zstep(0, 1)
    zstep(1, 0, (0,))
    xstart(1)
    xstep(0)
    zstep(0, 2)
    zstep(1, 0, (1,))
    plan(1)
    xend(0)
    zend(0)
    pairs = [(i, i + 1) for i in range(0, ROW, 2)]
    count_units(0, pairs[0])
    count_units(0, pairs[1])
    zstep(1, 1)
    count_units(0, pairs[2])
    count_units(0, pairs[3])
    count_rest(0)
    send_stats(0)
    xstep(1)
    zstep(1, 2)
    take_stats(0)
    grad_units(0, pairs[0])
    xend(1)
    grad_units(0, pairs[1])
    grad_units(0, pairs[2])
    zend(1)
    for units in pairs:
        count_units(1, units)
    count_rest(1)
    send_stats(1)
    grad_units(0, pairs[3])
    grad_rim(0)
    zbegin(0)
    xbegin(0)
    grad_own(0)
    give(0, range(4))
    take_stats(1)
    grad_units(1, pairs[0])
    zsum_on(0, 1)
    xsum_on(0, 1)
    grad_units(1, pairs[1])
    grad_units(1, pairs[2])
    zsum_on(0, 2)
    grad_units(1, pairs[3])
    grad_rim(1)
    zbegin(1)
    xbegin(1)
    zsum_on(0, 3)
    grad_own(1)
    give(1, range(4))
    zsum_on(1, 1)
    xsum_on(1, 1)
    finish(0, (0, 1))
    zsum_on(1, 2)
    finish(0, (2, 3))
    finish(1, (0, 1))
    zsum_on(1, 3)
    finish(1, (3, 2))
    for cp in sends:
        cp.wait_send()


def place_kernel(*refs):
    for n in range(4):
        refs[4 + n][...] = refs[n][...]


def vmem():
    return pl.BlockSpec(memory_space=pltpu.VMEM)


def smem():
    return pl.BlockSpec(memory_space=pltpu.SMEM)


def on_device(query_rows, key_rows, value_rows, out_grad, random_blocks):
    dma = pltpu.SemaphoreType.DMA
    mem = pltpu.VMEM
    tile = (BLK, HD)
    full = jax.ShapeDtypeStruct((BLK, 4 * HD), BF16)
    zs, xs = NZ // 2, NX // 2
    outs = pl.pallas_call(
        attention_kernel,
        out_shape=(full,) * 4,
        in_specs=[smem()] + [vmem()] * 4,
        out_specs=[vmem()] * 4,
        scratch_shapes=[
            *[mem((COL,) + tile, BF16)] * 4, *[mem((ROW,) + tile, BF16)] * 4,
            mem((2, 4, 3, ROW, HD), F32), mem((2, NX, 3, ROW, HD), F32), mem((2, 3, ROW, HD), F32),
            mem((2, 2, ENTRIES) + tile, F32), mem((2, 2) + tile, F32), mem((2, 2, 2) + tile, F32),
            mem((2, ROW) + tile, F32), mem((2, ROW) + tile, F32),
            mem((2, 2, zs, 2, 2) + tile, BF16), mem((2, 2, zs, 2, 2) + tile, BF16),
            mem((2, 2, xs, 2, 2) + tile, BF16), mem((2, 2, xs, 2, 2) + tile, BF16),
            mem((2, 2, 2, 2) + tile, BF16), mem((2, 2, 2, 2) + tile, BF16),
            mem((2, 4) + tile, BF16), mem((2, 4) + tile, BF16),
            pltpu.SMEM((2 * ENTRIES,), jnp.int32), pltpu.SMEM((2 * ENTRIES,), jnp.int32), pltpu.SMEM((2 * COL,), jnp.int32),
            dma((2, 3, 2 * NY)), dma((2, 3, 2 * NY)), dma((2, 3)), dma((2,)), dma((2,)), dma((2,)),
            dma((2, 2, zs, 2)), dma((2, 2, zs, 2)), dma((2, 2, xs, 2)), dma((2, 2, xs, 2)),
            dma((2, NX)), dma((2, NX)),
            dma((2, 2, zs, 2, 2)), dma((2, 2, zs, 2, 2)), dma((2, 2, xs, 2, 2)), dma((2, 2, xs, 2, 2)),
            dma((2, 2, 2, 2)), dma((2, 2, 2, 2)), dma((2, 2, 2, 2)), dma((2, 2, 2, 2)),
            dma((2, 4)), dma((2, 4)),
        ],
        compiler_params=pltpu.CompilerParams(collective_id=0, has_side_effects=True),
        name="attention",
    )(random_blocks.transpose(2, 0, 1), query_rows, key_rows, value_rows, out_grad)
    return pl.pallas_call(
        place_kernel,
        out_shape=(full,) * 4,
        in_specs=[vmem()] * 4,
        out_specs=[vmem()] * 4,
        name="place",
    )(*outs)


def solution(mesh):
    in_specs = (
        P(("seq", "head"), None),
        P(("seq", "head"), None),
        P(("seq", "head"), None),
        P("seq", "head"),
        P("head", None, None),
    )
    out_specs = (P("seq", "head"),) * 4
    return jax.shard_map(
        on_device, mesh=mesh, in_specs=in_specs, out_specs=out_specs, check_vma=False
    )
```

```python
import math

import jax
import jax.numpy as jnp
from jax import lax
from jax.experimental import pallas as pl
from jax.experimental.pallas import tpu as pltpu
from jax.sharding import PartitionSpec as P

HD = 128
BLK = 128
NX = 4
NZ = 8
NY = 4
COL = 2 * NZ
ROW = 2 * NX
RAND = 3
LEFT = RAND * ROW
RIGHT = LEFT + 1
WIDE = LEFT + 2
ENTRIES = LEFT + 3
SCALE = 1.0 / math.sqrt(HD)
NEG = -1e30
VMEM_LIMIT = 32 << 20
MESH = pl.DeviceIdType.MESH
NT = (((1,), (1,)), ((), ()))
NN = (((1,), (0,)), ((), ()))
TN = (((0,), (0,)), ((), ()))
F32 = jnp.float32
BF16 = jnp.bfloat16


def dot(a, b, dims):
    return lax.dot_general(a, b, dims, preferred_element_type=F32)


def place_of(x, z, c):
    return (x * NZ + z) * 2 + c


def remote(src, dst, send_sem, recv_sem, dev):
    return pltpu.make_async_remote_copy(
        src_ref=src, dst_ref=dst, send_sem=send_sem, recv_sem=recv_sem,
        device_id=dev, device_id_type=MESH,
    )


def meet(devs):
    barrier = pltpu.get_barrier_semaphore()
    for dev in devs:
        pl.semaphore_signal(barrier, inc=1, device_id=dev, device_id_type=MESH)
    pl.semaphore_wait(barrier, len(devs))


def attention_kernel(rb_in, q_ref, k_ref, v_ref, g_ref, o_out, dq_out, dk_out, dv_out,
                     kall0, kall1, vall0, vall1, qrow0, qrow1, grow0, grow1, sets, stats, rows, acc, wide_acc, own_acc, o_acc, dq_acc,
                     zin, zsum, xin, xsum, zfin, xfin, final, gift, rb_ref, owner_s, prev_s, last_s, rb_sem,
                     a_send, a_recv, a_own, g_send, g_recv, g_own, z_send, z_recv, x_send, x_recv, s_send, s_recv,
                     rz_send, rz_recv, rx_send, rx_recv, lz_send, lz_recv, lx_send, lx_recv, f_send, f_recv):
    s = lax.axis_index("seq")
    y = lax.axis_index("head")
    x = s // (2 * NZ)
    z = (s // 2) % NZ
    c = s % 2
    me = y * 2 + c
    kall, vall, qrow, grow = (kall0, kall1), (vall0, vall1), (qrow0, qrow1), (grow0, grow1)

    def member(d):
        other = (me + d) % (2 * NY)
        return other % 2, other // 2

    def at(xx, zz):
        return (place_of(xx, zz, c), y)

    group = []
    for d in range(1, 2 * NY):
        cc, yy = member(d)
        group.append((place_of(x, z, cc), yy))
    zdev = (at(x, (z + 1) % NZ), at(x, (z + NZ - 1) % NZ))
    xall = [at((x + d) % NX, z) for d in range(1, NX)]
    xdev = (xall[0], xall[NX - 2])
    partner = (place_of(x, z, 1 - c), y)

    def either(xx, zz):
        return [(place_of(xx, zz, b), y) for b in range(2)]

    def across(xx, zz):
        return (place_of(xx, zz, 1 - c), y)

    zcores = (either(x, (z + 1) % NZ), either(x, (z + NZ - 1) % NZ))
    xcores = (either((x + 1) % NX, z), either((x + NX - 1) % NX, z))
    meet(group + list(zdev) + xall + [across(x, (z + 1) % NZ), across(x, (z + NZ - 1) % NZ),
                                      across((x + 1) % NX, z), across((x + NX - 1) % NX, z)])

    lists = pltpu.make_async_copy(rb_in, rb_ref, rb_sem)
    lists.start()
    sends = []

    def go_on(cp):
        cp.start()
        sends.append(cp)

    def lanes_of(n):
        return pl.ds(pl.multiple_of(n * HD, HD), HD)

    ins = (k_ref, v_ref, q_ref)
    bufs = (kall, vall, qrow)
    slot = (2 * z, 2 * z, 2 * x)
    own = {}

    def exchange(h, t):
        dst = bufs[t][h].at[slot[t] + c, pl.ds(pl.multiple_of(y * 32, 32), 32), :]
        for d in range(1, 2 * NY):
            cc, yy = member(d)
            go_on(remote(ins[t].at[:, lanes_of(yy * 4 + cc * 2 + h)], dst, a_send.at[h, t, d], a_recv.at[h, t, d],
                         group[d - 1]))
        own[h, t] = pltpu.make_async_copy(ins[t].at[:, lanes_of(me * 2 + h)], dst, a_own.at[h, t])
        own[h, t].start()

    def exchange_grad(h):
        go_on(remote(g_ref.at[:, lanes_of(2 * (1 - c) + h)], grow[h].at[2 * x + c], g_send.at[h], g_recv.at[h], partner))
        own[h, 3] = pltpu.make_async_copy(g_ref.at[:, lanes_of(2 * c + h)], grow[h].at[2 * x + c], g_own.at[h])
        own[h, 3].start()

    def arrived(h, t):
        own[h, t].wait()
        for d in range(1, 2 * NY):
            other = (me + 2 * NY - d) % (2 * NY)
            cs, ys = other % 2, other // 2
            dst = bufs[t][h].at[slot[t] + cs, pl.ds(pl.multiple_of(ys * 32, 32), 32), :]
            remote(dst, dst, a_send.at[h, t, d], a_recv.at[h, t, d], partner).wait_recv()

    def arrived_grad(h):
        own[h, 3].wait()
        dst = grow[h].at[2 * x + 1 - c]
        remote(dst, dst, g_send.at[h], g_recv.at[h], partner).wait_recv()

    def ring(bufs2, send, recv, devs, pos, count):
        def piece(h, t, owner):
            return bufs2[t][h].at[pl.ds(2 * owner, 2)]

        def copy(h, direction, step, t):
            owner = (pos + count - step) % count if direction == 0 else (pos + step) % count
            ref = piece(h, t, owner)
            go_on(remote(ref, ref, send.at[h, direction, step, t], recv.at[h, direction, step, t], devs[direction]))

        def wait(h, direction, step, t):
            owner = (pos + count - 1 - step) % count if direction == 0 else (pos + 1 + step) % count
            ref = piece(h, t, owner)
            remote(ref, ref, send.at[h, direction, step, t], recv.at[h, direction, step, t],
                   devs[direction]).wait_recv()

        return copy, wait

    zcopy, zwait = ring((kall, vall), z_send, z_recv, zdev, z, NZ)
    xcopy, xwait = ring((qrow, grow), x_send, x_recv, xdev, x, NX)
    zlast = NZ // 2 - 1

    def zstart(h, t):
        arrived(h, t)
        for direction in range(2):
            zcopy(h, direction, 0, t)

    def xstart(h):
        arrived_grad(h)
        for direction in range(2):
            xcopy(h, direction, 0, 1)
        arrived(h, 2)
        for direction in range(2):
            xcopy(h, direction, 0, 0)

    def zstep(h, step, tensors=(0, 1)):
        for t in tensors:
            for direction in range(2):
                zwait(h, direction, step, t)
                if step + 1 < zlast or direction == t:
                    zcopy(h, direction, step + 1, t)

    def xstep(h):
        for t in (1, 0):
            for direction in range(2):
                xwait(h, direction, 0, t)
                if direction == t:
                    xcopy(h, direction, 1, t)

    def zend(h):
        for t in range(2):
            zwait(h, t, zlast, t)

    def xend(h):
        for t in range(2):
            xwait(h, t, 1, t)

    edge = (x == 0) | (x == NX - 1)
    wide_at = jnp.where(x == 0, 0, COL - 1)
    left_q = 2 * ((x + jnp.where(z == 0, 1, 0)) % NX)
    right_q = 2 * ((x + jnp.where(z == NZ - 1, NX - 1, 0)) % NX) + 1
    left_k = (2 * z + COL - 1) % COL
    right_k = (2 * z + 2) % COL

    def plan(h):
        owners = []
        for i in range(ROW):
            for r in range(RAND):
                j = rb_ref[r, 2 * c + h, COL * (i // 2) + 2 * z + i % 2] - COL * x
                owners.append(jnp.where((j >= 0) & (j < COL), j, -1))
        owners += [left_k, right_k, jnp.where(edge, wide_at, -1)]
        for e in range(ENTRIES):
            prev = jnp.int32(-1)
            for f in range(e):
                prev = jnp.where(owners[f] == owners[e], f, prev)
            owner_s[h * ENTRIES + e] = owners[e]
            prev_s[h * ENTRIES + e] = prev
        for j in range(COL):
            last = jnp.int32(-1)
            for e in range(ENTRIES):
                last = jnp.where(owners[e] == j, e, last)
            last_s[h * COL + j] = last

    def listed(h, e):
        j = owner_s[h * ENTRIES + e]
        return jnp.maximum(j, 0), jnp.where(j < 0, NEG, 0.0)

    wide_bias = jnp.where(edge, 0.0, NEG)

    def stack(tiles):
        return tiles[0] if len(tiles) == 1 else jnp.concatenate(tiles, axis=0)

    def pieces(value, count):
        size = value.shape[0] // count
        return [value[n * size:(n + 1) * size] for n in range(count)]

    def score(ks, q):
        scores = pieces(dot(stack([k for k, _ in ks]), q, NT), len(ks))
        return [sc * SCALE if bias is None else sc * SCALE + bias for sc, (_, bias) in zip(scores, ks)]

    def measure(ks, vs, q, g):
        scores = score(ks, q)
        peak = scores[0]
        for sc in scores[1:]:
            peak = jnp.maximum(peak, sc)
        peak = jnp.max(peak, axis=0, keepdims=True)
        total = weighted = None
        for sc, dp in zip(scores, pieces(dot(stack(vs), g, NT), len(vs))):
            e = jnp.exp(sc - peak)
            w = e * dp
            total = e if total is None else total + e
            weighted = w if weighted is None else weighted + w
        return peak, jnp.sum(total, axis=0, keepdims=True), jnp.sum(weighted, axis=0, keepdims=True)

    def window(h):
        mine = pl.ds(2 * z, 2)
        here = pl.ds(2 * x, 2)
        return tuple(ref[h][at_, :, :].reshape(2 * BLK, HD)
                     for ref, at_ in ((kall, mine), (vall, mine), (qrow, here), (grow, here)))

    def tiles_of(h, i):
        ks, vs = [], []
        for r in range(RAND):
            j, bias = listed(h, RAND * i + r)
            ks.append((kall[h][j], bias))
            vs.append(vall[h][j])
        ks.append((kall[h][wide_at], wide_bias))
        vs.append(vall[h][wide_at])
        return ks, vs

    def count_units(h, units):
        for i in units:
            ks, vs = tiles_of(h, i)
            for n, row in enumerate(measure(ks, vs, qrow[h][i], grow[h][i])):
                sets[h, 0, n, i:i + 1, :] = row

    def count_rest(h):
        for part in range(1, 4):
            sets[h, part, 0] = jnp.full((ROW, HD), NEG, F32)
            sets[h, part, 1] = jnp.zeros((ROW, HD), F32)
            sets[h, part, 2] = jnp.zeros((ROW, HD), F32)
        k, v, q, g = window(h)
        for n, row in enumerate(measure([(k, None)], [v], q, g)):
            sets[h, 1, n, pl.ds(2 * x, 1), :] = row[:, :HD]
            sets[h, 1, n, pl.ds(2 * x + 1, 1), :] = row[:, HD:]
        for part, qi, kj in ((2, left_q, left_k), (3, right_q, right_k)):
            for n, row in enumerate(measure([(kall[h][kj], None)], [vall[h][kj]], qrow[h][qi], grow[h][qi])):
                sets[h, part, n, pl.ds(qi, 1), :] = row

    def merge(parts):
        peak = jnp.maximum(jnp.maximum(parts[0][0], parts[1][0]), jnp.maximum(parts[2][0], parts[3][0]))
        shift = [jnp.exp(p[0] - peak) for p in parts]
        total = sum(p[1] * f for p, f in zip(parts, shift))
        return peak, total, sum(p[2] * f for p, f in zip(parts, shift))

    def send_stats(h):
        for n, value in enumerate(merge([[sets[h, part, n] for n in range(3)] for part in range(4)])):
            stats[h, x, n] = value
        for d in range(1, NX):
            go_on(remote(stats.at[h, x], stats.at[h, x], s_send.at[h, d], s_recv.at[h, d], xall[d - 1]))

    def take_stats(h):
        for d in range(1, NX):
            src = (x + NX - d) % NX
            remote(stats.at[h, src], stats.at[h, src], s_send.at[h, d], s_recv.at[h, d], xall[d - 1]).wait_recv()
        peak, total, weighted = merge([[stats[h, i, n] for n in range(3)] for i in range(NX)])
        inverse = 1.0 / total
        rows[h, 0] = peak
        rows[h, 1] = inverse
        rows[h, 2] = weighted * inverse

    def weigh(ks, vs, q, g, row):
        peak, inverse, delta = row
        wb, ds = [], []
        for sc, dp in zip(score(ks, q), pieces(dot(stack(vs), g, NT), len(vs))):
            w = jnp.exp(sc - peak) * inverse
            wb.append(w.astype(BF16))
            ds.append((w * (dp - delta)).astype(BF16))
        wb, ds = stack(wb), stack(ds)
        k, v = stack([k for k, _ in ks]), stack(vs)
        return dot(ds, q, NN), dot(wb, g, NN), dot(wb, v, TN), dot(ds, k, TN)

    def row_of(h, i):
        return [rows[h, n, pl.ds(i, 1), :] for n in range(3)]

    def store_entry(h, e, dk, dv):
        prev = prev_s[h * ENTRIES + e]
        back = jnp.maximum(prev, 0)
        acc[h, 0, e] = dk + jnp.where(prev < 0, 0.0, acc[h, 0, back])
        acc[h, 1, e] = dv + jnp.where(prev < 0, 0.0, acc[h, 1, back])

    def grad_units(h, units):
        for i in units:
            ks, vs = tiles_of(h, i)
            dks, dvs, o, dq = weigh(ks, vs, qrow[h][i], grow[h][i], row_of(h, i))
            for r, (dk, dv) in enumerate(zip(pieces(dks, len(ks)), pieces(dvs, len(vs)))):
                if r < RAND:
                    store_entry(h, RAND * i + r, dk, dv)
                elif i == 0:
                    wide_acc[h, 0] = dk
                    wide_acc[h, 1] = dv
                else:
                    wide_acc[h, 0] += dk
                    wide_acc[h, 1] += dv
            o_acc[h, i] = o
            dq_acc[h, i] = dq

    def grad_rim(h):
        for e, qi, kj in ((LEFT, left_q, left_k), (RIGHT, right_q, right_k)):
            dk, dv, o, dq = weigh([(kall[h][kj], None)], [vall[h][kj]], qrow[h][qi], grow[h][qi], row_of(h, qi))
            store_entry(h, e, dk, dv)
            o_acc[h, qi] += o
            dq_acc[h, qi] += dq
        store_entry(h, WIDE, wide_acc[h, 0], wide_acc[h, 1])

    def grad_own(h):
        k, v, q, g = window(h)
        row = [jnp.concatenate([a, b], axis=1) for a, b in zip(row_of(h, 2 * x), row_of(h, 2 * x + 1))]
        dk, dv, o, dq = weigh([(k, None)], [v], q, g, row)
        own_acc[h, 0] = dk.reshape(2, BLK, HD)
        own_acc[h, 1] = dv.reshape(2, BLK, HD)
        here = pl.ds(2 * x, 2)
        o_acc[h, here] += o.reshape(2, BLK, HD)
        dq_acc[h, here] += dq.reshape(2, BLK, HD)

    def key_part(h, t, target):
        def one(b):
            last = last_s[h * COL + 2 * target + b]
            value = acc[h, t, jnp.maximum(last, 0)]
            value = jnp.where(last < 0, 0.0, value)
            return value * SCALE if t == 0 else value
        return one

    def query_part(h, t, target):
        def one(b):
            value = (o_acc, dq_acc)[t][h, 2 * target + b]
            return value * SCALE if t == 1 else value
        return one

    def summing(part, arrive, summed, send, recv, devs, last, last_send, last_recv, cores, pos, count):
        steps = count // 2

        def wait(h, direction, step, t, b):
            ref = arrive.at[h, direction, step, t, b]
            remote(ref, ref, send.at[h, direction, step, t, b], recv.at[h, direction, step, t, b],
                   devs[direction]).wait_recv()
            return ref

        def go(h, direction, step, t):
            away = steps - step
            target = (pos + away) % count if direction == 0 else (pos + count - away) % count
            mine = part(h, t, target)
            for b in range(2):
                value = mine(b)
                if step != (0 if t == direction else 1):
                    value = value + wait(h, direction, step - 1, t, b)[...].astype(F32)
                src = summed.at[h, direction, step, t, b]
                src[...] = value.astype(BF16)
                if step == steps - 1:
                    go_on(remote(src, last.at[h, t, c, direction], last_send.at[h, direction, t, b],
                                 last_recv.at[h, direction, t, c], cores[direction][b]))
                else:
                    go_on(remote(src, arrive.at[h, direction, step, t, b], send.at[h, direction, step, t, b],
                                 recv.at[h, direction, step, t, b], devs[direction]))

        def begin(h):
            for direction in range(2):
                go(h, direction, 0, direction)
            for direction in range(2):
                go(h, direction, 1, 1 - direction)

        def step_on(h, step):
            for t in (1, 0):
                for direction in range(2):
                    if not (step == 1 and t != direction):
                        go(h, direction, step, t)

        def ended(h, t, core):
            total = None
            for direction in range(2):
                ref = last.at[h, t, core, direction]
                remote(ref, ref, last_send.at[h, direction, t, 0], last_recv.at[h, direction, t, core],
                       partner).wait_recv()
                total = ref[...].astype(F32) if total is None else total + ref[...].astype(F32)
            return total

        return begin, step_on, ended

    zbegin, zsum_on, zended = summing(key_part, zin, zsum, rz_send, rz_recv, zdev, zfin, lz_send, lz_recv, zcores, z, NZ)
    xbegin, xsum_on, xended = summing(query_part, xin, xsum, rx_send, rx_recv, xdev, xfin, lx_send, lx_recv, xcores, x, NX)
    outs = (o_out, dq_out, dk_out, dv_out)

    def own_part(h, n, b):
        if n < 2:
            return query_part(h, n, x)(b)
        value = own_acc[h, n - 2, b]
        return key_part(h, n - 2, z)(b) + (value * SCALE if n == 2 else value)

    def give(h, ns):
        for n in ns:
            final[h, n] = own_part(h, n, 1 - c).astype(BF16)
            go_on(remote(final.at[h, n], gift.at[h, n], f_send.at[h, n], f_recv.at[h, n], partner))

    def finish(h, ns):
        for n in ns:
            ended = xended if n < 2 else zended
            mine = own_part(h, n, c) + ended(h, n % 2, c)
            outs[n][:, lanes_of(2 * c + h)] = mine.astype(BF16)
            remote(gift.at[h, n], gift.at[h, n], f_send.at[h, n], f_recv.at[h, n], partner).wait_recv()
            theirs = gift[h, n].astype(F32) + ended(h, n % 2, 1 - c)
            outs[n][:, lanes_of(2 * (1 - c) + h)] = theirs.astype(BF16)

    exchange(0, 0)
    exchange(0, 1)
    exchange(1, 0)
    zstart(0, 0)
    exchange(1, 1)
    zstart(0, 1)
    exchange_grad(0)
    exchange(0, 2)
    zstart(1, 0)
    exchange_grad(1)
    exchange(1, 2)
    zstep(0, 0)
    zstart(1, 1)
    xstart(0)
    lists.wait()
    plan(0)
    zstep(0, 1)
    zstep(1, 0, (0,))
    xstart(1)
    xstep(0)
    zstep(0, 2)
    zstep(1, 0, (1,))
    plan(1)
    xend(0)
    zend(0)
    pairs = [(i, i + 1) for i in range(0, ROW, 2)]
    count_units(0, pairs[0])
    count_units(0, pairs[1])
    zstep(1, 1)
    count_units(0, pairs[2])
    count_units(0, pairs[3])
    count_rest(0)
    send_stats(0)
    xstep(1)
    zstep(1, 2)
    take_stats(0)
    grad_units(0, pairs[0])
    xend(1)
    grad_units(0, pairs[1])
    grad_units(0, pairs[2])
    zend(1)
    for units in pairs:
        count_units(1, units)
    count_rest(1)
    send_stats(1)
    grad_units(0, pairs[3])
    grad_rim(0)
    zbegin(0)
    xbegin(0)
    grad_own(0)
    give(0, range(4))
    take_stats(1)
    grad_units(1, pairs[0])
    zsum_on(0, 1)
    xsum_on(0, 1)
    grad_units(1, pairs[1])
    grad_units(1, pairs[2])
    zsum_on(0, 2)
    grad_units(1, pairs[3])
    grad_rim(1)
    zbegin(1)
    xbegin(1)
    zsum_on(0, 3)
    grad_own(1)
    give(1, range(4))
    zsum_on(1, 1)
    xsum_on(1, 1)
    finish(0, (0, 1))
    zsum_on(1, 2)
    finish(0, (2, 3))
    finish(1, (0, 1))
    zsum_on(1, 3)
    finish(1, (3, 2))
    for cp in sends:
        cp.wait_send()


def place_kernel(*refs):
    for n in range(4):
        refs[4 + n][...] = refs[n][...]


def vmem():
    return pl.BlockSpec(memory_space=pltpu.VMEM)


def smem():
    return pl.BlockSpec(memory_space=pltpu.SMEM)


def on_device(query_rows, key_rows, value_rows, out_grad, random_blocks):
    dma = pltpu.SemaphoreType.DMA
    mem = pltpu.VMEM
    tile = (BLK, HD)
    full = jax.ShapeDtypeStruct((BLK, 4 * HD), BF16)
    zs, xs = NZ // 2, NX // 2
    outs = pl.pallas_call(
        attention_kernel,
        out_shape=(full,) * 4,
        in_specs=[pl.BlockSpec(memory_space=pltpu.HBM)] * 5,
        out_specs=[vmem()] * 4,
        scratch_shapes=[
            *[mem((COL,) + tile, BF16)] * 4, *[mem((ROW,) + tile, BF16)] * 4,
            mem((2, 4, 3, ROW, HD), F32), mem((2, NX, 3, ROW, HD), F32), mem((2, 3, ROW, HD), F32),
            mem((2, 2, ENTRIES) + tile, F32), mem((2, 2) + tile, F32), mem((2, 2, 2) + tile, F32),
            mem((2, ROW) + tile, F32), mem((2, ROW) + tile, F32),
            mem((2, 2, zs, 2, 2) + tile, BF16), mem((2, 2, zs, 2, 2) + tile, BF16),
            mem((2, 2, xs, 2, 2) + tile, BF16), mem((2, 2, xs, 2, 2) + tile, BF16),
            mem((2, 2, 2, 2) + tile, BF16), mem((2, 2, 2, 2) + tile, BF16),
            mem((2, 4) + tile, BF16), mem((2, 4) + tile, BF16),
            pltpu.SMEM((RAND, 4, NX * COL), jnp.int32),
            pltpu.SMEM((2 * ENTRIES,), jnp.int32), pltpu.SMEM((2 * ENTRIES,), jnp.int32), pltpu.SMEM((2 * COL,), jnp.int32), dma,
            dma((2, 3, 2 * NY)), dma((2, 3, 2 * NY)), dma((2, 3)), dma((2,)), dma((2,)), dma((2,)),
            dma((2, 2, zs, 2)), dma((2, 2, zs, 2)), dma((2, 2, xs, 2)), dma((2, 2, xs, 2)),
            dma((2, NX)), dma((2, NX)),
            dma((2, 2, zs, 2, 2)), dma((2, 2, zs, 2, 2)), dma((2, 2, xs, 2, 2)), dma((2, 2, xs, 2, 2)),
            dma((2, 2, 2, 2)), dma((2, 2, 2, 2)), dma((2, 2, 2, 2)), dma((2, 2, 2, 2)),
            dma((2, 4)), dma((2, 4)),
        ],
        compiler_params=pltpu.CompilerParams(collective_id=0, has_side_effects=True, vmem_limit_bytes=VMEM_LIMIT),
        name="attention",
    )(*(pltpu.with_memory_space_constraint(a, pltpu.HBM)
        for a in (random_blocks.transpose(2, 0, 1), query_rows, key_rows, value_rows, out_grad)))
    return pl.pallas_call(
        place_kernel,
        out_shape=(full,) * 4,
        in_specs=[vmem()] * 4,
        out_specs=[vmem()] * 4,
        compiler_params=pltpu.CompilerParams(vmem_limit_bytes=4 << 20),
        name="place",
    )(*outs)


def solution(mesh):
    in_specs = (
        P(("seq", "head"), None),
        P(("seq", "head"), None),
        P(("seq", "head"), None),
        P("seq", "head"),
        P("head", None, None),
    )
    out_specs = (P("seq", "head"),) * 4
    return jax.shard_map(
        on_device, mesh=mesh, in_specs=in_specs, out_specs=out_specs, check_vma=False
    )
```

```python
import math

import jax
import jax.numpy as jnp
from jax import lax
from jax.experimental import pallas as pl
from jax.experimental.pallas import tpu as pltpu
from jax.sharding import PartitionSpec as P

HD = 128
BLK = 128
NX = 4
NZ = 8
NY = 4
COL = 2 * NZ
ROW = 2 * NX
RAND = 3
LEFT = RAND * ROW
RIGHT = LEFT + 1
WIDE = LEFT + 2
ENTRIES = LEFT + 3
SCALE = 1.0 / math.sqrt(HD)
NEG = -1e30
VMEM_LIMIT = 44 << 20
MESH = pl.DeviceIdType.MESH
NT = (((1,), (1,)), ((), ()))
NN = (((1,), (0,)), ((), ()))
TN = (((0,), (0,)), ((), ()))
F32 = jnp.float32
BF16 = jnp.bfloat16


def dot(a, b, dims):
    return lax.dot_general(a, b, dims, preferred_element_type=F32)


def place_of(x, z, c):
    return (x * NZ + z) * 2 + c


def remote(src, dst, send_sem, recv_sem, dev):
    return pltpu.make_async_remote_copy(
        src_ref=src, dst_ref=dst, send_sem=send_sem, recv_sem=recv_sem,
        device_id=dev, device_id_type=MESH,
    )


def meet(devs):
    barrier = pltpu.get_barrier_semaphore()
    for dev in devs:
        pl.semaphore_signal(barrier, inc=1, device_id=dev, device_id_type=MESH)
    pl.semaphore_wait(barrier, len(devs))


def attention_kernel(rb_in, q_ref, k_ref, v_ref, g_ref, o_out, dq_out, dk_out, dv_out,
                     kall0, kall1, vall0, vall1, qrow0, qrow1, grow0, grow1, sets, stats, rows, acc, wide_acc, own_acc, o_acc, dq_acc,
                     zin, zsum, xin, xsum, zfin, xfin, final, gift, kept_e, kept_p, rb_ref, owner_s, prev_s, last_s, rb_sem,
                     a_send, a_recv, a_own, g_send, g_recv, g_own, z_send, z_recv, x_send, x_recv, s_send, s_recv,
                     rz_send, rz_recv, rx_send, rx_recv, lz_send, lz_recv, lx_send, lx_recv, f_send, f_recv):
    s = lax.axis_index("seq")
    y = lax.axis_index("head")
    x = s // (2 * NZ)
    z = (s // 2) % NZ
    c = s % 2
    me = y * 2 + c
    kall, vall, qrow, grow = (kall0, kall1), (vall0, vall1), (qrow0, qrow1), (grow0, grow1)

    def member(d):
        other = (me + d) % (2 * NY)
        return other % 2, other // 2

    def at(xx, zz):
        return (place_of(xx, zz, c), y)

    group = []
    for d in range(1, 2 * NY):
        cc, yy = member(d)
        group.append((place_of(x, z, cc), yy))
    zdev = (at(x, (z + 1) % NZ), at(x, (z + NZ - 1) % NZ))
    xall = [at((x + d) % NX, z) for d in range(1, NX)]
    xdev = (xall[0], xall[NX - 2])
    partner = (place_of(x, z, 1 - c), y)

    def either(xx, zz):
        return [(place_of(xx, zz, b), y) for b in range(2)]

    def across(xx, zz):
        return (place_of(xx, zz, 1 - c), y)

    zcores = (either(x, (z + 1) % NZ), either(x, (z + NZ - 1) % NZ))
    xcores = (either((x + 1) % NX, z), either((x + NX - 1) % NX, z))
    meet(group + list(zdev) + xall + [across(x, (z + 1) % NZ), across(x, (z + NZ - 1) % NZ),
                                      across((x + 1) % NX, z), across((x + NX - 1) % NX, z)])

    lists = pltpu.make_async_copy(rb_in, rb_ref, rb_sem)
    lists.start()
    sends = []

    def go_on(cp):
        cp.start()
        sends.append(cp)

    def lanes_of(n):
        return pl.ds(pl.multiple_of(n * HD, HD), HD)

    ins = (k_ref, v_ref, q_ref)
    bufs = (kall, vall, qrow)
    slot = (2 * z, 2 * z, 2 * x)
    own = {}

    def exchange(h, t):
        dst = bufs[t][h].at[slot[t] + c, pl.ds(pl.multiple_of(y * 32, 32), 32), :]
        for d in range(1, 2 * NY):
            cc, yy = member(d)
            go_on(remote(ins[t].at[:, lanes_of(yy * 4 + cc * 2 + h)], dst, a_send.at[h, t, d], a_recv.at[h, t, d],
                         group[d - 1]))
        own[h, t] = pltpu.make_async_copy(ins[t].at[:, lanes_of(me * 2 + h)], dst, a_own.at[h, t])
        own[h, t].start()

    def exchange_grad(h):
        go_on(remote(g_ref.at[:, lanes_of(2 * (1 - c) + h)], grow[h].at[2 * x + c], g_send.at[h], g_recv.at[h], partner))
        own[h, 3] = pltpu.make_async_copy(g_ref.at[:, lanes_of(2 * c + h)], grow[h].at[2 * x + c], g_own.at[h])
        own[h, 3].start()

    def arrived(h, t):
        own[h, t].wait()
        for d in range(1, 2 * NY):
            other = (me + 2 * NY - d) % (2 * NY)
            cs, ys = other % 2, other // 2
            dst = bufs[t][h].at[slot[t] + cs, pl.ds(pl.multiple_of(ys * 32, 32), 32), :]
            remote(dst, dst, a_send.at[h, t, d], a_recv.at[h, t, d], partner).wait_recv()

    def arrived_grad(h):
        own[h, 3].wait()
        dst = grow[h].at[2 * x + 1 - c]
        remote(dst, dst, g_send.at[h], g_recv.at[h], partner).wait_recv()

    def ring(bufs2, send, recv, devs, pos, count):
        def piece(h, t, owner):
            return bufs2[t][h].at[pl.ds(2 * owner, 2)]

        def copy(h, direction, step, t):
            owner = (pos + count - step) % count if direction == 0 else (pos + step) % count
            ref = piece(h, t, owner)
            go_on(remote(ref, ref, send.at[h, direction, step, t], recv.at[h, direction, step, t], devs[direction]))

        def wait(h, direction, step, t):
            owner = (pos + count - 1 - step) % count if direction == 0 else (pos + 1 + step) % count
            ref = piece(h, t, owner)
            remote(ref, ref, send.at[h, direction, step, t], recv.at[h, direction, step, t],
                   devs[direction]).wait_recv()

        return copy, wait

    zcopy, zwait = ring((kall, vall), z_send, z_recv, zdev, z, NZ)
    xcopy, xwait = ring((qrow, grow), x_send, x_recv, xdev, x, NX)
    zlast = NZ // 2 - 1

    def zstart(h, t):
        arrived(h, t)
        for direction in range(2):
            zcopy(h, direction, 0, t)

    def xstart(h):
        arrived_grad(h)
        for direction in range(2):
            xcopy(h, direction, 0, 1)
        arrived(h, 2)
        for direction in range(2):
            xcopy(h, direction, 0, 0)

    def zstep(h, step, tensors=(0, 1)):
        for t in tensors:
            for direction in range(2):
                zwait(h, direction, step, t)
                if step + 1 < zlast or direction == t:
                    zcopy(h, direction, step + 1, t)

    def xstep(h):
        for t in (1, 0):
            for direction in range(2):
                xwait(h, direction, 0, t)
                if direction == t:
                    xcopy(h, direction, 1, t)

    def zend(h):
        for t in range(2):
            zwait(h, t, zlast, t)

    def xend(h):
        for t in range(2):
            xwait(h, t, 1, t)

    edge = (x == 0) | (x == NX - 1)
    wide_at = jnp.where(x == 0, 0, COL - 1)
    left_q = 2 * ((x + jnp.where(z == 0, 1, 0)) % NX)
    right_q = 2 * ((x + jnp.where(z == NZ - 1, NX - 1, 0)) % NX) + 1
    left_k = (2 * z + COL - 1) % COL
    right_k = (2 * z + 2) % COL

    def plan(h):
        owners = []
        for i in range(ROW):
            for r in range(RAND):
                j = rb_ref[r, 2 * c + h, COL * (i // 2) + 2 * z + i % 2] - COL * x
                owners.append(jnp.where((j >= 0) & (j < COL), j, -1))
        owners += [left_k, right_k, jnp.where(edge, wide_at, -1)]
        for e in range(ENTRIES):
            prev = jnp.int32(-1)
            for f in range(e):
                prev = jnp.where(owners[f] == owners[e], f, prev)
            owner_s[h * ENTRIES + e] = owners[e]
            prev_s[h * ENTRIES + e] = prev
        for j in range(COL):
            last = jnp.int32(-1)
            for e in range(ENTRIES):
                last = jnp.where(owners[e] == j, e, last)
            last_s[h * COL + j] = last

    def listed(h, e):
        j = owner_s[h * ENTRIES + e]
        return jnp.maximum(j, 0), jnp.where(j < 0, NEG, 0.0)

    wide_bias = jnp.where(edge, 0.0, NEG)

    def stack(tiles):
        return tiles[0] if len(tiles) == 1 else jnp.concatenate(tiles, axis=0)

    def pieces(value, count):
        size = value.shape[0] // count
        return [value[n * size:(n + 1) * size] for n in range(count)]

    def score(ks, q):
        scores = pieces(dot(stack([k for k, _ in ks]), q, NT), len(ks))
        return [sc * SCALE if bias is None else sc * SCALE + bias for sc, (_, bias) in zip(scores, ks)]

    def measure(ks, vs, q, g, keep=None):
        scores = score(ks, q)
        peak = scores[0]
        for sc in scores[1:]:
            peak = jnp.maximum(peak, sc)
        peak = jnp.max(peak, axis=0, keepdims=True)
        total = weighted = None
        for n, (sc, dp) in enumerate(zip(scores, pieces(dot(stack(vs), g, NT), len(vs)))):
            e = jnp.exp(sc - peak)
            if keep is not None:
                h, i = keep
                kept_e[h, i, n] = e
                kept_p[h, i, n] = dp
            w = e * dp
            total = e if total is None else total + e
            weighted = w if weighted is None else weighted + w
        return peak, jnp.sum(total, axis=0, keepdims=True), jnp.sum(weighted, axis=0, keepdims=True)

    def window(h):
        mine = pl.ds(2 * z, 2)
        here = pl.ds(2 * x, 2)
        return tuple(ref[h][at_, :, :].reshape(2 * BLK, HD)
                     for ref, at_ in ((kall, mine), (vall, mine), (qrow, here), (grow, here)))

    def tiles_of(h, i):
        ks, vs = [], []
        for r in range(RAND):
            j, bias = listed(h, RAND * i + r)
            ks.append((kall[h][j], bias))
            vs.append(vall[h][j])
        ks.append((kall[h][wide_at], wide_bias))
        vs.append(vall[h][wide_at])
        return ks, vs

    def count_units(h, units):
        for i in units:
            ks, vs = tiles_of(h, i)
            for n, row in enumerate(measure(ks, vs, qrow[h][i], grow[h][i], (h, i))):
                sets[h, 0, n, i:i + 1, :] = row

    def count_rest(h):
        for part in range(1, 4):
            sets[h, part, 0] = jnp.full((ROW, HD), NEG, F32)
            sets[h, part, 1] = jnp.zeros((ROW, HD), F32)
            sets[h, part, 2] = jnp.zeros((ROW, HD), F32)
        k, v, q, g = window(h)
        for n, row in enumerate(measure([(k, None)], [v], q, g)):
            sets[h, 1, n, pl.ds(2 * x, 1), :] = row[:, :HD]
            sets[h, 1, n, pl.ds(2 * x + 1, 1), :] = row[:, HD:]
        for part, qi, kj in ((2, left_q, left_k), (3, right_q, right_k)):
            for n, row in enumerate(measure([(kall[h][kj], None)], [vall[h][kj]], qrow[h][qi], grow[h][qi])):
                sets[h, part, n, pl.ds(qi, 1), :] = row

    def merge(parts):
        peak = jnp.maximum(jnp.maximum(parts[0][0], parts[1][0]), jnp.maximum(parts[2][0], parts[3][0]))
        shift = [jnp.exp(p[0] - peak) for p in parts]
        total = sum(p[1] * f for p, f in zip(parts, shift))
        return peak, total, sum(p[2] * f for p, f in zip(parts, shift))

    def send_stats(h):
        for n, value in enumerate(merge([[sets[h, part, n] for n in range(3)] for part in range(4)])):
            stats[h, x, n] = value
        for d in range(1, NX):
            go_on(remote(stats.at[h, x], stats.at[h, x], s_send.at[h, d], s_recv.at[h, d], xall[d - 1]))

    def take_stats(h):
        for d in range(1, NX):
            src = (x + NX - d) % NX
            remote(stats.at[h, src], stats.at[h, src], s_send.at[h, d], s_recv.at[h, d], xall[d - 1]).wait_recv()
        peak, total, weighted = merge([[stats[h, i, n] for n in range(3)] for i in range(NX)])
        inverse = 1.0 / total
        rows[h, 0] = peak
        rows[h, 1] = inverse
        rows[h, 2] = weighted * inverse

    def weigh(ks, vs, q, g, row):
        peak, inverse, delta = row
        wb, ds = [], []
        for sc, dp in zip(score(ks, q), pieces(dot(stack(vs), g, NT), len(vs))):
            w = jnp.exp(sc - peak) * inverse
            wb.append(w.astype(BF16))
            ds.append((w * (dp - delta)).astype(BF16))
        return spread(wb, ds, ks, vs, q, g)

    def spread(wb, ds, ks, vs, q, g):
        wb, ds = stack(wb), stack(ds)
        k, v = stack([k for k, _ in ks]), stack(vs)
        return dot(ds, q, NN), dot(wb, g, NN), dot(wb, v, TN), dot(ds, k, TN)

    def reweigh(h, i, ks, vs, q, g):
        peak, inverse, delta = row_of(h, i)
        factor = jnp.exp(sets[h, 0, 0, i:i + 1, :] - peak) * inverse
        wb, ds = [], []
        for n in range(len(ks)):
            w = kept_e[h, i, n] * factor
            wb.append(w.astype(BF16))
            ds.append((w * (kept_p[h, i, n] - delta)).astype(BF16))
        return spread(wb, ds, ks, vs, q, g)

    def row_of(h, i):
        return [rows[h, n, pl.ds(i, 1), :] for n in range(3)]

    def store_entry(h, e, dk, dv):
        prev = prev_s[h * ENTRIES + e]
        back = jnp.maximum(prev, 0)
        acc[h, 0, e] = dk + jnp.where(prev < 0, 0.0, acc[h, 0, back])
        acc[h, 1, e] = dv + jnp.where(prev < 0, 0.0, acc[h, 1, back])

    def grad_units(h, units):
        for i in units:
            ks, vs = tiles_of(h, i)
            dks, dvs, o, dq = reweigh(h, i, ks, vs, qrow[h][i], grow[h][i])
            for r, (dk, dv) in enumerate(zip(pieces(dks, len(ks)), pieces(dvs, len(vs)))):
                if r < RAND:
                    store_entry(h, RAND * i + r, dk, dv)
                elif i == 0:
                    wide_acc[h, 0] = dk
                    wide_acc[h, 1] = dv
                else:
                    wide_acc[h, 0] += dk
                    wide_acc[h, 1] += dv
            o_acc[h, i] = o
            dq_acc[h, i] = dq

    def grad_rim(h):
        for e, qi, kj in ((LEFT, left_q, left_k), (RIGHT, right_q, right_k)):
            dk, dv, o, dq = weigh([(kall[h][kj], None)], [vall[h][kj]], qrow[h][qi], grow[h][qi], row_of(h, qi))
            store_entry(h, e, dk, dv)
            o_acc[h, qi] += o
            dq_acc[h, qi] += dq
        store_entry(h, WIDE, wide_acc[h, 0], wide_acc[h, 1])

    def grad_own(h):
        k, v, q, g = window(h)
        row = [jnp.concatenate([a, b], axis=1) for a, b in zip(row_of(h, 2 * x), row_of(h, 2 * x + 1))]
        dk, dv, o, dq = weigh([(k, None)], [v], q, g, row)
        own_acc[h, 0] = dk.reshape(2, BLK, HD)
        own_acc[h, 1] = dv.reshape(2, BLK, HD)
        here = pl.ds(2 * x, 2)
        o_acc[h, here] += o.reshape(2, BLK, HD)
        dq_acc[h, here] += dq.reshape(2, BLK, HD)

    def key_part(h, t, target):
        def one(b):
            last = last_s[h * COL + 2 * target + b]
            value = acc[h, t, jnp.maximum(last, 0)]
            value = jnp.where(last < 0, 0.0, value)
            return value * SCALE if t == 0 else value
        return one

    def query_part(h, t, target):
        def one(b):
            value = (o_acc, dq_acc)[t][h, 2 * target + b]
            return value * SCALE if t == 1 else value
        return one

    def summing(part, arrive, summed, send, recv, devs, last, last_send, last_recv, cores, pos, count):
        steps = count // 2

        def wait(h, direction, step, t, b):
            ref = arrive.at[h, direction, step, t, b]
            remote(ref, ref, send.at[h, direction, step, t, b], recv.at[h, direction, step, t, b],
                   devs[direction]).wait_recv()
            return ref

        def go(h, direction, step, t):
            away = steps - step
            target = (pos + away) % count if direction == 0 else (pos + count - away) % count
            mine = part(h, t, target)
            for b in range(2):
                value = mine(b)
                if step != (0 if t == direction else 1):
                    value = value + wait(h, direction, step - 1, t, b)[...].astype(F32)
                src = summed.at[h, direction, step, t, b]
                src[...] = value.astype(BF16)
                if step == steps - 1:
                    go_on(remote(src, last.at[h, t, c, direction], last_send.at[h, direction, t, b],
                                 last_recv.at[h, direction, t, c], cores[direction][b]))
                else:
                    go_on(remote(src, arrive.at[h, direction, step, t, b], send.at[h, direction, step, t, b],
                                 recv.at[h, direction, step, t, b], devs[direction]))

        def begin(h):
            for direction in range(2):
                go(h, direction, 0, direction)
            for direction in range(2):
                go(h, direction, 1, 1 - direction)

        def step_on(h, step):
            for t in (1, 0):
                for direction in range(2):
                    if not (step == 1 and t != direction):
                        go(h, direction, step, t)

        def ended(h, t, core):
            total = None
            for direction in range(2):
                ref = last.at[h, t, core, direction]
                remote(ref, ref, last_send.at[h, direction, t, 0], last_recv.at[h, direction, t, core],
                       partner).wait_recv()
                total = ref[...].astype(F32) if total is None else total + ref[...].astype(F32)
            return total

        return begin, step_on, ended

    zbegin, zsum_on, zended = summing(key_part, zin, zsum, rz_send, rz_recv, zdev, zfin, lz_send, lz_recv, zcores, z, NZ)
    xbegin, xsum_on, xended = summing(query_part, xin, xsum, rx_send, rx_recv, xdev, xfin, lx_send, lx_recv, xcores, x, NX)
    outs = (o_out, dq_out, dk_out, dv_out)

    def own_part(h, n, b):
        if n < 2:
            return query_part(h, n, x)(b)
        value = own_acc[h, n - 2, b]
        return key_part(h, n - 2, z)(b) + (value * SCALE if n == 2 else value)

    def give(h, ns):
        for n in ns:
            final[h, n] = own_part(h, n, 1 - c).astype(BF16)
            go_on(remote(final.at[h, n], gift.at[h, n], f_send.at[h, n], f_recv.at[h, n], partner))

    def finish(h, ns):
        for n in ns:
            ended = xended if n < 2 else zended
            mine = own_part(h, n, c) + ended(h, n % 2, c)
            outs[n][:, lanes_of(2 * c + h)] = mine.astype(BF16)
            remote(gift.at[h, n], gift.at[h, n], f_send.at[h, n], f_recv.at[h, n], partner).wait_recv()
            theirs = gift[h, n].astype(F32) + ended(h, n % 2, 1 - c)
            outs[n][:, lanes_of(2 * (1 - c) + h)] = theirs.astype(BF16)

    exchange(0, 0)
    exchange(0, 1)
    exchange(1, 0)
    zstart(0, 0)
    exchange(1, 1)
    zstart(0, 1)
    exchange_grad(0)
    exchange(0, 2)
    zstart(1, 0)
    exchange_grad(1)
    exchange(1, 2)
    zstep(0, 0)
    zstart(1, 1)
    xstart(0)
    lists.wait()
    plan(0)
    zstep(0, 1)
    zstep(1, 0, (0,))
    xstart(1)
    xstep(0)
    zstep(0, 2)
    zstep(1, 0, (1,))
    plan(1)
    xend(0)
    zend(0)
    pairs = [(i, i + 1) for i in range(0, ROW, 2)]
    count_units(0, pairs[0])
    count_units(0, pairs[1])
    zstep(1, 1)
    count_units(0, pairs[2])
    count_units(0, pairs[3])
    count_rest(0)
    send_stats(0)
    xstep(1)
    zstep(1, 2)
    take_stats(0)
    grad_units(0, pairs[0])
    xend(1)
    grad_units(0, pairs[1])
    grad_units(0, pairs[2])
    zend(1)
    for units in pairs:
        count_units(1, units)
    count_rest(1)
    send_stats(1)
    grad_units(0, pairs[3])
    grad_rim(0)
    zbegin(0)
    xbegin(0)
    grad_own(0)
    give(0, range(4))
    take_stats(1)
    grad_units(1, pairs[0])
    zsum_on(0, 1)
    xsum_on(0, 1)
    grad_units(1, pairs[1])
    grad_units(1, pairs[2])
    zsum_on(0, 2)
    grad_units(1, pairs[3])
    grad_rim(1)
    zbegin(1)
    xbegin(1)
    zsum_on(0, 3)
    grad_own(1)
    give(1, range(4))
    zsum_on(1, 1)
    xsum_on(1, 1)
    finish(0, (0, 1))
    zsum_on(1, 2)
    finish(0, (2, 3))
    finish(1, (0, 1))
    zsum_on(1, 3)
    finish(1, (3, 2))
    for cp in sends:
        cp.wait_send()


def place_kernel(*refs):
    for n in range(4):
        refs[4 + n][...] = refs[n][...]


def vmem():
    return pl.BlockSpec(memory_space=pltpu.VMEM)


def smem():
    return pl.BlockSpec(memory_space=pltpu.SMEM)


def on_device(query_rows, key_rows, value_rows, out_grad, random_blocks):
    dma = pltpu.SemaphoreType.DMA
    mem = pltpu.VMEM
    tile = (BLK, HD)
    full = jax.ShapeDtypeStruct((BLK, 4 * HD), BF16)
    zs, xs = NZ // 2, NX // 2
    outs = pl.pallas_call(
        attention_kernel,
        out_shape=(full,) * 4,
        in_specs=[pl.BlockSpec(memory_space=pltpu.HBM)] * 5,
        out_specs=[vmem()] * 4,
        scratch_shapes=[
            *[mem((COL,) + tile, BF16)] * 4, *[mem((ROW,) + tile, BF16)] * 4,
            mem((2, 4, 3, ROW, HD), F32), mem((2, NX, 3, ROW, HD), F32), mem((2, 3, ROW, HD), F32),
            mem((2, 2, ENTRIES) + tile, F32), mem((2, 2) + tile, F32), mem((2, 2, 2) + tile, F32),
            mem((2, ROW) + tile, F32), mem((2, ROW) + tile, F32),
            mem((2, 2, zs, 2, 2) + tile, BF16), mem((2, 2, zs, 2, 2) + tile, BF16),
            mem((2, 2, xs, 2, 2) + tile, BF16), mem((2, 2, xs, 2, 2) + tile, BF16),
            mem((2, 2, 2, 2) + tile, BF16), mem((2, 2, 2, 2) + tile, BF16),
            mem((2, 4) + tile, BF16), mem((2, 4) + tile, BF16),
            mem((2, ROW, RAND + 1) + tile, F32), mem((2, ROW, RAND + 1) + tile, F32),
            pltpu.SMEM((RAND, 4, NX * COL), jnp.int32),
            pltpu.SMEM((2 * ENTRIES,), jnp.int32), pltpu.SMEM((2 * ENTRIES,), jnp.int32), pltpu.SMEM((2 * COL,), jnp.int32), dma,
            dma((2, 3, 2 * NY)), dma((2, 3, 2 * NY)), dma((2, 3)), dma((2,)), dma((2,)), dma((2,)),
            dma((2, 2, zs, 2)), dma((2, 2, zs, 2)), dma((2, 2, xs, 2)), dma((2, 2, xs, 2)),
            dma((2, NX)), dma((2, NX)),
            dma((2, 2, zs, 2, 2)), dma((2, 2, zs, 2, 2)), dma((2, 2, xs, 2, 2)), dma((2, 2, xs, 2, 2)),
            dma((2, 2, 2, 2)), dma((2, 2, 2, 2)), dma((2, 2, 2, 2)), dma((2, 2, 2, 2)),
            dma((2, 4)), dma((2, 4)),
        ],
        compiler_params=pltpu.CompilerParams(collective_id=0, has_side_effects=True, vmem_limit_bytes=VMEM_LIMIT),
        name="attention",
    )(*(pltpu.with_memory_space_constraint(a, pltpu.HBM)
        for a in (random_blocks.transpose(2, 0, 1), query_rows, key_rows, value_rows, out_grad)))
    return pl.pallas_call(
        place_kernel,
        out_shape=(full,) * 4,
        in_specs=[vmem()] * 4,
        out_specs=[vmem()] * 4,
        compiler_params=pltpu.CompilerParams(vmem_limit_bytes=4 << 20),
        name="place",
    )(*outs)


def solution(mesh):
    in_specs = (
        P(("seq", "head"), None),
        P(("seq", "head"), None),
        P(("seq", "head"), None),
        P("seq", "head"),
        P("head", None, None),
    )
    out_specs = (P("seq", "head"),) * 4
    return jax.shard_map(
        on_device, mesh=mesh, in_specs=in_specs, out_specs=out_specs, check_vma=False
    )
```

```python
import math

import jax
import jax.numpy as jnp
from jax import lax
from jax.experimental import pallas as pl
from jax.experimental.pallas import tpu as pltpu
from jax.sharding import PartitionSpec as P

HD = 128
BLK = 128
NX = 4
NZ = 8
NY = 4
COL = 2 * NZ
ROW = 2 * NX
RAND = 3
LEFT = RAND * ROW
RIGHT = LEFT + 1
WIDE = LEFT + 2
ENTRIES = LEFT + 3
SCALE = 1.0 / math.sqrt(HD)
NEG = -1e30
VMEM_LIMIT = 44 << 20
MESH = pl.DeviceIdType.MESH
NT = (((1,), (1,)), ((), ()))
NN = (((1,), (0,)), ((), ()))
TN = (((0,), (0,)), ((), ()))
F32 = jnp.float32
BF16 = jnp.bfloat16


def dot(a, b, dims):
    return lax.dot_general(a, b, dims, preferred_element_type=F32)


def place_of(x, z, c):
    return (x * NZ + z) * 2 + c


def remote(src, dst, send_sem, recv_sem, dev):
    return pltpu.make_async_remote_copy(
        src_ref=src, dst_ref=dst, send_sem=send_sem, recv_sem=recv_sem,
        device_id=dev, device_id_type=MESH,
    )


def meet(devs):
    barrier = pltpu.get_barrier_semaphore()
    for dev in devs:
        pl.semaphore_signal(barrier, inc=1, device_id=dev, device_id_type=MESH)
    pl.semaphore_wait(barrier, len(devs))


def attention_kernel(rb_in, q_ref, k_ref, v_ref, g_ref, o_out, dq_out, dk_out, dv_out,
                     kall0, kall1, vall0, vall1, qrow0, qrow1, grow0, grow1, sets, stats, rows, acc, wide_acc, own_acc, o_acc, dq_acc,
                     zin, zsum, xin, xsum, zfin, xfin, final, gift, kept_e, kept_p, rb_ref, owner_s, prev_s, last_s, rb_sem,
                     a_send, a_recv, a_own, g_send, g_recv, g_own, z_send, z_recv, x_send, x_recv, s_send, s_recv,
                     rz_send, rz_recv, rx_send, rx_recv, lz_send, lz_recv, lx_send, lx_recv, f_send, f_recv):
    s = lax.axis_index("seq")
    y = lax.axis_index("head")
    x = s // (2 * NZ)
    z = (s // 2) % NZ
    c = s % 2
    me = y * 2 + c
    kall, vall, qrow, grow = (kall0, kall1), (vall0, vall1), (qrow0, qrow1), (grow0, grow1)

    def member(d):
        other = (me + d) % (2 * NY)
        return other % 2, other // 2

    def at(xx, zz):
        return (place_of(xx, zz, c), y)

    group = []
    for d in range(1, 2 * NY):
        cc, yy = member(d)
        group.append((place_of(x, z, cc), yy))
    zdev = (at(x, (z + 1) % NZ), at(x, (z + NZ - 1) % NZ))
    xall = [at((x + d) % NX, z) for d in range(1, NX)]
    xdev = (xall[0], xall[NX - 2])
    partner = (place_of(x, z, 1 - c), y)

    def either(xx, zz):
        return [(place_of(xx, zz, b), y) for b in range(2)]

    def across(xx, zz):
        return (place_of(xx, zz, 1 - c), y)

    zcores = (either(x, (z + 1) % NZ), either(x, (z + NZ - 1) % NZ))
    xcores = (either((x + 1) % NX, z), either((x + NX - 1) % NX, z))
    meet(group + list(zdev) + xall + [across(x, (z + 1) % NZ), across(x, (z + NZ - 1) % NZ),
                                      across((x + 1) % NX, z), across((x + NX - 1) % NX, z)])

    lists = pltpu.make_async_copy(rb_in, rb_ref, rb_sem)
    lists.start()
    sends = []

    def go_on(cp):
        cp.start()
        sends.append(cp)

    def lanes_of(n):
        return pl.ds(pl.multiple_of(n * HD, HD), HD)

    ins = (k_ref, v_ref, q_ref)
    bufs = (kall, vall, qrow)
    slot = (2 * z, 2 * z, 2 * x)
    own = {}

    def exchange(h, t):
        dst = bufs[t][h].at[slot[t] + c, pl.ds(pl.multiple_of(y * 32, 32), 32), :]
        for d in range(1, 2 * NY):
            cc, yy = member(d)
            go_on(remote(ins[t].at[:, lanes_of(yy * 4 + cc * 2 + h)], dst, a_send.at[h, t, d], a_recv.at[h, t, d],
                         group[d - 1]))
        own[h, t] = pltpu.make_async_copy(ins[t].at[:, lanes_of(me * 2 + h)], dst, a_own.at[h, t])
        own[h, t].start()

    def exchange_grad(h):
        go_on(remote(g_ref.at[:, lanes_of(2 * (1 - c) + h)], grow[h].at[2 * x + c], g_send.at[h], g_recv.at[h], partner))
        own[h, 3] = pltpu.make_async_copy(g_ref.at[:, lanes_of(2 * c + h)], grow[h].at[2 * x + c], g_own.at[h])
        own[h, 3].start()

    def arrived(h, t):
        own[h, t].wait()
        for d in range(1, 2 * NY):
            other = (me + 2 * NY - d) % (2 * NY)
            cs, ys = other % 2, other // 2
            dst = bufs[t][h].at[slot[t] + cs, pl.ds(pl.multiple_of(ys * 32, 32), 32), :]
            remote(dst, dst, a_send.at[h, t, d], a_recv.at[h, t, d], partner).wait_recv()

    def arrived_grad(h):
        own[h, 3].wait()
        dst = grow[h].at[2 * x + 1 - c]
        remote(dst, dst, g_send.at[h], g_recv.at[h], partner).wait_recv()

    def ring(bufs2, send, recv, devs, pos, count):
        def piece(h, t, owner):
            return bufs2[t][h].at[pl.ds(2 * owner, 2)]

        def copy(h, direction, step, t):
            owner = (pos + count - step) % count if direction == 0 else (pos + step) % count
            ref = piece(h, t, owner)
            go_on(remote(ref, ref, send.at[h, direction, step, t], recv.at[h, direction, step, t], devs[direction]))

        def wait(h, direction, step, t):
            owner = (pos + count - 1 - step) % count if direction == 0 else (pos + 1 + step) % count
            ref = piece(h, t, owner)
            remote(ref, ref, send.at[h, direction, step, t], recv.at[h, direction, step, t],
                   devs[direction]).wait_recv()

        return copy, wait

    zcopy, zwait = ring((kall, vall), z_send, z_recv, zdev, z, NZ)
    xcopy, xwait = ring((qrow, grow), x_send, x_recv, xdev, x, NX)
    zlast = NZ // 2 - 1

    def zstart(h, t):
        arrived(h, t)
        for direction in range(2):
            zcopy(h, direction, 0, t)

    def xstart(h):
        arrived_grad(h)
        for direction in range(2):
            xcopy(h, direction, 0, 1)
        arrived(h, 2)
        for direction in range(2):
            xcopy(h, direction, 0, 0)

    def zstep(h, step, tensors=(0, 1)):
        for t in tensors:
            for direction in range(2):
                zwait(h, direction, step, t)
                if step + 1 < zlast or direction == t:
                    zcopy(h, direction, step + 1, t)

    def xstep(h):
        for t in (1, 0):
            for direction in range(2):
                xwait(h, direction, 0, t)
                if direction == t:
                    xcopy(h, direction, 1, t)

    def zend(h):
        for t in range(2):
            zwait(h, t, zlast, t)

    def xend(h):
        for t in range(2):
            xwait(h, t, 1, t)

    edge = (x == 0) | (x == NX - 1)
    wide_at = jnp.where(x == 0, 0, COL - 1)
    left_q = 2 * ((x + jnp.where(z == 0, 1, 0)) % NX)
    right_q = 2 * ((x + jnp.where(z == NZ - 1, NX - 1, 0)) % NX) + 1
    left_k = (2 * z + COL - 1) % COL
    right_k = (2 * z + 2) % COL

    def plan(h):
        owners = []
        for i in range(ROW):
            for r in range(RAND):
                j = rb_ref[r, 2 * c + h, COL * (i // 2) + 2 * z + i % 2] - COL * x
                owners.append(jnp.where((j >= 0) & (j < COL), j, -1))
        owners += [left_k, right_k, jnp.where(edge, wide_at, -1)]
        for e in range(ENTRIES):
            prev = jnp.int32(-1)
            for f in range(e):
                prev = jnp.where(owners[f] == owners[e], f, prev)
            owner_s[h * ENTRIES + e] = owners[e]
            prev_s[h * ENTRIES + e] = prev
        for j in range(COL):
            last = jnp.int32(-1)
            for e in range(ENTRIES):
                last = jnp.where(owners[e] == j, e, last)
            last_s[h * COL + j] = last

    def listed(h, e):
        j = owner_s[h * ENTRIES + e]
        return jnp.maximum(j, 0), jnp.where(j < 0, NEG, 0.0)

    wide_bias = jnp.where(edge, 0.0, NEG)

    def stack(tiles):
        return tiles[0] if len(tiles) == 1 else jnp.concatenate(tiles, axis=0)

    def pieces(value, count):
        size = value.shape[0] // count
        return [value[n * size:(n + 1) * size] for n in range(count)]

    def score(ks, q):
        scores = pieces(dot(stack([k for k, _ in ks]), q, NT), len(ks))
        return [sc * SCALE if bias is None else sc * SCALE + bias for sc, (_, bias) in zip(scores, ks)]

    def measure(ks, vs, q, g, keep=None):
        scores = score(ks, q)
        peak = scores[0]
        for sc in scores[1:]:
            peak = jnp.maximum(peak, sc)
        peak = jnp.max(peak, axis=0, keepdims=True)
        total = weighted = None
        for n, (sc, dp) in enumerate(zip(scores, pieces(dot(stack(vs), g, NT), len(vs)))):
            e = jnp.exp(sc - peak)
            if keep is not None:
                h, i = keep
                kept_e[h, i, n] = e
                kept_p[h, i, n] = dp
            w = e * dp
            total = e if total is None else total + e
            weighted = w if weighted is None else weighted + w
        return peak, jnp.sum(total, axis=0, keepdims=True), jnp.sum(weighted, axis=0, keepdims=True)

    def window(h):
        mine = pl.ds(2 * z, 2)
        here = pl.ds(2 * x, 2)
        return tuple(ref[h][at_, :, :].reshape(2 * BLK, HD)
                     for ref, at_ in ((kall, mine), (vall, mine), (qrow, here), (grow, here)))

    def tiles_of(h, i):
        ks, vs = [], []
        for r in range(RAND):
            j, bias = listed(h, RAND * i + r)
            ks.append((kall[h][j], bias))
            vs.append(vall[h][j])
        ks.append((kall[h][wide_at], wide_bias))
        vs.append(vall[h][wide_at])
        return ks, vs

    def count_units(h, units):
        for i in units:
            ks, vs = tiles_of(h, i)
            for n, row in enumerate(measure(ks, vs, qrow[h][i], grow[h][i], (h, i))):
                sets[h, 0, n, i:i + 1, :] = row

    def count_rest(h):
        for part in range(1, 4):
            sets[h, part, 0] = jnp.full((ROW, HD), NEG, F32)
            sets[h, part, 1] = jnp.zeros((ROW, HD), F32)
            sets[h, part, 2] = jnp.zeros((ROW, HD), F32)
        k, v, q, g = window(h)
        for n, row in enumerate(measure([(k, None)], [v], q, g)):
            sets[h, 1, n, pl.ds(2 * x, 1), :] = row[:, :HD]
            sets[h, 1, n, pl.ds(2 * x + 1, 1), :] = row[:, HD:]
        for part, qi, kj in ((2, left_q, left_k), (3, right_q, right_k)):
            for n, row in enumerate(measure([(kall[h][kj], None)], [vall[h][kj]], qrow[h][qi], grow[h][qi])):
                sets[h, part, n, pl.ds(qi, 1), :] = row

    def merge(parts):
        peak = jnp.maximum(jnp.maximum(parts[0][0], parts[1][0]), jnp.maximum(parts[2][0], parts[3][0]))
        shift = [jnp.exp(p[0] - peak) for p in parts]
        total = sum(p[1] * f for p, f in zip(parts, shift))
        return peak, total, sum(p[2] * f for p, f in zip(parts, shift))

    def send_stats(h):
        for n, value in enumerate(merge([[sets[h, part, n] for n in range(3)] for part in range(4)])):
            stats[h, x, n] = value
        for d in range(1, NX):
            go_on(remote(stats.at[h, x], stats.at[h, x], s_send.at[h, d], s_recv.at[h, d], xall[d - 1]))

    def take_stats(h):
        for d in range(1, NX):
            src = (x + NX - d) % NX
            remote(stats.at[h, src], stats.at[h, src], s_send.at[h, d], s_recv.at[h, d], xall[d - 1]).wait_recv()
        peak, total, weighted = merge([[stats[h, i, n] for n in range(3)] for i in range(NX)])
        inverse = 1.0 / total
        rows[h, 0] = peak
        rows[h, 1] = inverse
        rows[h, 2] = weighted * inverse

    def weigh(ks, vs, q, g, row):
        peak, inverse, delta = row
        wb, ds = [], []
        for sc, dp in zip(score(ks, q), pieces(dot(stack(vs), g, NT), len(vs))):
            w = jnp.exp(sc - peak) * inverse
            wb.append(w.astype(BF16))
            ds.append((w * (dp - delta)).astype(BF16))
        return spread(wb, ds, ks, vs, q, g)

    def spread(wb, ds, ks, vs, q, g):
        wb, ds = stack(wb), stack(ds)
        k, v = stack([k for k, _ in ks]), stack(vs)
        return dot(ds, q, NN), dot(wb, g, NN), dot(wb, v, TN), dot(ds, k, TN)

    def reweigh(h, i, ks, vs, q, g):
        peak, inverse, delta = row_of(h, i)
        factor = jnp.exp(sets[h, 0, 0, i:i + 1, :] - peak) * inverse
        wb, ds = [], []
        for n in range(len(ks)):
            w = kept_e[h, i, n] * factor
            wb.append(w.astype(BF16))
            ds.append((w * (kept_p[h, i, n] - delta)).astype(BF16))
        return spread(wb, ds, ks, vs, q, g)

    def row_of(h, i):
        return [rows[h, n, pl.ds(i, 1), :] for n in range(3)]

    def store_entry(h, e, dk, dv):
        prev = prev_s[h * ENTRIES + e]
        back = jnp.maximum(prev, 0)
        acc[h, 0, e] = dk + jnp.where(prev < 0, 0.0, acc[h, 0, back])
        acc[h, 1, e] = dv + jnp.where(prev < 0, 0.0, acc[h, 1, back])

    def grad_units(h, units):
        for i in units:
            ks, vs = tiles_of(h, i)
            dks, dvs, o, dq = reweigh(h, i, ks, vs, qrow[h][i], grow[h][i])
            for r, (dk, dv) in enumerate(zip(pieces(dks, len(ks)), pieces(dvs, len(vs)))):
                if r < RAND:
                    store_entry(h, RAND * i + r, dk, dv)
                elif i == 0:
                    wide_acc[h, 0] = dk
                    wide_acc[h, 1] = dv
                else:
                    wide_acc[h, 0] += dk
                    wide_acc[h, 1] += dv
            o_acc[h, i] = o
            dq_acc[h, i] = dq

    def grad_rim(h):
        for e, qi, kj in ((LEFT, left_q, left_k), (RIGHT, right_q, right_k)):
            dk, dv, o, dq = weigh([(kall[h][kj], None)], [vall[h][kj]], qrow[h][qi], grow[h][qi], row_of(h, qi))
            store_entry(h, e, dk, dv)
            o_acc[h, qi] += o
            dq_acc[h, qi] += dq
        store_entry(h, WIDE, wide_acc[h, 0], wide_acc[h, 1])

    def grad_own(h):
        k, v, q, g = window(h)
        row = [jnp.concatenate([a, b], axis=1) for a, b in zip(row_of(h, 2 * x), row_of(h, 2 * x + 1))]
        dk, dv, o, dq = weigh([(k, None)], [v], q, g, row)
        own_acc[h, 0] = dk.reshape(2, BLK, HD)
        own_acc[h, 1] = dv.reshape(2, BLK, HD)
        here = pl.ds(2 * x, 2)
        o_acc[h, here] += o.reshape(2, BLK, HD)
        dq_acc[h, here] += dq.reshape(2, BLK, HD)

    def key_part(h, t, target):
        def one(b):
            last = last_s[h * COL + 2 * target + b]
            value = acc[h, t, jnp.maximum(last, 0)]
            value = jnp.where(last < 0, 0.0, value)
            return value * SCALE if t == 0 else value
        return one

    def query_part(h, t, target):
        def one(b):
            value = (o_acc, dq_acc)[t][h, 2 * target + b]
            return value * SCALE if t == 1 else value
        return one

    def summing(part, arrive, summed, send, recv, devs, last, last_send, last_recv, cores, pos, count):
        steps = count // 2

        def wait(h, direction, step, t, b):
            ref = arrive.at[h, direction, step, t, b]
            remote(ref, ref, send.at[h, direction, step, t, b], recv.at[h, direction, step, t, b],
                   devs[direction]).wait_recv()
            return ref

        def go(h, direction, step, t):
            away = steps - step
            target = (pos + away) % count if direction == 0 else (pos + count - away) % count
            mine = part(h, t, target)
            for b in range(2):
                value = mine(b)
                if step != (0 if t == direction else 1):
                    value = value + wait(h, direction, step - 1, t, b)[...].astype(F32)
                src = summed.at[h, direction, step, t, b]
                src[...] = value.astype(BF16)
                if step == steps - 1:
                    go_on(remote(src, last.at[h, t, c, direction], last_send.at[h, direction, t, b],
                                 last_recv.at[h, direction, t, c], cores[direction][b]))
                else:
                    go_on(remote(src, arrive.at[h, direction, step, t, b], send.at[h, direction, step, t, b],
                                 recv.at[h, direction, step, t, b], devs[direction]))

        def begin(h):
            for direction in range(2):
                go(h, direction, 0, direction)
            for direction in range(2):
                go(h, direction, 1, 1 - direction)

        def step_on(h, step):
            for ahead in (1, 0):
                for direction in range(2):
                    if not (step == 1 and ahead):
                        go(h, direction, step, direction ^ ahead)

        def ended(h, t, core):
            total = None
            for direction in range(2):
                ref = last.at[h, t, core, direction]
                remote(ref, ref, last_send.at[h, direction, t, 0], last_recv.at[h, direction, t, core],
                       partner).wait_recv()
                total = ref[...].astype(F32) if total is None else total + ref[...].astype(F32)
            return total

        return begin, step_on, ended

    zbegin, zsum_on, zended = summing(key_part, zin, zsum, rz_send, rz_recv, zdev, zfin, lz_send, lz_recv, zcores, z, NZ)
    xbegin, xsum_on, xended = summing(query_part, xin, xsum, rx_send, rx_recv, xdev, xfin, lx_send, lx_recv, xcores, x, NX)
    outs = (o_out, dq_out, dk_out, dv_out)

    def own_part(h, n, b):
        if n < 2:
            return query_part(h, n, x)(b)
        value = own_acc[h, n - 2, b]
        return key_part(h, n - 2, z)(b) + (value * SCALE if n == 2 else value)

    def give(h, ns):
        for n in ns:
            final[h, n] = own_part(h, n, 1 - c).astype(BF16)
            go_on(remote(final.at[h, n], gift.at[h, n], f_send.at[h, n], f_recv.at[h, n], partner))

    def finish(h, ns):
        for n in ns:
            ended = xended if n < 2 else zended
            mine = own_part(h, n, c) + ended(h, n % 2, c)
            outs[n][:, lanes_of(2 * c + h)] = mine.astype(BF16)
            remote(gift.at[h, n], gift.at[h, n], f_send.at[h, n], f_recv.at[h, n], partner).wait_recv()
            theirs = gift[h, n].astype(F32) + ended(h, n % 2, 1 - c)
            outs[n][:, lanes_of(2 * (1 - c) + h)] = theirs.astype(BF16)

    exchange(0, 0)
    exchange(0, 1)
    exchange(1, 0)
    zstart(0, 0)
    exchange(1, 1)
    zstart(0, 1)
    exchange_grad(0)
    exchange(0, 2)
    zstart(1, 0)
    exchange_grad(1)
    exchange(1, 2)
    zstep(0, 0)
    zstart(1, 1)
    xstart(0)
    lists.wait()
    plan(0)
    zstep(0, 1)
    zstep(1, 0, (0,))
    xstart(1)
    xstep(0)
    zstep(0, 2)
    zstep(1, 0, (1,))
    plan(1)
    xend(0)
    zend(0)
    pairs = [(i, i + 1) for i in range(0, ROW, 2)]
    count_units(0, pairs[0])
    count_units(0, pairs[1])
    zstep(1, 1)
    count_units(0, pairs[2])
    count_units(0, pairs[3])
    count_rest(0)
    send_stats(0)
    xstep(1)
    zstep(1, 2)
    take_stats(0)
    grad_units(0, pairs[0])
    xend(1)
    grad_units(0, pairs[1])
    grad_units(0, pairs[2])
    zend(1)
    for units in pairs:
        count_units(1, units)
    count_rest(1)
    send_stats(1)
    grad_units(0, pairs[3])
    grad_rim(0)
    zbegin(0)
    xbegin(0)
    grad_own(0)
    give(0, range(4))
    take_stats(1)
    grad_units(1, pairs[0])
    zsum_on(0, 1)
    xsum_on(0, 1)
    grad_units(1, pairs[1])
    grad_units(1, pairs[2])
    zsum_on(0, 2)
    grad_units(1, pairs[3])
    grad_rim(1)
    zbegin(1)
    xbegin(1)
    zsum_on(0, 3)
    grad_own(1)
    give(1, range(4))
    zsum_on(1, 1)
    xsum_on(1, 1)
    finish(0, (0, 1))
    zsum_on(1, 2)
    finish(0, (2, 3))
    finish(1, (0, 1))
    zsum_on(1, 3)
    finish(1, (3, 2))
    for cp in sends:
        cp.wait_send()


def place_kernel(*refs):
    for n in range(4):
        refs[4 + n][...] = refs[n][...]


def vmem():
    return pl.BlockSpec(memory_space=pltpu.VMEM)


def smem():
    return pl.BlockSpec(memory_space=pltpu.SMEM)


def on_device(query_rows, key_rows, value_rows, out_grad, random_blocks):
    dma = pltpu.SemaphoreType.DMA
    mem = pltpu.VMEM
    tile = (BLK, HD)
    full = jax.ShapeDtypeStruct((BLK, 4 * HD), BF16)
    zs, xs = NZ // 2, NX // 2
    outs = pl.pallas_call(
        attention_kernel,
        out_shape=(full,) * 4,
        in_specs=[pl.BlockSpec(memory_space=pltpu.HBM)] * 5,
        out_specs=[vmem()] * 4,
        scratch_shapes=[
            *[mem((COL,) + tile, BF16)] * 4, *[mem((ROW,) + tile, BF16)] * 4,
            mem((2, 4, 3, ROW, HD), F32), mem((2, NX, 3, ROW, HD), F32), mem((2, 3, ROW, HD), F32),
            mem((2, 2, ENTRIES) + tile, F32), mem((2, 2) + tile, F32), mem((2, 2, 2) + tile, F32),
            mem((2, ROW) + tile, F32), mem((2, ROW) + tile, F32),
            mem((2, 2, zs, 2, 2) + tile, BF16), mem((2, 2, zs, 2, 2) + tile, BF16),
            mem((2, 2, xs, 2, 2) + tile, BF16), mem((2, 2, xs, 2, 2) + tile, BF16),
            mem((2, 2, 2, 2) + tile, BF16), mem((2, 2, 2, 2) + tile, BF16),
            mem((2, 4) + tile, BF16), mem((2, 4) + tile, BF16),
            mem((2, ROW, RAND + 1) + tile, F32), mem((2, ROW, RAND + 1) + tile, F32),
            pltpu.SMEM((RAND, 4, NX * COL), jnp.int32),
            pltpu.SMEM((2 * ENTRIES,), jnp.int32), pltpu.SMEM((2 * ENTRIES,), jnp.int32), pltpu.SMEM((2 * COL,), jnp.int32), dma,
            dma((2, 3, 2 * NY)), dma((2, 3, 2 * NY)), dma((2, 3)), dma((2,)), dma((2,)), dma((2,)),
            dma((2, 2, zs, 2)), dma((2, 2, zs, 2)), dma((2, 2, xs, 2)), dma((2, 2, xs, 2)),
            dma((2, NX)), dma((2, NX)),
            dma((2, 2, zs, 2, 2)), dma((2, 2, zs, 2, 2)), dma((2, 2, xs, 2, 2)), dma((2, 2, xs, 2, 2)),
            dma((2, 2, 2, 2)), dma((2, 2, 2, 2)), dma((2, 2, 2, 2)), dma((2, 2, 2, 2)),
            dma((2, 4)), dma((2, 4)),
        ],
        compiler_params=pltpu.CompilerParams(collective_id=0, has_side_effects=True, vmem_limit_bytes=VMEM_LIMIT),
        name="attention",
    )(*(pltpu.with_memory_space_constraint(a, pltpu.HBM)
        for a in (random_blocks.transpose(2, 0, 1), query_rows, key_rows, value_rows, out_grad)))
    return pl.pallas_call(
        place_kernel,
        out_shape=(full,) * 4,
        in_specs=[vmem()] * 4,
        out_specs=[vmem()] * 4,
        compiler_params=pltpu.CompilerParams(vmem_limit_bytes=4 << 20),
        name="place",
    )(*outs)


def solution(mesh):
    in_specs = (
        P(("seq", "head"), None),
        P(("seq", "head"), None),
        P(("seq", "head"), None),
        P("seq", "head"),
        P("head", None, None),
    )
    out_specs = (P("seq", "head"),) * 4
    return jax.shard_map(
        on_device, mesh=mesh, in_specs=in_specs, out_specs=out_specs, check_vma=False
    )
```

```python
import math

import jax
import jax.numpy as jnp
from jax import lax
from jax.experimental import pallas as pl
from jax.experimental.pallas import tpu as pltpu
from jax.sharding import PartitionSpec as P

HD = 128
BLK = 128
NX = 4
NZ = 8
NY = 4
COL = 2 * NZ
ROW = 2 * NX
RAND = 3
LEFT = RAND * ROW
RIGHT = LEFT + 1
WIDE = LEFT + 2
ENTRIES = LEFT + 3
SCALE = 1.0 / math.sqrt(HD)
NEG = -1e30
VMEM_LIMIT = 44 << 20
MESH = pl.DeviceIdType.MESH
NT = (((1,), (1,)), ((), ()))
NN = (((1,), (0,)), ((), ()))
TN = (((0,), (0,)), ((), ()))
F32 = jnp.float32
BF16 = jnp.bfloat16


def dot(a, b, dims):
    return lax.dot_general(a, b, dims, preferred_element_type=F32)


def place_of(x, z, c):
    return (x * NZ + z) * 2 + c


def remote(src, dst, send_sem, recv_sem, dev):
    return pltpu.make_async_remote_copy(
        src_ref=src, dst_ref=dst, send_sem=send_sem, recv_sem=recv_sem,
        device_id=dev, device_id_type=MESH,
    )


def meet(devs):
    barrier = pltpu.get_barrier_semaphore()
    for dev in devs:
        pl.semaphore_signal(barrier, inc=1, device_id=dev, device_id_type=MESH)
    pl.semaphore_wait(barrier, len(devs))


def attention_kernel(rb_in, q_ref, k_ref, v_ref, g_ref, o_out, dq_out, dk_out, dv_out,
                     kall0, kall1, vall0, vall1, qrow0, qrow1, grow0, grow1, sets, stats, rows, acc, wide_acc, own_acc, o_acc, dq_acc,
                     zin, zsum, xin, xsum, zfin, xfin, final, gift, kept_e, kept_p, rb_ref, owner_s, prev_s, last_s, rb_sem,
                     a_send, a_recv, a_own, g_send, g_recv, g_own, z_send, z_recv, x_send, x_recv, s_send, s_recv,
                     rz_send, rz_recv, rx_send, rx_recv, lz_send, lz_recv, lx_send, lx_recv, f_send, f_recv):
    s = lax.axis_index("seq")
    y = lax.axis_index("head")
    x = s // (2 * NZ)
    z = (s // 2) % NZ
    c = s % 2
    me = y * 2 + c
    kall, vall, qrow, grow = (kall0, kall1), (vall0, vall1), (qrow0, qrow1), (grow0, grow1)

    def member(d):
        other = (me + d) % (2 * NY)
        return other % 2, other // 2

    def at(xx, zz):
        return (place_of(xx, zz, c), y)

    group = []
    for d in range(1, 2 * NY):
        cc, yy = member(d)
        group.append((place_of(x, z, cc), yy))
    zdev = (at(x, (z + 1) % NZ), at(x, (z + NZ - 1) % NZ))
    xall = [at((x + d) % NX, z) for d in range(1, NX)]
    xdev = (xall[0], xall[NX - 2])
    partner = (place_of(x, z, 1 - c), y)

    def either(xx, zz):
        return [(place_of(xx, zz, b), y) for b in range(2)]

    def across(xx, zz):
        return (place_of(xx, zz, 1 - c), y)

    zcores = (either(x, (z + 1) % NZ), either(x, (z + NZ - 1) % NZ))
    xcores = (either((x + 1) % NX, z), either((x + NX - 1) % NX, z))
    meet(group + list(zdev) + xall + [across(x, (z + 1) % NZ), across(x, (z + NZ - 1) % NZ),
                                      across((x + 1) % NX, z), across((x + NX - 1) % NX, z)])

    lists = pltpu.make_async_copy(rb_in, rb_ref, rb_sem)
    lists.start()
    sends = []

    def go_on(cp):
        cp.start()
        sends.append(cp)

    def lanes_of(n):
        return pl.ds(pl.multiple_of(n * HD, HD), HD)

    ins = (k_ref, v_ref, q_ref)
    bufs = (kall, vall, qrow)
    slot = (2 * z, 2 * z, 2 * x)
    own = {}

    def exchange(h, t):
        dst = bufs[t][h].at[slot[t] + c, pl.ds(pl.multiple_of(y * 32, 32), 32), :]
        for d in range(1, 2 * NY):
            cc, yy = member(d)
            go_on(remote(ins[t].at[:, lanes_of(yy * 4 + cc * 2 + h)], dst, a_send.at[h, t, d], a_recv.at[h, t, d],
                         group[d - 1]))
        own[h, t] = pltpu.make_async_copy(ins[t].at[:, lanes_of(me * 2 + h)], dst, a_own.at[h, t])
        own[h, t].start()

    def exchange_grad(h):
        go_on(remote(g_ref.at[:, lanes_of(2 * (1 - c) + h)], grow[h].at[2 * x + c], g_send.at[h], g_recv.at[h], partner))
        own[h, 3] = pltpu.make_async_copy(g_ref.at[:, lanes_of(2 * c + h)], grow[h].at[2 * x + c], g_own.at[h])
        own[h, 3].start()

    def arrived(h, t):
        own[h, t].wait()
        for d in range(1, 2 * NY):
            other = (me + 2 * NY - d) % (2 * NY)
            cs, ys = other % 2, other // 2
            dst = bufs[t][h].at[slot[t] + cs, pl.ds(pl.multiple_of(ys * 32, 32), 32), :]
            remote(dst, dst, a_send.at[h, t, d], a_recv.at[h, t, d], partner).wait_recv()

    def arrived_grad(h):
        own[h, 3].wait()
        dst = grow[h].at[2 * x + 1 - c]
        remote(dst, dst, g_send.at[h], g_recv.at[h], partner).wait_recv()

    def ring(bufs2, send, recv, devs, pos, count):
        def piece(h, t, owner):
            return bufs2[t][h].at[pl.ds(2 * owner, 2)]

        def copy(h, direction, step, t):
            owner = (pos + count - step) % count if direction == 0 else (pos + step) % count
            ref = piece(h, t, owner)
            go_on(remote(ref, ref, send.at[h, direction, step, t], recv.at[h, direction, step, t], devs[direction]))

        def wait(h, direction, step, t):
            owner = (pos + count - 1 - step) % count if direction == 0 else (pos + 1 + step) % count
            ref = piece(h, t, owner)
            remote(ref, ref, send.at[h, direction, step, t], recv.at[h, direction, step, t],
                   devs[direction]).wait_recv()

        return copy, wait

    zcopy, zwait = ring((kall, vall), z_send, z_recv, zdev, z, NZ)
    xcopy, xwait = ring((qrow, grow), x_send, x_recv, xdev, x, NX)
    zlast = NZ // 2 - 1

    def zstart(h, t):
        arrived(h, t)
        for direction in range(2):
            zcopy(h, direction, 0, t)

    def xstart(h):
        arrived_grad(h)
        for direction in range(2):
            xcopy(h, direction, 0, 1)
        arrived(h, 2)
        for direction in range(2):
            xcopy(h, direction, 0, 0)

    def zstep(h, step, tensors=(0, 1)):
        for t in tensors:
            for direction in range(2):
                zwait(h, direction, step, t)
                if step + 1 < zlast or direction == t:
                    zcopy(h, direction, step + 1, t)

    def xstep(h):
        for t in (1, 0):
            for direction in range(2):
                xwait(h, direction, 0, t)
                if direction == t:
                    xcopy(h, direction, 1, t)

    def zend(h):
        for t in range(2):
            zwait(h, t, zlast, t)

    def xend(h):
        for t in range(2):
            xwait(h, t, 1, t)

    edge = (x == 0) | (x == NX - 1)
    wide_at = jnp.where(x == 0, 0, COL - 1)
    left_q = 2 * ((x + jnp.where(z == 0, 1, 0)) % NX)
    right_q = 2 * ((x + jnp.where(z == NZ - 1, NX - 1, 0)) % NX) + 1
    left_k = (2 * z + COL - 1) % COL
    right_k = (2 * z + 2) % COL

    def plan(h):
        owners = []
        for i in range(ROW):
            for r in range(RAND):
                j = rb_ref[r, 2 * c + h, COL * (i // 2) + 2 * z + i % 2] - COL * x
                owners.append(jnp.where((j >= 0) & (j < COL), j, -1))
        owners += [left_k, right_k, jnp.where(edge, wide_at, -1)]
        for e in range(ENTRIES):
            prev = jnp.int32(-1)
            for f in range(e):
                prev = jnp.where(owners[f] == owners[e], f, prev)
            owner_s[h * ENTRIES + e] = owners[e]
            prev_s[h * ENTRIES + e] = prev
        for j in range(COL):
            last = jnp.int32(-1)
            for e in range(ENTRIES):
                last = jnp.where(owners[e] == j, e, last)
            last_s[h * COL + j] = last

    def listed(h, e):
        j = owner_s[h * ENTRIES + e]
        return jnp.maximum(j, 0), jnp.where(j < 0, NEG, 0.0)

    wide_bias = jnp.where(edge, 0.0, NEG)

    def stack(tiles):
        return tiles[0] if len(tiles) == 1 else jnp.concatenate(tiles, axis=0)

    def pieces(value, count):
        size = value.shape[0] // count
        return [value[n * size:(n + 1) * size] for n in range(count)]

    def score(ks, q):
        scores = pieces(dot(stack([k for k, _ in ks]), q, NT), len(ks))
        return [sc * SCALE if bias is None else sc * SCALE + bias for sc, (_, bias) in zip(scores, ks)]

    def measure(ks, vs, q, g, keep=None):
        scores = score(ks, q)
        peak = scores[0]
        for sc in scores[1:]:
            peak = jnp.maximum(peak, sc)
        peak = jnp.max(peak, axis=0, keepdims=True)
        total = weighted = None
        for n, (sc, dp) in enumerate(zip(scores, pieces(dot(stack(vs), g, NT), len(vs)))):
            e = jnp.exp(sc - peak)
            if keep is not None:
                h, i = keep
                kept_e[h, i, n] = e
                kept_p[h, i, n] = dp
            w = e * dp
            total = e if total is None else total + e
            weighted = w if weighted is None else weighted + w
        return peak, jnp.sum(total, axis=0, keepdims=True), jnp.sum(weighted, axis=0, keepdims=True)

    def window(h):
        mine = pl.ds(2 * z, 2)
        here = pl.ds(2 * x, 2)
        return tuple(ref[h][at_, :, :].reshape(2 * BLK, HD)
                     for ref, at_ in ((kall, mine), (vall, mine), (qrow, here), (grow, here)))

    def tiles_of(h, i):
        ks, vs = [], []
        for r in range(RAND):
            j, bias = listed(h, RAND * i + r)
            ks.append((kall[h][j], bias))
            vs.append(vall[h][j])
        ks.append((kall[h][wide_at], wide_bias))
        vs.append(vall[h][wide_at])
        return ks, vs

    def count_units(h, units):
        for i in units:
            ks, vs = tiles_of(h, i)
            for n, row in enumerate(measure(ks, vs, qrow[h][i], grow[h][i], (h, i))):
                sets[h, 0, n, i:i + 1, :] = row

    def count_rest(h):
        for part in range(1, 4):
            sets[h, part, 0] = jnp.full((ROW, HD), NEG, F32)
            sets[h, part, 1] = jnp.zeros((ROW, HD), F32)
            sets[h, part, 2] = jnp.zeros((ROW, HD), F32)
        k, v, q, g = window(h)
        for n, row in enumerate(measure([(k, None)], [v], q, g)):
            sets[h, 1, n, pl.ds(2 * x, 1), :] = row[:, :HD]
            sets[h, 1, n, pl.ds(2 * x + 1, 1), :] = row[:, HD:]
        for part, qi, kj in ((2, left_q, left_k), (3, right_q, right_k)):
            for n, row in enumerate(measure([(kall[h][kj], None)], [vall[h][kj]], qrow[h][qi], grow[h][qi])):
                sets[h, part, n, pl.ds(qi, 1), :] = row

    def merge(parts):
        peak = jnp.maximum(jnp.maximum(parts[0][0], parts[1][0]), jnp.maximum(parts[2][0], parts[3][0]))
        shift = [jnp.exp(p[0] - peak) for p in parts]
        total = sum(p[1] * f for p, f in zip(parts, shift))
        return peak, total, sum(p[2] * f for p, f in zip(parts, shift))

    def send_stats(h):
        for n, value in enumerate(merge([[sets[h, part, n] for n in range(3)] for part in range(4)])):
            stats[h, x, n] = value
        for d in range(1, NX):
            go_on(remote(stats.at[h, x], stats.at[h, x], s_send.at[h, d], s_recv.at[h, d], xall[d - 1]))

    def take_stats(h):
        for d in range(1, NX):
            src = (x + NX - d) % NX
            remote(stats.at[h, src], stats.at[h, src], s_send.at[h, d], s_recv.at[h, d], xall[d - 1]).wait_recv()
        peak, total, weighted = merge([[stats[h, i, n] for n in range(3)] for i in range(NX)])
        inverse = 1.0 / total
        rows[h, 0] = peak
        rows[h, 1] = inverse
        rows[h, 2] = weighted * inverse

    def weigh(ks, vs, q, g, row):
        peak, inverse, delta = row
        wb, ds = [], []
        for sc, dp in zip(score(ks, q), pieces(dot(stack(vs), g, NT), len(vs))):
            w = jnp.exp(sc - peak) * inverse
            wb.append(w.astype(BF16))
            ds.append((w * (dp - delta)).astype(BF16))
        return spread(wb, ds, ks, vs, q, g)

    def spread(wb, ds, ks, vs, q, g):
        wb, ds = stack(wb), stack(ds)
        k, v = stack([k for k, _ in ks]), stack(vs)
        return dot(ds, q, NN), dot(wb, g, NN), dot(wb, v, TN), dot(ds, k, TN)

    def reweigh(h, i, ks, vs, q, g):
        peak, inverse, delta = row_of(h, i)
        factor = jnp.exp(sets[h, 0, 0, i:i + 1, :] - peak) * inverse
        wb, ds = [], []
        for n in range(len(ks)):
            w = kept_e[h, i, n] * factor
            wb.append(w.astype(BF16))
            ds.append((w * (kept_p[h, i, n] - delta)).astype(BF16))
        return spread(wb, ds, ks, vs, q, g)

    def row_of(h, i):
        return [rows[h, n, pl.ds(i, 1), :] for n in range(3)]

    def store_entry(h, e, dk, dv):
        prev = prev_s[h * ENTRIES + e]
        back = jnp.maximum(prev, 0)
        acc[h, 0, e] = dk + jnp.where(prev < 0, 0.0, acc[h, 0, back])
        acc[h, 1, e] = dv + jnp.where(prev < 0, 0.0, acc[h, 1, back])

    def grad_units(h, units):
        for i in units:
            ks, vs = tiles_of(h, i)
            dks, dvs, o, dq = reweigh(h, i, ks, vs, qrow[h][i], grow[h][i])
            for r, (dk, dv) in enumerate(zip(pieces(dks, len(ks)), pieces(dvs, len(vs)))):
                if r < RAND:
                    store_entry(h, RAND * i + r, dk, dv)
                elif i == 0:
                    wide_acc[h, 0] = dk
                    wide_acc[h, 1] = dv
                else:
                    wide_acc[h, 0] += dk
                    wide_acc[h, 1] += dv
            o_acc[h, i] = o
            dq_acc[h, i] = dq

    def grad_rim(h):
        for e, qi, kj in ((LEFT, left_q, left_k), (RIGHT, right_q, right_k)):
            dk, dv, o, dq = weigh([(kall[h][kj], None)], [vall[h][kj]], qrow[h][qi], grow[h][qi], row_of(h, qi))
            store_entry(h, e, dk, dv)
            o_acc[h, qi] += o
            dq_acc[h, qi] += dq
        store_entry(h, WIDE, wide_acc[h, 0], wide_acc[h, 1])

    def grad_own(h):
        k, v, q, g = window(h)
        row = [jnp.concatenate([a, b], axis=1) for a, b in zip(row_of(h, 2 * x), row_of(h, 2 * x + 1))]
        dk, dv, o, dq = weigh([(k, None)], [v], q, g, row)
        own_acc[h, 0] = dk.reshape(2, BLK, HD)
        own_acc[h, 1] = dv.reshape(2, BLK, HD)
        here = pl.ds(2 * x, 2)
        o_acc[h, here] += o.reshape(2, BLK, HD)
        dq_acc[h, here] += dq.reshape(2, BLK, HD)

    def key_part(h, t, target):
        def one(b):
            last = last_s[h * COL + 2 * target + b]
            value = acc[h, t, jnp.maximum(last, 0)]
            value = jnp.where(last < 0, 0.0, value)
            return value * SCALE if t == 0 else value
        return one

    def query_part(h, t, target):
        def one(b):
            value = (o_acc, dq_acc)[t][h, 2 * target + b]
            return value * SCALE if t == 1 else value
        return one

    def summing(part, arrive, summed, send, recv, devs, last, last_send, last_recv, cores, pos, count):
        steps = count // 2

        def wait(h, direction, step, t, b):
            ref = arrive.at[h, direction, step, t, b]
            remote(ref, ref, send.at[h, direction, step, t, b], recv.at[h, direction, step, t, b],
                   devs[direction]).wait_recv()
            return ref

        def go(h, direction, step, t):
            away = steps - step
            target = (pos + away) % count if direction == 0 else (pos + count - away) % count
            mine = part(h, t, target)
            for b in range(2):
                value = mine(b)
                if step != (0 if t == direction else 1):
                    value = value + wait(h, direction, step - 1, t, b)[...].astype(F32)
                src = summed.at[h, direction, step, t, b]
                src[...] = value.astype(BF16)
                if step == steps - 1:
                    go_on(remote(src, last.at[h, t, c, direction], last_send.at[h, direction, t, b],
                                 last_recv.at[h, direction, t, c], cores[direction][b]))
                else:
                    go_on(remote(src, arrive.at[h, direction, step, t, b], send.at[h, direction, step, t, b],
                                 recv.at[h, direction, step, t, b], devs[direction]))

        def begin(h):
            for direction in range(2):
                go(h, direction, 0, direction)
            for direction in range(2):
                go(h, direction, 1, 1 - direction)

        def step_on(h, step):
            for ahead in (1, 0):
                for direction in range(2):
                    if not (step == 1 and ahead):
                        go(h, direction, step, direction ^ ahead)

        def ended(h, t, core):
            total = None
            for direction in range(2):
                ref = last.at[h, t, core, direction]
                remote(ref, ref, last_send.at[h, direction, t, 0], last_recv.at[h, direction, t, core],
                       partner).wait_recv()
                total = ref[...].astype(F32) if total is None else total + ref[...].astype(F32)
            return total

        return begin, step_on, ended

    zbegin, zsum_on, zended = summing(key_part, zin, zsum, rz_send, rz_recv, zdev, zfin, lz_send, lz_recv, zcores, z, NZ)
    xbegin, xsum_on, xended = summing(query_part, xin, xsum, rx_send, rx_recv, xdev, xfin, lx_send, lx_recv, xcores, x, NX)
    outs = (o_out, dq_out, dk_out, dv_out)

    def own_part(h, n, b):
        if n < 2:
            return query_part(h, n, x)(b)
        value = own_acc[h, n - 2, b]
        return key_part(h, n - 2, z)(b) + (value * SCALE if n == 2 else value)

    def give(h, ns):
        for n in ns:
            final[h, n] = own_part(h, n, 1 - c).astype(BF16)
            go_on(remote(final.at[h, n], gift.at[h, n], f_send.at[h, n], f_recv.at[h, n], partner))

    def finish(h, ns):
        for n in ns:
            ended = xended if n < 2 else zended
            mine = own_part(h, n, c) + ended(h, n % 2, c)
            outs[n][:, lanes_of(2 * c + h)] = mine.astype(BF16)
            remote(gift.at[h, n], gift.at[h, n], f_send.at[h, n], f_recv.at[h, n], partner).wait_recv()
            theirs = gift[h, n].astype(F32) + ended(h, n % 2, 1 - c)
            outs[n][:, lanes_of(2 * (1 - c) + h)] = theirs.astype(BF16)

    exchange(0, 0)
    exchange(0, 1)
    exchange(1, 0)
    lists.wait()
    plan(0)
    plan(1)
    zstart(0, 0)
    exchange(1, 1)
    zstart(0, 1)
    exchange_grad(0)
    exchange(0, 2)
    zstart(1, 0)
    exchange_grad(1)
    exchange(1, 2)
    zstep(0, 0)
    zstart(1, 1)
    xstart(0)
    zstep(0, 1)
    zstep(1, 0, (0,))
    xstart(1)
    xstep(0)
    zstep(0, 2)
    zstep(1, 0, (1,))
    xend(0)
    zend(0)
    pairs = [(i, i + 1) for i in range(0, ROW, 2)]
    count_units(0, pairs[0])
    count_units(0, pairs[1])
    zstep(1, 1)
    count_units(0, pairs[2])
    count_units(0, pairs[3])
    count_rest(0)
    send_stats(0)
    xstep(1)
    zstep(1, 2)
    take_stats(0)
    grad_units(0, pairs[0])
    xend(1)
    grad_units(0, pairs[1])
    grad_units(0, pairs[2])
    zend(1)
    for units in pairs:
        count_units(1, units)
    count_rest(1)
    send_stats(1)
    grad_units(0, pairs[3])
    grad_rim(0)
    zbegin(0)
    xbegin(0)
    grad_own(0)
    give(0, range(4))
    take_stats(1)
    grad_units(1, pairs[0])
    zsum_on(0, 1)
    xsum_on(0, 1)
    grad_units(1, pairs[1])
    grad_units(1, pairs[2])
    zsum_on(0, 2)
    grad_units(1, pairs[3])
    grad_rim(1)
    zbegin(1)
    xbegin(1)
    grad_own(1)
    zsum_on(0, 3)
    zsum_on(1, 1)
    xsum_on(1, 1)
    give(1, range(4))
    zsum_on(1, 2)
    finish(0, (0, 1))
    finish(1, (0, 1))
    finish(0, (2, 3))
    zsum_on(1, 3)
    finish(1, (3, 2))
    for cp in sends:
        cp.wait_send()


def place_kernel(*refs):
    for n in range(4):
        refs[4 + n][...] = refs[n][...]


def vmem():
    return pl.BlockSpec(memory_space=pltpu.VMEM)


def smem():
    return pl.BlockSpec(memory_space=pltpu.SMEM)


def on_device(query_rows, key_rows, value_rows, out_grad, random_blocks):
    dma = pltpu.SemaphoreType.DMA
    mem = pltpu.VMEM
    tile = (BLK, HD)
    full = jax.ShapeDtypeStruct((BLK, 4 * HD), BF16)
    zs, xs = NZ // 2, NX // 2
    outs = pl.pallas_call(
        attention_kernel,
        out_shape=(full,) * 4,
        in_specs=[pl.BlockSpec(memory_space=pltpu.HBM)] * 5,
        out_specs=[vmem()] * 4,
        scratch_shapes=[
            *[mem((COL,) + tile, BF16)] * 4, *[mem((ROW,) + tile, BF16)] * 4,
            mem((2, 4, 3, ROW, HD), F32), mem((2, NX, 3, ROW, HD), F32), mem((2, 3, ROW, HD), F32),
            mem((2, 2, ENTRIES) + tile, F32), mem((2, 2) + tile, F32), mem((2, 2, 2) + tile, F32),
            mem((2, ROW) + tile, F32), mem((2, ROW) + tile, F32),
            mem((2, 2, zs, 2, 2) + tile, BF16), mem((2, 2, zs, 2, 2) + tile, BF16),
            mem((2, 2, xs, 2, 2) + tile, BF16), mem((2, 2, xs, 2, 2) + tile, BF16),
            mem((2, 2, 2, 2) + tile, BF16), mem((2, 2, 2, 2) + tile, BF16),
            mem((2, 4) + tile, BF16), mem((2, 4) + tile, BF16),
            mem((2, ROW, RAND + 1) + tile, F32), mem((2, ROW, RAND + 1) + tile, F32),
            pltpu.SMEM((RAND, 4, NX * COL), jnp.int32),
            pltpu.SMEM((2 * ENTRIES,), jnp.int32), pltpu.SMEM((2 * ENTRIES,), jnp.int32), pltpu.SMEM((2 * COL,), jnp.int32), dma,
            dma((2, 3, 2 * NY)), dma((2, 3, 2 * NY)), dma((2, 3)), dma((2,)), dma((2,)), dma((2,)),
            dma((2, 2, zs, 2)), dma((2, 2, zs, 2)), dma((2, 2, xs, 2)), dma((2, 2, xs, 2)),
            dma((2, NX)), dma((2, NX)),
            dma((2, 2, zs, 2, 2)), dma((2, 2, zs, 2, 2)), dma((2, 2, xs, 2, 2)), dma((2, 2, xs, 2, 2)),
            dma((2, 2, 2, 2)), dma((2, 2, 2, 2)), dma((2, 2, 2, 2)), dma((2, 2, 2, 2)),
            dma((2, 4)), dma((2, 4)),
        ],
        compiler_params=pltpu.CompilerParams(collective_id=0, has_side_effects=True, vmem_limit_bytes=VMEM_LIMIT),
        name="attention",
    )(*(pltpu.with_memory_space_constraint(a, pltpu.HBM)
        for a in (random_blocks.transpose(2, 0, 1), query_rows, key_rows, value_rows, out_grad)))
    return pl.pallas_call(
        place_kernel,
        out_shape=(full,) * 4,
        in_specs=[vmem()] * 4,
        out_specs=[vmem()] * 4,
        compiler_params=pltpu.CompilerParams(vmem_limit_bytes=4 << 20),
        name="place",
    )(*outs)


def solution(mesh):
    in_specs = (
        P(("seq", "head"), None),
        P(("seq", "head"), None),
        P(("seq", "head"), None),
        P("seq", "head"),
        P("head", None, None),
    )
    out_specs = (P("seq", "head"),) * 4
    return jax.shard_map(
        on_device, mesh=mesh, in_specs=in_specs, out_specs=out_specs, check_vma=False
    )
```
